256 devices in a mesh: beads: 64 (over x, y, z_hi, core), waves: 4 (over z_lo).
Axes of the slice: x: 4, y: 4, z: 8 (z_hi: 2, z_lo: 4; z = z_hi * 4 + z_lo), core: 2. Of those that a mesh axis runs over, the one named last changes fastest.
Arguments:
- positions: float32 [3, 32768], P(None, 'beads'), may hold values from 0 to 256
- features: bfloat16 [32768, 256], P(('beads', 'waves')), may hold values from -6 to 6
- cotangent: bfloat16 [32768, 256], P(('beads', 'waves')), may hold values from -6 to 6
- wavevectors: float32 [3, 4096], replicated, may hold values from -0.25 to 0.25
- filter_gain: bfloat16 [4096, 256], P(('beads', 'waves')), may hold values from -6 to 6
Outputs:
- grad_features: bfloat16 [32768, 256], P(('beads', 'waves'))
- grad_positions: float32 [3, 32768], P(None, ('beads', 'waves'))
- grad_filter: float32 [4096, 256], P(('beads', 'waves'))
The draws below stay inside these ranges and needn't reach their ends.
All inputs are finite; a program needn't handle non-finite values.
Results may differ from the reference program's by a relative error of at most 0.012.
Values may be sent and summed in bfloat16 or wider, within the bound.
No kernel may reach another device: no remote copies, remote signals or barrier semaphores. Data moves between devices by JAX's collectives and lax.ppermute only.
A program may use at most 64 MiB of HBM per device.

```python
import math
import jax
import jax.numpy as jnp
from jax import lax

WIDTH = 256
K = 4096
BEADS = 32768


def block_levels(own_key, dims, split, least, top_value):
    loudness, own = 1.0, jax.random.fold_in(own_key, 6)
    for dim, shards_of in split:
        heights = jnp.exp(jax.random.uniform(jax.random.fold_in(own, dim), (shards_of,), jnp.float32, least / len(split), top_value / len(split)))
        loudness = loudness * jnp.repeat(heights, dims[dim] // shards_of).reshape([-1 if axis == dim else 1 for axis in range(len(dims))])
    return loudness


def centred(own_key, shape, scale, limit, shards=(), held_as=jnp.bfloat16):
    entries = scale * jax.random.normal(own_key, shape, jnp.float32)
    if shards:
        entries = entries * block_levels(own_key, shape, shards, -0.22, 0.18)
    return jnp.clip(entries, -limit, limit).astype(held_as)


def setup_inputs(seed: int = 0) -> dict:
    streams_of = jax.random.split(jax.random.key(seed), 6)
    return {
        "positions": jnp.clip(256.0 * jax.random.uniform(streams_of[0], (3, BEADS), jnp.float32) ** block_levels(streams_of[0], (3, BEADS), ((1, 64),), -0.2, 0.2), 0.0, 256.0),
        "features": centred(streams_of[1], (BEADS, WIDTH), 1.0, 6.0, ((0, 256),)),
        "cotangent": centred(streams_of[2], (BEADS, WIDTH), 1.0, 6.0, ((0, 256),)),
        "wavevectors": jnp.clip(jax.random.uniform(streams_of[3], (3, K), jnp.float32, -0.25, 0.25), -0.25, 0.25),
        "filter_gain": centred(streams_of[4], (K, WIDTH), 1.0, 6.0, ((0, 256),)),
    }


def phases(pos, kvec):
    return pos[0][:, None] * kvec[0][None, :] + pos[1][:, None] * kvec[1][None, :] + pos[2][:, None] * kvec[2][None, :]

def reference(positions, features, cotangent, wavevectors, filter_gain):
    nbeads = features.shape[0]
    nwaves = wavevectors.shape[1]
    width = features.shape[1]
    blk = min(1024, nbeads)
    nblk = nbeads // blk
    spec_scale = 1.0 / math.sqrt(nbeads)
    wave_scale = 1.0 / math.sqrt(nwaves)
    pos_blocks = positions.reshape(3, nblk, blk).transpose(1, 0, 2)
    feat_blocks = features.reshape(nblk, blk, width)
    cot_blocks = cotangent.reshape(nblk, blk, width)

    def accumulate(total, items):
        pos, feat, cot = items
        theta = phases(pos, wavevectors)
        cosine = jnp.cos(theta).astype(jnp.bfloat16).astype(jnp.float32)
        sine = jnp.sin(theta).astype(jnp.bfloat16).astype(jnp.float32)
        joined = jnp.concatenate([feat, cot], 1).astype(jnp.float32)
        part_cos = jnp.dot(cosine.T, joined)
        part_sin = jnp.dot(sine.T, joined)
        term = jnp.concatenate([part_cos[:, :width] * spec_scale, part_sin[:, :width] * spec_scale, part_cos[:, width:] * wave_scale, part_sin[:, width:] * wave_scale], 1)
        return (total + term, None)
    start = jnp.zeros((nwaves, 4 * width), jnp.float32)
    total, _ = lax.scan(accumulate, start, (pos_blocks, feat_blocks, cot_blocks))
    spec_r = total[:, :width]
    spec_i = total[:, width:2 * width]
    cot_r = total[:, 2 * width:3 * width]
    cot_i = total[:, 3 * width:]
    gains = filter_gain.astype(jnp.float32)
    grad_filter = cot_r * spec_r + cot_i * spec_i
    filt_r = (gains * spec_r).astype(jnp.bfloat16).astype(jnp.float32)
    filt_i = (gains * spec_i).astype(jnp.bfloat16).astype(jnp.float32)
    dspec_r = (gains * cot_r).astype(jnp.bfloat16).astype(jnp.float32)
    dspec_i = (gains * cot_i).astype(jnp.bfloat16).astype(jnp.float32)

    def backward(items):
        pos, feat, cot = items
        theta = phases(pos, wavevectors)
        cosine = jnp.cos(theta).astype(jnp.bfloat16).astype(jnp.float32)
        sine = jnp.sin(theta).astype(jnp.bfloat16).astype(jnp.float32)
        feat32 = feat.astype(jnp.float32)
        cot32 = cot.astype(jnp.float32)
        grad_feat = (jnp.dot(cosine, dspec_r) + jnp.dot(sine, dspec_i)) * spec_scale
        first = jnp.dot(cot32, filt_r.T) * wave_scale + jnp.dot(feat32, dspec_r.T) * spec_scale
        second = jnp.dot(cot32, filt_i.T) * wave_scale + jnp.dot(feat32, dspec_i.T) * spec_scale
        dtheta = -sine * first + cosine * second
        grad_pos = jnp.dot(wavevectors, dtheta.T, precision=lax.Precision.HIGHEST)
        return (grad_feat, grad_pos)
    grad_feat, grad_pos = lax.map(backward, (pos_blocks, feat_blocks, cot_blocks))
    grad_features = grad_feat.reshape(nbeads, width).astype(jnp.bfloat16)
    grad_positions = grad_pos.transpose(1, 0, 2).reshape(3, nbeads)
    return (grad_features, grad_positions, grad_filter)
```

```python
import math

import jax
import jax.numpy as jnp
from jax import lax
from jax.experimental import pallas as pl
from jax.experimental.pallas import tpu as pltpu
from jax.sharding import Mesh
from jax.sharding import PartitionSpec as P

ALL = ("x", "y", "zh", "core", "zl")
Z = ("zh", "zl")
XY = ("x", "y")
BF16 = jnp.bfloat16
F32 = jnp.float32
LANES = 128

SIN_TURN = (6.28318501, -41.3416557, 81.6010056, -76.5497818, 39.536705)


def sin_turn(h):
    s = h * h
    poly = SIN_TURN[-1]
    for c in SIN_TURN[-2::-1]:
        poly = poly * s + c
    return poly * h


def trig_kernel(scal, pos_own, pos_far, wv, cs, kvrel, pos_all, kvt):
    zh, zl, core = scal[0], scal[1], scal[2]
    n_xy = cs.shape[1]
    n_z = cs.shape[4] // LANES
    here = zh * (n_z // 2) + zl
    for shift in range(n_z):
        zz = lax.rem(here + n_z - shift, n_z)
        far = zz // (n_z // 2)
        at = pl.multiple_of(lax.rem(zz, n_z // 2) * LANES, LANES)
        own = pos_own[:, pl.ds(at, LANES)]
        other = pos_far[:, pl.ds(at, LANES)]
        pos_all[0:3, shift * LANES : (shift + 1) * LANES] = jnp.where(far == zh, own, other)
    for xy in range(n_xy):
        at = pl.multiple_of((xy * 2 + zh) * LANES, LANES)
        piece = wv[:, pl.ds(at, LANES)]
        piece = jnp.concatenate([piece, jnp.zeros((5, LANES), F32)], 0)
        kvt[xy, :, 0:8] = piece.T
    turn = 1.0 / (2.0 * math.pi)
    for dc in range(2):
        at = pl.multiple_of((jnp.bitwise_xor(core, dc) * (n_z // 2) + zl) * 16, 16)

        def step(xy, carry):
            cols = kvt[xy, pl.ds(at, 16), 0:8]
            hi = cols.astype(BF16)
            lo = (cols - hi.astype(F32)).astype(BF16)
            kvrel[pl.ds(pl.multiple_of((dc * n_xy + xy) * 16, 16), 16), :] = jnp.concatenate(
                [hi, lo], 1
            )
            cols = cols * turn
            t = (
                cols[:, 0:1] * pos_all[0:1, :]
                + cols[:, 1:2] * pos_all[1:2, :]
                + cols[:, 2:3] * pos_all[2:3, :]
            )
            f = t - jnp.round(t)
            cosine = sin_turn(0.25 - jnp.abs(f))
            sine = sin_turn(jnp.maximum(jnp.minimum(f, 0.5 - f), -0.5 - f))
            cs[dc, xy, 0] = cosine.astype(BF16)
            cs[dc, xy, 1] = sine.astype(BF16)
            return carry

        lax.fori_loop(0, n_xy, step, 0)


def spectra_kernel(dc, cs, *refs):
    pieces, out = refs[:-1], refs[-1]
    n_xy, _, _, beads = cs.shape[1:]
    beads_all = jnp.concatenate([p[...] for p in pieces], 0)
    rows = cs[dc].reshape(n_xy * 32, beads)
    part = jnp.dot(rows, beads_all, preferred_element_type=F32)
    out[...] = part.reshape(out.shape).astype(out.dtype)


def filter_kernel(spec_scale, wave_scale, arrived, gain, out, grad_filter):
    n = arrived.shape[0]
    width = gain.shape[1]
    total = arrived[0].astype(F32)
    for i in range(1, n):
        total = total + arrived[i].astype(F32)
    total = total.reshape(2, 16, 2 * width)
    cot = total[:, :, :width] * wave_scale
    spec = total[:, :, width:] * spec_scale
    g = gain[...].astype(F32)
    grad_filter[...] = cot[0] * spec[0] + cot[1] * spec[1]
    filt = (g[None] * spec * (wave_scale / spec_scale)).astype(BF16)
    dspec = (g[None] * cot).astype(BF16)
    both = jnp.concatenate([filt, dspec], 2).reshape(32, 2 * width)
    for i in range(n):
        out[i] = both


def half_gradients(dc, cs, kvrel, stacked, beads_all):
    n_xy, beads = cs.shape[1], cs.shape[4]
    width = beads_all.shape[1] // 2
    both = stacked[...].reshape(n_xy * 32, 2 * width)
    ab = lax.dot_general(both, beads_all, (((1,), (1,)), ((), ())), preferred_element_type=F32)
    ab = ab.reshape(n_xy, 2, 16, beads)
    d = cs[dc, :, 0].astype(F32) * ab[:, 1] - cs[dc, :, 1].astype(F32) * ab[:, 0]
    d = d.reshape(n_xy * 16, beads).astype(BF16)
    kv = kvrel[dc * n_xy * 16 : (dc + 1) * n_xy * 16, :]
    gp = lax.dot_general(kv, d, (((0,), (0,)), ((), ())), preferred_element_type=F32)
    rows = cs[dc].reshape(n_xy * 32, beads)
    gf = lax.dot_general(
        rows, both[:, width:], (((0,), (0,)), ((), ())), preferred_element_type=F32
    )
    return gf, gp[0:8] + gp[8:16]


def grads_near_kernel(cs, kvrel, stacked, *refs):
    pieces, (gf_out, gp_out) = refs[:-2], refs[-2:]
    beads_all = jnp.concatenate([p[...] for p in pieces], 0)
    gf, gp = half_gradients(0, cs, kvrel, stacked, beads_all)
    gf_out[...] = gf
    gp_out[...] = gp


def grads_far_kernel(spec_scale, n_blocks, cs, kvrel, stacked, gf_in, gp_in, *refs):
    pieces, outs = refs[:n_blocks], refs[n_blocks:]
    beads_all = jnp.concatenate([p[...] for p in pieces], 0)
    gf, gp = half_gradients(1, cs, kvrel, stacked, beads_all)
    gf = ((gf + gf_in[...]) * spec_scale).astype(BF16)
    gp = (gp + gp_in[...]) * spec_scale
    hi = gp.astype(BF16)
    lo = (gp - hi.astype(F32)).astype(BF16)
    pad = jnp.zeros((8, 2 * LANES), BF16)
    for shift in range(len(outs)):
        at = slice(shift * LANES, (shift + 1) * LANES)
        outs[shift][0:LANES, :] = gf[at]
        tail = jnp.concatenate([hi[:, at], lo[:, at]], 1)
        outs[shift][LANES : LANES + 16, :] = jnp.concatenate([tail, pad], 0)


def total_kernel(*refs):
    pieces, (gf_out, gp_out) = refs[:-2], refs[-2:]
    total = pieces[0][...].astype(F32)
    for p in pieces[1:]:
        total = total + p[...].astype(F32)
    gf_out[...] = total[:LANES].astype(BF16)
    tail = total[LANES : LANES + 8]
    gp_out[...] = (tail[:, :LANES] + tail[:, LANES:])[0:3]


def call(kernel, out_shape, n_in, scalars=0, scratch=()):
    specs = [pl.BlockSpec(memory_space=pltpu.SMEM)] * scalars
    specs += [pl.BlockSpec(memory_space=pltpu.VMEM)] * (n_in - scalars)
    outs = jax.tree.map(lambda _: pl.BlockSpec(memory_space=pltpu.VMEM), out_shape)
    return pl.pallas_call(
        kernel, out_shape=out_shape, in_specs=specs, out_specs=outs, scratch_shapes=scratch
    )


def shape(dims, dtype):
    return jax.ShapeDtypeStruct(dims, dtype)


def body(positions, features, cotangent, wavevectors, filter_gain):
    n_z = lax.axis_size(Z)
    n_xy = lax.axis_size(XY)
    beads_dev, width = features.shape
    beads_grp = beads_dev * n_z
    n_beads = beads_grp * n_xy * 2
    spec_scale = 1.0 / math.sqrt(n_beads)
    wave_scale = 1.0 / math.sqrt(wavevectors.shape[1])

    def along_z(a, k):
        return lax.ppermute(a, Z, [(i, (i + k) % n_z) for i in range(n_z)])

    def across(a, axis):
        return lax.ppermute(a, axis, [(0, 1), (1, 0)])

    own = jnp.concatenate([cotangent, features], 1)
    pieces = {0: own, 1: along_z(own, 1), 7: along_z(own, -1)}
    pieces[2], pieces[6] = along_z(own, 2), along_z(own, -2)
    half = beads_dev // 2
    pieces[3], pieces[5] = along_z(pieces[2], 1), along_z(pieces[6], -1)
    ahead, behind = along_z(pieces[2][:half], 2), along_z(pieces[6][half:], -2)
    blocks = [pieces[0], pieces[1], pieces[2], pieces[3], ahead, behind]
    blocks += [pieces[5], pieces[6], pieces[7]]

    scal = jnp.stack([lax.axis_index("zh"), lax.axis_index("zl"), lax.axis_index("core")])
    cs, kvrel = call(
        trig_kernel,
        (shape((2, n_xy, 2, 16, beads_grp), BF16), shape((2 * n_xy * 16, 16), BF16)),
        4,
        scalars=1,
        scratch=[pltpu.VMEM((8, beads_grp), F32), pltpu.VMEM((n_xy, LANES, 8), F32)],
    )(scal.astype(jnp.int32), positions, across(positions, "zh"), wavevectors)

    def spectra(dc, dtype):
        return call(
            lambda *refs: spectra_kernel(dc, *refs),
            shape((n_xy, 32, 2 * width), dtype),
            1 + len(blocks),
        )(cs, *blocks)

    theirs = across(spectra(1, BF16), "core")
    mine = (spectra(0, F32) + theirs.astype(F32)).astype(BF16)
    arrived = lax.all_to_all(mine, XY, 0, 0, tiled=True)
    copies, grad_filter = call(
        lambda *refs: filter_kernel(spec_scale, wave_scale, *refs),
        (shape((n_xy, 32, 2 * width), BF16), shape((16, width), F32)),
        2,
    )(arrived, filter_gain)
    near = lax.all_to_all(copies, XY, 0, 0, tiled=True)
    far = across(near, "core")
    gf, gp = call(
        grads_near_kernel,
        (shape((beads_grp, width), F32), shape((8, beads_grp), F32)),
        3 + len(blocks),
    )(cs, kvrel, near, *blocks)
    n_blocks = len(blocks)
    outs = call(
        lambda *refs: grads_far_kernel(spec_scale, n_blocks, *refs),
        [shape((beads_dev + 16, width), BF16)] * n_z,
        5 + n_blocks,
    )(cs, kvrel, far, gf, gp, *blocks)
    sums = [outs[0]] + [along_z(outs[k], -k) for k in range(1, n_z)]
    grad_feat, grad_pos = call(
        total_kernel, (shape((beads_dev, width), BF16), shape((3, beads_dev), F32)), n_z
    )(*sums)
    return grad_feat, grad_pos, grad_filter


def solution(mesh):
    torus = Mesh(mesh.devices.reshape(4, 4, 2, 2, mesh.shape["waves"]), ALL)
    beads = ("x", "y", "zh", "core")
    return jax.shard_map(
        body,
        mesh=torus,
        in_specs=(P(None, beads), P(ALL, None), P(ALL, None), P(), P(ALL, None)),
        out_specs=(P(ALL, None), P(None, ALL), P(ALL, None)),
        check_vma=False,
    )
```

```python
import math

import jax
import jax.numpy as jnp
from jax import lax
from jax.experimental import pallas as pl
from jax.experimental.pallas import tpu as pltpu
from jax.sharding import Mesh
from jax.sharding import PartitionSpec as P

ALL = ("x", "y", "zh", "core", "zl")
Z = ("zh", "zl")
XY = ("x", "y")
BF16 = jnp.bfloat16
F32 = jnp.float32
LANES = 128

SIN_TURN = (6.28318501, -41.3416557, 81.6010056, -76.5497818, 39.536705)


def sin_turn(h):
    s = h * h
    poly = SIN_TURN[-1]
    for c in SIN_TURN[-2::-1]:
        poly = poly * s + c
    return poly * h


def join_kernel(left, right, out):
    width = left.shape[1]
    out[:, :width] = left[...]
    out[:, width:] = right[...]


def trig_kernel(far, scal, pos, wv, *refs):
    cs, kvrel, kvt = refs[-3:]
    zh, zl, core = scal[0], scal[1], scal[2]
    n_xy = cs.shape[1]
    n_z = cs.shape[4] // LANES
    n_zl = n_z // 2
    first = (jnp.bitwise_xor(zh, 1) if far else zh) * n_zl
    for xy in range(n_xy):
        at = pl.multiple_of((xy * 2 + zh) * LANES, LANES)
        piece = wv[:, pl.ds(at, LANES)]
        piece = jnp.concatenate([piece, jnp.zeros((5, LANES), F32)], 0)
        kvt[xy, :, 0:8] = piece.T
    turn = 1.0 / (2.0 * math.pi)
    columns = [
        pl.multiple_of(lax.rem(zh * n_zl + zl + n_z - first - i, n_z) * LANES, LANES)
        for i in range(n_zl)
    ]
    for dc in range(2):
        at = pl.multiple_of((jnp.bitwise_xor(core, dc) * n_zl + zl) * 16, 16)

        def step(xy, carry):
            cols = kvt[xy, pl.ds(at, 16), 0:8]
            if not far:
                hi = cols.astype(BF16)
                lo = (cols - hi.astype(F32)).astype(BF16)
                kvrel[pl.ds(pl.multiple_of((dc * n_xy + xy) * 16, 16), 16), :] = jnp.concatenate(
                    [hi, lo], 1
                )
            cols = cols * turn
            t = (
                cols[:, 0:1] * pos[0:1, :]
                + cols[:, 1:2] * pos[1:2, :]
                + cols[:, 2:3] * pos[2:3, :]
            )
            f = t - jnp.round(t)
            cosine = sin_turn(0.25 - jnp.abs(f)).astype(BF16)
            sine = sin_turn(jnp.maximum(jnp.minimum(f, 0.5 - f), -0.5 - f)).astype(BF16)
            for i, column in enumerate(columns):
                part = slice(i * LANES, (i + 1) * LANES)
                cs[dc, xy, 0, :, pl.ds(column, LANES)] = cosine[:, part]
                cs[dc, xy, 1, :, pl.ds(column, LANES)] = sine[:, part]
            return carry

        lax.fori_loop(0, n_xy, step, 0, unroll=2)


def spectra_kernel(dc, cs, *refs):
    pieces, out = refs[:-1], refs[-1]
    n_xy, _, _, beads = cs.shape[1:]
    beads_all = jnp.concatenate([p[...] for p in pieces], 0)
    rows = cs[dc].reshape(n_xy * 32, beads)
    part = jnp.dot(rows, beads_all, preferred_element_type=F32)
    out[...] = part.reshape(out.shape).astype(out.dtype)


def filter_kernel(spec_scale, wave_scale, arrived, gain, out, grad_filter):
    n = arrived.shape[0]
    width = gain.shape[1]
    total = arrived[0].astype(F32)
    for i in range(1, n):
        total = total + arrived[i].astype(F32)
    total = total.reshape(2, 16, 2 * width)
    cot = total[:, :, :width] * wave_scale
    spec = total[:, :, width:] * spec_scale
    g = gain[...].astype(F32)
    grad_filter[...] = cot[0] * spec[0] + cot[1] * spec[1]
    filt = (g[None] * spec * (wave_scale / spec_scale)).astype(BF16)
    dspec = (g[None] * cot).astype(BF16)
    both = jnp.concatenate([filt, dspec], 2).reshape(32, 2 * width)
    for i in range(n):
        out[i] = both


def half_gradients(dc, cs, kvrel, stacked, beads_all):
    n_xy, beads = cs.shape[1], cs.shape[4]
    width = beads_all.shape[1] // 2
    both = stacked[...].reshape(n_xy * 32, 2 * width)
    ab = lax.dot_general(both, beads_all, (((1,), (1,)), ((), ())), preferred_element_type=F32)
    ab = ab.reshape(n_xy, 2, 16, beads)
    d = cs[dc, :, 0].astype(F32) * ab[:, 1] - cs[dc, :, 1].astype(F32) * ab[:, 0]
    d = d.reshape(n_xy * 16, beads).astype(BF16)
    kv = kvrel[dc * n_xy * 16 : (dc + 1) * n_xy * 16, :]
    gp = lax.dot_general(kv, d, (((0,), (0,)), ((), ())), preferred_element_type=F32)
    rows = cs[dc].reshape(n_xy * 32, beads)
    gf = lax.dot_general(
        rows, both[:, width:], (((0,), (0,)), ((), ())), preferred_element_type=F32
    )
    return gf, gp[0:8] + gp[8:16]


def grads_near_kernel(cs, kvrel, stacked, *refs):
    pieces, (gf_out, gp_out) = refs[:-2], refs[-2:]
    beads_all = jnp.concatenate([p[...] for p in pieces], 0)
    gf, gp = half_gradients(0, cs, kvrel, stacked, beads_all)
    gf_out[...] = gf
    gp_out[...] = gp


def grads_far_kernel(spec_scale, n_blocks, cs, kvrel, stacked, gf_in, gp_in, *refs):
    pieces, outs = refs[:n_blocks], refs[n_blocks:]
    beads_all = jnp.concatenate([p[...] for p in pieces], 0)
    gf, gp = half_gradients(1, cs, kvrel, stacked, beads_all)
    gf = ((gf + gf_in[...]) * spec_scale).astype(BF16)
    gp = (gp + gp_in[...]) * spec_scale
    hi = gp.astype(BF16)
    lo = (gp - hi.astype(F32)).astype(BF16)
    for shift in range(len(outs)):
        at = slice(shift * LANES, (shift + 1) * LANES)
        outs[shift][0:LANES, :] = gf[at]
        outs[shift][LANES : LANES + 8, :] = jnp.concatenate([hi[:, at], lo[:, at]], 1)


def total_kernel(*refs):
    pieces, (gf_out, gp_out) = refs[:-2], refs[-2:]
    total = pieces[0][...].astype(F32)
    for p in pieces[1:]:
        total = total + p[...].astype(F32)
    gf_out[...] = total[:LANES].astype(BF16)
    tail = total[LANES : LANES + 8]
    gp_out[...] = (tail[:, :LANES] + tail[:, LANES:])[0:3]


def call(kernel, out_shape, n_in, scalars=0, scratch=(), aliases=None):
    specs = [pl.BlockSpec(memory_space=pltpu.SMEM)] * scalars
    specs += [pl.BlockSpec(memory_space=pltpu.VMEM)] * (n_in - scalars)
    outs = jax.tree.map(lambda _: pl.BlockSpec(memory_space=pltpu.VMEM), out_shape)
    return pl.pallas_call(
        kernel,
        out_shape=out_shape,
        in_specs=specs,
        out_specs=outs,
        scratch_shapes=scratch,
        input_output_aliases=aliases or {},
        compiler_params=pltpu.CompilerParams(vmem_limit_bytes=16 << 20),
    )


def shape(dims, dtype):
    return jax.ShapeDtypeStruct(dims, dtype)


def body(positions, features, cotangent, wavevectors, filter_gain):
    n_z = lax.axis_size(Z)
    n_xy = lax.axis_size(XY)
    beads_dev, width = features.shape
    beads_grp = beads_dev * n_z
    n_beads = beads_grp * n_xy * 2
    spec_scale = 1.0 / math.sqrt(n_beads)
    wave_scale = 1.0 / math.sqrt(wavevectors.shape[1])

    def along_z(a, k):
        return lax.ppermute(a, Z, [(i, (i + k) % n_z) for i in range(n_z)])

    def across(a, axis):
        return lax.ppermute(a, axis, [(0, 1), (1, 0)])

    own = call(join_kernel, shape((beads_dev, 2 * width), BF16), 2)(cotangent, features)
    pieces = {0: own, 2: along_z(own, 2), 6: along_z(own, -2)}
    pieces[1], pieces[7] = along_z(own, 1), along_z(own, -1)
    pos_far = across(positions, "zh")

    scal = jnp.stack([lax.axis_index("zh"), lax.axis_index("zl"), lax.axis_index("core")])
    scal = scal.astype(jnp.int32)
    trig_shapes = (shape((2, n_xy, 2, 16, beads_grp), BF16), shape((2 * n_xy * 16, 16), BF16))
    kvt = [pltpu.VMEM((n_xy, LANES, 8), F32)]
    trig = call(lambda *refs: trig_kernel(False, *refs), trig_shapes, 3, scalars=1, scratch=kvt)(
        scal, positions, wavevectors
    )
    pieces[2], pieces[6], pos_far, trig = lax.optimization_barrier(
        (pieces[2], pieces[6], pos_far, trig)
    )
    half = beads_dev // 2
    pieces[3], pieces[5] = along_z(pieces[2], 1), along_z(pieces[6], -1)
    ahead, behind = along_z(pieces[2][:half], 2), along_z(pieces[6][half:], -2)
    blocks = [pieces[0], pieces[1], pieces[2], pieces[3], ahead, behind]
    blocks += [pieces[5], pieces[6], pieces[7]]
    cs, kvrel = call(
        lambda *refs: trig_kernel(True, *refs),
        trig_shapes,
        5,
        scalars=1,
        scratch=kvt,
        aliases={3: 0, 4: 1},
    )(scal, pos_far, wavevectors, *trig)

    def spectra(dc, dtype):
        return call(
            lambda *refs: spectra_kernel(dc, *refs),
            shape((n_xy, 32, 2 * width), dtype),
            1 + len(blocks),
        )(cs, *blocks)

    theirs = across(spectra(1, BF16), "core")
    mine = (spectra(0, F32) + theirs.astype(F32)).astype(BF16)
    arrived = lax.all_to_all(mine, XY, 0, 0, tiled=True)
    copies, grad_filter = call(
        lambda *refs: filter_kernel(spec_scale, wave_scale, *refs),
        (shape((n_xy, 32, 2 * width), BF16), shape((16, width), F32)),
        2,
    )(arrived, filter_gain)
    near = lax.all_to_all(copies, XY, 0, 0, tiled=True)
    far = across(near, "core")
    gf, gp = call(
        grads_near_kernel,
        (shape((beads_grp, width), F32), shape((8, beads_grp), F32)),
        3 + len(blocks),
    )(cs, kvrel, near, *blocks)
    n_blocks = len(blocks)
    outs = call(
        lambda *refs: grads_far_kernel(spec_scale, n_blocks, *refs),
        [shape((beads_dev + 8, width), BF16)] * n_z,
        5 + n_blocks,
    )(cs, kvrel, far, gf, gp, *blocks)
    sums = [outs[0]] + [along_z(outs[k], -k) for k in range(1, n_z)]
    grad_feat, grad_pos = call(
        total_kernel, (shape((beads_dev, width), BF16), shape((3, beads_dev), F32)), n_z
    )(*sums)
    return grad_feat, grad_pos, grad_filter


def solution(mesh):
    torus = Mesh(mesh.devices.reshape(4, 4, 2, 2, mesh.shape["waves"]), ALL)
    beads = ("x", "y", "zh", "core")
    return jax.shard_map(
        body,
        mesh=torus,
        in_specs=(P(None, beads), P(ALL, None), P(ALL, None), P(), P(ALL, None)),
        out_specs=(P(ALL, None), P(None, ALL), P(ALL, None)),
        check_vma=False,
    )
```

```python
import math

import jax
import jax.numpy as jnp
from jax import lax
from jax.experimental import pallas as pl
from jax.experimental.pallas import tpu as pltpu
from jax.sharding import Mesh
from jax.sharding import PartitionSpec as P

ALL = ("x", "y", "zh", "core", "zl")
Z = ("zh", "zl")
XY = ("x", "y")
BF16 = jnp.bfloat16
F32 = jnp.float32
LANES = 128

SIN_TURN = (6.28318501, -41.3416557, 81.6010056, -76.5497818, 39.536705)


def sin_turn(h):
    s = h * h
    poly = SIN_TURN[-1]
    for c in SIN_TURN[-2::-1]:
        poly = poly * s + c
    return poly * h


def load_kernel(cot, feat, pos, wv, own, sent, pos_near, wv_near, sems):
    beads, width = cot.shape
    copies = [
        pltpu.make_async_copy(cot, own.at[:, :width], sems.at[0]),
        pltpu.make_async_copy(feat, own.at[:, width:], sems.at[1]),
        pltpu.make_async_copy(pos, pos_near, sems.at[2]),
        pltpu.make_async_copy(wv, wv_near, sems.at[3]),
    ]
    for c in copies:
        c.start()
    for c in copies:
        c.wait()
    sent[:beads, :] = own[...]
    left = pos_near[...]
    parts = []
    for _ in range(3):
        part = left.astype(BF16).astype(F32)
        parts.append(part)
        left = left - part
    parts.append(jnp.zeros((7, left.shape[1]), F32))
    sent[beads:, :] = jnp.concatenate(parts, 0).astype(BF16)


def trig_rows(kcols, pos, cs, zh, zl, first):
    n_xy = cs.shape[1]
    n_z = cs.shape[4] // LANES
    n_zl = n_z // 2
    columns = [
        pl.multiple_of(lax.rem(zh * n_zl + zl + n_z - first - i, n_z) * LANES, LANES)
        for i in range(n_zl)
    ]

    def step(i, carry):
        dc, xy = i // n_xy, lax.rem(i, n_xy)
        cols = kcols[pl.ds(pl.multiple_of(i * 16, 16), 16), :]
        t = cols[:, 0:1] * pos[0:1] + cols[:, 1:2] * pos[1:2] + cols[:, 2:3] * pos[2:3]
        f = t - jnp.round(t)
        cosine = sin_turn(0.25 - jnp.abs(f)).astype(BF16)
        sine = sin_turn(jnp.maximum(jnp.minimum(f, 0.5 - f), -0.5 - f)).astype(BF16)
        for j, column in enumerate(columns):
            part = slice(j * LANES, (j + 1) * LANES)
            cs[dc, xy, 0, :, pl.ds(column, LANES)] = cosine[:, part]
            cs[dc, xy, 1, :, pl.ds(column, LANES)] = sine[:, part]
        return carry

    lax.fori_loop(0, 2 * n_xy, step, 0, unroll=4)


def trig_near_kernel(scal, pos, wv, cs, kvrel, kcols, kvt):
    zh, zl, core = scal[0], scal[1], scal[2]
    n_xy = cs.shape[1]
    n_zl = cs.shape[4] // LANES // 2
    for xy in range(n_xy):
        at = pl.multiple_of((xy * 2 + zh) * LANES, LANES)
        piece = wv[:, pl.ds(at, LANES)]
        piece = jnp.concatenate([piece, jnp.zeros((5, LANES), F32)], 0)
        kvt[xy, :, 0:8] = piece.T
    for dc in range(2):
        at = pl.multiple_of((jnp.bitwise_xor(core, dc) * n_zl + zl) * 16, 16)
        for xy in range(n_xy):
            cols = kvt[xy, pl.ds(at, 16), 0:8]
            rows = slice((dc * n_xy + xy) * 16, (dc * n_xy + xy + 1) * 16)
            hi = cols.astype(BF16)
            lo = (cols - hi.astype(F32)).astype(BF16)
            kvrel[rows, :] = jnp.concatenate([hi, lo], 1)
            kcols[rows, :] = cols * (1.0 / (2.0 * math.pi))
    trig_rows(kcols, pos[...], cs, zh, zl, zh * n_zl)


def trig_far_kernel(scal, ahead, behind, kcols, _, cs):
    zh, zl = scal[0], scal[1]
    n_zl = cs.shape[4] // LANES // 2
    beads = ahead.shape[0] - 16
    rows = jnp.where(zl < n_zl // 2, ahead[beads:, :], behind[beads:, :]).astype(F32)
    pos = rows[0:3] + rows[3:6] + rows[6:9]
    trig_rows(kcols, pos, cs, zh, zl, jnp.bitwise_xor(zh, 1) * n_zl)


def spectra_kernel(dc, cs, *refs):
    pieces, out = refs[:-1], refs[-1]
    n_xy, _, _, beads = cs.shape[1:]
    beads_all = jnp.concatenate([p[: min(LANES, p.shape[0])] for p in pieces], 0)
    rows = cs[dc].reshape(n_xy * 32, beads)
    part = jnp.dot(rows, beads_all, preferred_element_type=F32)
    out[...] = part.reshape(out.shape).astype(out.dtype)


def filter_kernel(spec_scale, wave_scale, arrived, gain, out, grad_filter):
    n = arrived.shape[0]
    width = gain.shape[1]
    total = arrived[0].astype(F32)
    for i in range(1, n):
        total = total + arrived[i].astype(F32)
    total = total.reshape(2, 16, 2 * width)
    cot = total[:, :, :width] * wave_scale
    spec = total[:, :, width:] * spec_scale
    g = gain[...].astype(F32)
    grad_filter[...] = cot[0] * spec[0] + cot[1] * spec[1]
    filt = (g[None] * spec * (wave_scale / spec_scale)).astype(BF16)
    dspec = (g[None] * cot).astype(BF16)
    both = jnp.concatenate([filt, dspec], 2).reshape(32, 2 * width)
    for i in range(n):
        out[i] = both


def half_gradients(dc, cs, kvrel, stacked, beads_all):
    n_xy, beads = cs.shape[1], cs.shape[4]
    width = beads_all.shape[1] // 2
    both = stacked[...].reshape(n_xy * 32, 2 * width)
    ab = lax.dot_general(both, beads_all, (((1,), (1,)), ((), ())), preferred_element_type=F32)
    ab = ab.reshape(n_xy, 2, 16, beads)
    d = cs[dc, :, 0].astype(F32) * ab[:, 1] - cs[dc, :, 1].astype(F32) * ab[:, 0]
    d = d.reshape(n_xy * 16, beads).astype(BF16)
    kv = kvrel[dc * n_xy * 16 : (dc + 1) * n_xy * 16, :]
    gp = lax.dot_general(kv, d, (((0,), (0,)), ((), ())), preferred_element_type=F32)
    rows = cs[dc].reshape(n_xy * 32, beads)
    gf = lax.dot_general(
        rows, both[:, width:], (((0,), (0,)), ((), ())), preferred_element_type=F32
    )
    return gf, gp[0:8] + gp[8:16]


def grads_near_kernel(cs, kvrel, stacked, *refs):
    pieces, (gf_out, gp_out) = refs[:-2], refs[-2:]
    beads_all = jnp.concatenate([p[: min(LANES, p.shape[0])] for p in pieces], 0)
    gf, gp = half_gradients(0, cs, kvrel, stacked, beads_all)
    gf_out[...] = gf
    gp_out[...] = gp


def grads_far_kernel(spec_scale, scal, cs, kvrel, stacked, gf_in, gp_in, *refs):
    pieces, out = refs[:-1], refs[-1]
    beads_all = jnp.concatenate([p[: min(LANES, p.shape[0])] for p in pieces], 0)
    gf, gp = half_gradients(1, cs, kvrel, stacked, beads_all)
    gf = ((gf + gf_in[...]) * spec_scale).astype(BF16)
    gp = (gp + gp_in[...]) * spec_scale
    hi = gp.astype(BF16)
    lo = (gp - hi.astype(F32)).astype(BF16)
    n_z = out.shape[0]
    here = scal[0] * (n_z // 2) + scal[1]
    for shift in range(n_z):
        at = slice(shift * LANES, (shift + 1) * LANES)
        to = lax.rem(here + n_z - shift, n_z)
        out[to, 0:LANES, :] = gf[at]
        out[to, LANES : LANES + 8, :] = jnp.concatenate([hi[:, at], lo[:, at]], 1)


def total_kernel(arrived, gf_out, gp_out):
    total = arrived[0].astype(F32)
    for i in range(1, arrived.shape[0]):
        total = total + arrived[i].astype(F32)
    gf_out[...] = total[:LANES].astype(BF16)
    tail = total[LANES : LANES + 8]
    gp_out[...] = (tail[:, :LANES] + tail[:, LANES:])[0:3]


def call(kernel, out_shape, n_in, scalars=0, scratch=(), aliases=None, space=pltpu.VMEM):
    specs = [pl.BlockSpec(memory_space=pltpu.SMEM)] * scalars
    specs += [pl.BlockSpec(memory_space=space)] * (n_in - scalars)
    outs = jax.tree.map(lambda _: pl.BlockSpec(memory_space=pltpu.VMEM), out_shape)
    return pl.pallas_call(
        kernel,
        out_shape=out_shape,
        in_specs=specs,
        out_specs=outs,
        scratch_shapes=scratch,
        input_output_aliases=aliases or {},
        compiler_params=pltpu.CompilerParams(vmem_limit_bytes=16 << 20),
    )


def shape(dims, dtype):
    return jax.ShapeDtypeStruct(dims, dtype)


def body(positions, features, cotangent, wavevectors, filter_gain):
    n_z = lax.axis_size(Z)
    n_xy = lax.axis_size(XY)
    beads_dev, width = features.shape
    beads_grp = beads_dev * n_z
    n_beads = beads_grp * n_xy * 2
    spec_scale = 1.0 / math.sqrt(n_beads)
    wave_scale = 1.0 / math.sqrt(wavevectors.shape[1])

    def along_z(a, k):
        return lax.ppermute(a, Z, [(i, (i + k) % n_z) for i in range(n_z)])

    def across(a):
        return lax.ppermute(a, "core", [(0, 1), (1, 0)])

    own, sent, pos_near, wv_near = call(
        load_kernel,
        (
            shape((beads_dev, 2 * width), BF16),
            shape((beads_dev + 16, 2 * width), BF16),
            shape(positions.shape, F32),
            shape(wavevectors.shape, F32),
        ),
        4,
        scratch=[pltpu.SemaphoreType.DMA((4,))],
        space=pltpu.HBM,
    )(cotangent, features, positions, wavevectors)
    pieces = {0: own, 2: along_z(sent, 2), 6: along_z(sent, -2)}
    pieces[1], pieces[7] = along_z(own, 1), along_z(own, -1)

    scal = jnp.stack([lax.axis_index("zh"), lax.axis_index("zl"), lax.axis_index("core")])
    scal = scal.astype(jnp.int32)
    n_rows = 2 * n_xy * 16
    cs_shape = shape((2, n_xy, 2, 16, beads_grp), BF16)
    trig = call(
        trig_near_kernel,
        (cs_shape, shape((n_rows, 16), BF16), shape((n_rows, 8), F32)),
        3,
        scalars=1,
        scratch=[pltpu.VMEM((n_xy, LANES, 8), F32)],
    )(scal, pos_near, wv_near)
    pieces[2], pieces[6], trig = lax.optimization_barrier((pieces[2], pieces[6], trig))
    ahead, behind = pieces[2][:beads_dev], pieces[6][:beads_dev]
    half = beads_dev // 2
    pieces[3], pieces[5] = along_z(ahead, 1), along_z(behind, -1)
    blocks = [pieces[0], pieces[1], pieces[2], pieces[3]]
    blocks += [along_z(ahead[:half], 2), along_z(behind[half:], -2)]
    blocks += [pieces[5], pieces[6], pieces[7]]
    cs = call(trig_far_kernel, cs_shape, 5, scalars=1, aliases={4: 0})(
        scal, pieces[2], pieces[6], trig[2], trig[0]
    )
    kvrel = trig[1]

    def spectra(dc, dtype):
        return call(
            lambda *refs: spectra_kernel(dc, *refs),
            shape((n_xy, 32, 2 * width), dtype),
            1 + len(blocks),
        )(cs, *blocks)

    theirs = across(spectra(1, BF16))
    mine = (spectra(0, F32) + theirs.astype(F32)).astype(BF16)
    arrived = lax.all_to_all(mine, XY, 0, 0, tiled=True)
    copies, grad_filter = call(
        lambda *refs: filter_kernel(spec_scale, wave_scale, *refs),
        (shape((n_xy, 32, 2 * width), BF16), shape((16, width), F32)),
        2,
    )(arrived, filter_gain)
    near = lax.all_to_all(copies, XY, 0, 0, tiled=True)
    far = across(near)
    gf, gp = call(
        grads_near_kernel,
        (shape((beads_grp, width), F32), shape((8, beads_grp), F32)),
        3 + len(blocks),
    )(cs, kvrel, near, *blocks)
    parts = call(
        lambda *refs: grads_far_kernel(spec_scale, *refs),
        shape((n_z, beads_dev + 8, width), BF16),
        6 + len(blocks),
        scalars=1,
    )(scal, cs, kvrel, far, gf, gp, *blocks)
    grad_feat, grad_pos = call(
        total_kernel, (shape((beads_dev, width), BF16), shape((3, beads_dev), F32)), 1
    )(lax.all_to_all(parts, Z, 0, 0, tiled=True))
    return grad_feat, grad_pos, grad_filter


def solution(mesh):
    torus = Mesh(mesh.devices.reshape(4, 4, 2, 2, mesh.shape["waves"]), ALL)
    beads = ("x", "y", "zh", "core")
    return jax.shard_map(
        body,
        mesh=torus,
        in_specs=(P(None, beads), P(ALL, None), P(ALL, None), P(), P(ALL, None)),
        out_specs=(P(ALL, None), P(None, ALL), P(ALL, None)),
        check_vma=False,
    )
```

```python
import math

import jax
import jax.numpy as jnp
from jax import lax
from jax.experimental import pallas as pl
from jax.experimental.pallas import tpu as pltpu
from jax.sharding import Mesh
from jax.sharding import PartitionSpec as P

ALL = ("x", "y", "zh", "core", "zl")
Z = ("zh", "zl")
XY = ("x", "y")
BF16 = jnp.bfloat16
F32 = jnp.float32
LANES = 128

SIN_TURN = (6.28318501, -41.3416557, 81.6010056, -76.5497818, 39.536705)


def sin_turn(h):
    s = h * h
    poly = SIN_TURN[-1]
    for c in SIN_TURN[-2::-1]:
        poly = poly * s + c
    return poly * h


def load_kernel(cot, feat, pos, own, sent, pos_near, sems):
    beads, width = cot.shape
    copies = [
        pltpu.make_async_copy(cot, own.at[:, :width], sems.at[0]),
        pltpu.make_async_copy(feat, own.at[:, width:], sems.at[1]),
        pltpu.make_async_copy(pos, pos_near, sems.at[2]),
    ]
    for c in copies:
        c.start()
    for c in copies:
        c.wait()
    sent[:beads, :] = own[...]
    left = pos_near[...]
    parts = []
    for _ in range(3):
        part = left.astype(BF16).astype(F32)
        parts.append(part)
        left = left - part
    parts.append(jnp.zeros((7, left.shape[1]), F32))
    sent[beads:, :] = jnp.concatenate(parts, 0).astype(BF16)


def trig_rows(kcols, pos, cs, zh, zl, first):
    n_xy = cs.shape[1]
    n_z = cs.shape[4] // LANES
    n_zl = n_z // 2
    columns = [
        pl.multiple_of(lax.rem(zh * n_zl + zl + n_z - first - i, n_z) * LANES, LANES)
        for i in range(n_zl)
    ]

    def step(i, carry):
        dc, xy = i // n_xy, lax.rem(i, n_xy)
        cols = kcols[pl.ds(pl.multiple_of(i * 16, 16), 16), :]
        t = cols[:, 0:1] * pos[0:1] + cols[:, 1:2] * pos[1:2] + cols[:, 2:3] * pos[2:3]
        f = t - jnp.round(t)
        cosine = sin_turn(0.25 - jnp.abs(f)).astype(BF16)
        sine = sin_turn(jnp.maximum(jnp.minimum(f, 0.5 - f), -0.5 - f)).astype(BF16)
        for j, column in enumerate(columns):
            part = slice(j * LANES, (j + 1) * LANES)
            cs[dc, xy, 0, :, pl.ds(column, LANES)] = cosine[:, part]
            cs[dc, xy, 1, :, pl.ds(column, LANES)] = sine[:, part]
        return carry

    lax.fori_loop(0, 2 * n_xy, step, 0, unroll=4)


def trig_near_kernel(scal, pos, wv, cs, kvrel, kcols, kvt):
    zh, zl, core = scal[0], scal[1], scal[2]
    n_xy = cs.shape[1]
    n_zl = cs.shape[4] // LANES // 2
    for xy in range(n_xy):
        at = pl.multiple_of((xy * 2 + zh) * LANES, LANES)
        piece = wv[:, pl.ds(at, LANES)]
        piece = jnp.concatenate([piece, jnp.zeros((5, LANES), F32)], 0)
        kvt[xy, :, 0:8] = piece.T
    for dc in range(2):
        at = pl.multiple_of((jnp.bitwise_xor(core, dc) * n_zl + zl) * 16, 16)
        for xy in range(n_xy):
            cols = kvt[xy, pl.ds(at, 16), 0:8]
            rows = slice((dc * n_xy + xy) * 16, (dc * n_xy + xy + 1) * 16)
            hi = cols.astype(BF16)
            lo = (cols - hi.astype(F32)).astype(BF16)
            kvrel[rows, :] = jnp.concatenate([hi, lo], 1)
            kcols[rows, :] = cols * (1.0 / (2.0 * math.pi))
    trig_rows(kcols, pos[...], cs, zh, zl, zh * n_zl)


def trig_far_kernel(scal, ahead, behind, kcols, _, cs):
    zh, zl = scal[0], scal[1]
    n_zl = cs.shape[4] // LANES // 2
    beads = ahead.shape[0] - 16
    rows = jnp.where(zl < n_zl // 2, ahead[beads:, :], behind[beads:, :]).astype(F32)
    pos = rows[0:3] + rows[3:6] + rows[6:9]
    trig_rows(kcols, pos, cs, zh, zl, jnp.bitwise_xor(zh, 1) * n_zl)


def spectra_kernel(dc, cs, *refs):
    pieces, out = refs[:-1], refs[-1]
    n_xy, _, _, beads = cs.shape[1:]
    beads_all = jnp.concatenate([p[: min(LANES, p.shape[0])] for p in pieces], 0)
    rows = cs[dc].reshape(n_xy * 32, beads)
    part = jnp.dot(rows, beads_all, preferred_element_type=F32)
    out[...] = part.reshape(out.shape).astype(out.dtype)


def filter_kernel(spec_scale, wave_scale, arrived, gain, out, grad_filter):
    n = arrived.shape[0]
    width = gain.shape[1]
    total = arrived[0].astype(F32)
    for i in range(1, n):
        total = total + arrived[i].astype(F32)
    total = total.reshape(2, 16, 2 * width)
    cot = total[:, :, :width] * wave_scale
    spec = total[:, :, width:] * spec_scale
    g = gain[...].astype(F32)
    grad_filter[...] = cot[0] * spec[0] + cot[1] * spec[1]
    filt = (g[None] * spec * (wave_scale / spec_scale)).astype(BF16)
    dspec = (g[None] * cot).astype(BF16)
    both = jnp.concatenate([filt, dspec], 2).reshape(32, 2 * width)
    for i in range(n):
        out[i] = both


def half_gradients(dc, cs, kvrel, stacked, beads_all):
    n_xy, beads = cs.shape[1], cs.shape[4]
    width = beads_all.shape[1] // 2
    both = stacked[...].reshape(n_xy * 32, 2 * width)
    ab = lax.dot_general(both, beads_all, (((1,), (1,)), ((), ())), preferred_element_type=F32)
    ab = ab.reshape(n_xy, 2, 16, beads)
    d = cs[dc, :, 0].astype(F32) * ab[:, 1] - cs[dc, :, 1].astype(F32) * ab[:, 0]
    d = d.reshape(n_xy * 16, beads).astype(BF16)
    kv = kvrel[dc * n_xy * 16 : (dc + 1) * n_xy * 16, :]
    gp = lax.dot_general(kv, d, (((0,), (0,)), ((), ())), preferred_element_type=F32)
    rows = cs[dc].reshape(n_xy * 32, beads)
    gf = lax.dot_general(
        rows, both[:, width:], (((0,), (0,)), ((), ())), preferred_element_type=F32
    )
    return gf, gp[0:8] + gp[8:16]


def grads_near_kernel(cs, kvrel, stacked, *refs):
    pieces, (gf_out, gp_out) = refs[:-2], refs[-2:]
    beads_all = jnp.concatenate([p[: min(LANES, p.shape[0])] for p in pieces], 0)
    gf, gp = half_gradients(0, cs, kvrel, stacked, beads_all)
    gf_out[...] = gf
    gp_out[...] = gp


def grads_far_kernel(spec_scale, scal, cs, kvrel, stacked, gf_in, gp_in, *refs):
    pieces, out = refs[:-1], refs[-1]
    beads_all = jnp.concatenate([p[: min(LANES, p.shape[0])] for p in pieces], 0)
    gf, gp = half_gradients(1, cs, kvrel, stacked, beads_all)
    gf = ((gf + gf_in[...]) * spec_scale).astype(BF16)
    gp = (gp + gp_in[...]) * spec_scale
    hi = gp.astype(BF16)
    lo = (gp - hi.astype(F32)).astype(BF16)
    n_z = out.shape[0]
    here = scal[0] * (n_z // 2) + scal[1]
    for shift in range(n_z):
        at = slice(shift * LANES, (shift + 1) * LANES)
        to = lax.rem(here + n_z - shift, n_z)
        out[to, 0:LANES, :] = gf[at]
        out[to, LANES : LANES + 8, :] = jnp.concatenate([hi[:, at], lo[:, at]], 1)


def total_kernel(arrived, gf_out, gp_out):
    total = arrived[0].astype(F32)
    for i in range(1, arrived.shape[0]):
        total = total + arrived[i].astype(F32)
    gf_out[...] = total[:LANES].astype(BF16)
    tail = total[LANES : LANES + 8]
    gp_out[...] = (tail[:, :LANES] + tail[:, LANES:])[0:3]


def call(kernel, out_shape, n_in, scalars=0, scratch=(), aliases=None, space=pltpu.VMEM):
    specs = [pl.BlockSpec(memory_space=pltpu.SMEM)] * scalars
    specs += [pl.BlockSpec(memory_space=space)] * (n_in - scalars)
    outs = jax.tree.map(lambda _: pl.BlockSpec(memory_space=pltpu.VMEM), out_shape)
    return pl.pallas_call(
        kernel,
        out_shape=out_shape,
        in_specs=specs,
        out_specs=outs,
        scratch_shapes=scratch,
        input_output_aliases=aliases or {},
        compiler_params=pltpu.CompilerParams(vmem_limit_bytes=16 << 20),
    )


def shape(dims, dtype):
    return jax.ShapeDtypeStruct(dims, dtype)


def body(positions, features, cotangent, wavevectors, filter_gain):
    n_z = lax.axis_size(Z)
    n_xy = lax.axis_size(XY)
    beads_dev, width = features.shape
    beads_grp = beads_dev * n_z
    n_beads = beads_grp * n_xy * 2
    spec_scale = 1.0 / math.sqrt(n_beads)
    wave_scale = 1.0 / math.sqrt(wavevectors.shape[1])

    def along_z(a, k):
        return lax.ppermute(a, Z, [(i, (i + k) % n_z) for i in range(n_z)])

    def across(a):
        return lax.ppermute(a, "core", [(0, 1), (1, 0)])

    inputs = [pltpu.with_memory_space_constraint(a, pltpu.HBM) for a in (cotangent, features, positions)]
    own, sent, pos_near = call(
        load_kernel,
        (
            shape((beads_dev, 2 * width), BF16),
            shape((beads_dev + 16, 2 * width), BF16),
            shape(positions.shape, F32),
        ),
        3,
        scratch=[pltpu.SemaphoreType.DMA((3,))],
        space=pltpu.HBM,
    )(*inputs)
    pieces = {0: own, 2: along_z(sent, 2), 6: along_z(sent, -2)}

    scal = jnp.stack([lax.axis_index("zh"), lax.axis_index("zl"), lax.axis_index("core")])
    scal = scal.astype(jnp.int32)
    n_rows = 2 * n_xy * 16
    cs_shape = shape((2, n_xy, 2, 16, beads_grp), BF16)
    trig = call(
        trig_near_kernel,
        (cs_shape, shape((n_rows, 16), BF16), shape((n_rows, 8), F32)),
        3,
        scalars=1,
        scratch=[pltpu.VMEM((n_xy, LANES, 8), F32)],
    )(scal, pos_near, wavevectors)
    own, trig = lax.optimization_barrier((own, trig))
    pieces[1], pieces[7] = along_z(own, 1), along_z(own, -1)
    pieces[2], pieces[6], trig = lax.optimization_barrier((pieces[2], pieces[6], trig))
    ahead, behind = pieces[2][:beads_dev], pieces[6][:beads_dev]
    half = beads_dev // 2
    pieces[3], pieces[5] = along_z(ahead, 1), along_z(behind, -1)
    blocks = [pieces[0], pieces[1], pieces[2], pieces[3]]
    blocks += [along_z(ahead[:half], 2), along_z(behind[half:], -2)]
    blocks += [pieces[5], pieces[6], pieces[7]]
    cs = call(trig_far_kernel, cs_shape, 5, scalars=1, aliases={4: 0})(
        scal, pieces[2], pieces[6], trig[2], trig[0]
    )
    kvrel = trig[1]

    def spectra(dc, dtype):
        return call(
            lambda *refs: spectra_kernel(dc, *refs),
            shape((n_xy, 32, 2 * width), dtype),
            1 + len(blocks),
        )(cs, *blocks)

    theirs = across(spectra(1, BF16))
    mine = (spectra(0, F32) + theirs.astype(F32)).astype(BF16)
    arrived = lax.all_to_all(mine, XY, 0, 0, tiled=True)
    copies, grad_filter = call(
        lambda *refs: filter_kernel(spec_scale, wave_scale, *refs),
        (shape((n_xy, 32, 2 * width), BF16), shape((16, width), F32)),
        2,
    )(arrived, filter_gain)
    near = lax.all_to_all(copies, XY, 0, 0, tiled=True)
    far = across(near)
    gf, gp = call(
        grads_near_kernel,
        (shape((beads_grp, width), F32), shape((8, beads_grp), F32)),
        3 + len(blocks),
    )(cs, kvrel, near, *blocks)
    parts = call(
        lambda *refs: grads_far_kernel(spec_scale, *refs),
        shape((n_z, beads_dev + 8, width), BF16),
        6 + len(blocks),
        scalars=1,
    )(scal, cs, kvrel, far, gf, gp, *blocks)
    grad_feat, grad_pos = call(
        total_kernel, (shape((beads_dev, width), BF16), shape((3, beads_dev), F32)), 1
    )(lax.all_to_all(parts, Z, 0, 0, tiled=True))
    return grad_feat, grad_pos, grad_filter


def solution(mesh):
    torus = Mesh(mesh.devices.reshape(4, 4, 2, 2, mesh.shape["waves"]), ALL)
    beads = ("x", "y", "zh", "core")
    return jax.shard_map(
        body,
        mesh=torus,
        in_specs=(P(None, beads), P(ALL, None), P(ALL, None), P(), P(ALL, None)),
        out_specs=(P(ALL, None), P(None, ALL), P(ALL, None)),
        check_vma=False,
    )
```

```python
import math

import jax
import jax.numpy as jnp
from jax import lax
from jax.experimental import pallas as pl
from jax.experimental.pallas import tpu as pltpu
from jax.sharding import Mesh
from jax.sharding import PartitionSpec as P

ALL = ("x", "y", "zh", "core", "zl")
Z = ("zh", "zl")
XY = ("x", "y")
BF16 = jnp.bfloat16
F32 = jnp.float32
LANES = 128

SIN_TURN = (6.28318501, -41.3416557, 81.6010056, -76.5497818, 39.536705)


def sin_turn(h):
    s = h * h
    poly = SIN_TURN[-1]
    for c in SIN_TURN[-2::-1]:
        poly = poly * s + c
    return poly * h


def load_kernel(cot, feat, pos, wv, own, sent, pos_near, wv_near, sems):
    beads, width = cot.shape
    copies = [
        pltpu.make_async_copy(cot, own.at[:, :width], sems.at[0]),
        pltpu.make_async_copy(feat, own.at[:, width:], sems.at[1]),
        pltpu.make_async_copy(pos, pos_near, sems.at[2]),
        pltpu.make_async_copy(wv, wv_near, sems.at[3]),
    ]
    for c in copies:
        c.start()
    for c in copies:
        c.wait()
    sent[:beads, :] = own[...]
    left = pos_near[...]
    parts = []
    for _ in range(3):
        part = left.astype(BF16).astype(F32)
        parts.append(part)
        left = left - part
    parts.append(jnp.zeros((7, left.shape[1]), F32))
    sent[beads:, :] = jnp.concatenate(parts, 0).astype(BF16)


def trig_rows(kcols, pos, cs, zh, zl, first):
    n_xy = cs.shape[1]
    n_z = cs.shape[4] // LANES
    n_zl = n_z // 2
    columns = [
        pl.multiple_of(lax.rem(zh * n_zl + zl + n_z - first - i, n_z) * LANES, LANES)
        for i in range(n_zl)
    ]

    def step(i, carry):
        dc, xy = i // n_xy, lax.rem(i, n_xy)
        cols = kcols[pl.ds(pl.multiple_of(i * 16, 16), 16), :]
        t = cols[:, 0:1] * pos[0:1] + cols[:, 1:2] * pos[1:2] + cols[:, 2:3] * pos[2:3]
        f = t - jnp.round(t)
        cosine = sin_turn(0.25 - jnp.abs(f)).astype(BF16)
        sine = sin_turn(jnp.maximum(jnp.minimum(f, 0.5 - f), -0.5 - f)).astype(BF16)
        for j, column in enumerate(columns):
            part = slice(j * LANES, (j + 1) * LANES)
            cs[dc, xy, 0, :, pl.ds(column, LANES)] = cosine[:, part]
            cs[dc, xy, 1, :, pl.ds(column, LANES)] = sine[:, part]
        return carry

    lax.fori_loop(0, 2 * n_xy, step, 0, unroll=4)


def trig_near_kernel(scal, pos, wv, cs, kvrel, kcols, kvt):
    zh, zl, core = scal[0], scal[1], scal[2]
    n_xy = cs.shape[1]
    n_zl = cs.shape[4] // LANES // 2
    for xy in range(n_xy):
        at = pl.multiple_of((xy * 2 + zh) * LANES, LANES)
        piece = wv[:, pl.ds(at, LANES)]
        piece = jnp.concatenate([piece, jnp.zeros((5, LANES), F32)], 0)
        kvt[xy, :, 0:8] = piece.T
    for dc in range(2):
        at = pl.multiple_of((jnp.bitwise_xor(core, dc) * n_zl + zl) * 16, 16)
        for xy in range(n_xy):
            cols = kvt[xy, pl.ds(at, 16), 0:8]
            rows = slice((dc * n_xy + xy) * 16, (dc * n_xy + xy + 1) * 16)
            hi = cols.astype(BF16)
            lo = (cols - hi.astype(F32)).astype(BF16)
            kvrel[rows, :] = jnp.concatenate([hi, lo], 1)
            kcols[rows, :] = cols * (1.0 / (2.0 * math.pi))
    trig_rows(kcols, pos[...], cs, zh, zl, zh * n_zl)


def trig_far_kernel(scal, ahead, behind, kcols, _, cs):
    zh, zl = scal[0], scal[1]
    n_zl = cs.shape[4] // LANES // 2
    beads = ahead.shape[0] - 16
    rows = jnp.where(zl < n_zl // 2, ahead[beads:, :], behind[beads:, :]).astype(F32)
    pos = rows[0:3] + rows[3:6] + rows[6:9]
    trig_rows(kcols, pos, cs, zh, zl, jnp.bitwise_xor(zh, 1) * n_zl)


def joined(pieces):
    return jnp.concatenate([p[:LANES] for p in pieces], 0)


def early_kernel(cs, *refs):
    pieces, out = refs[:-1], refs[-1]
    rows = cs[...].reshape(-1, cs.shape[4])
    n = 3 * LANES
    near = jnp.dot(rows[:, :n], joined(pieces[:3]), preferred_element_type=F32)
    m = rows.shape[1] - 2 * LANES
    near += jnp.dot(rows[:, m:], joined(pieces[3:]), preferred_element_type=F32)
    out[...] = near.reshape(out.shape)


def late_kernel(dc, cs, early, *refs):
    pieces, out = refs[:-1], refs[-1]
    rows = cs[dc].reshape(-1, cs.shape[4])
    m = rows.shape[1] - 2 * LANES
    part = jnp.dot(rows[:, 3 * LANES : m], joined(pieces), preferred_element_type=F32)
    out[...] = (part.reshape(out.shape) + early[dc]).astype(out.dtype)


def filter_kernel(spec_scale, wave_scale, arrived, gain, out, grad_filter):
    n = arrived.shape[0]
    width = gain.shape[1]
    total = arrived[0].astype(F32)
    for i in range(1, n):
        total = total + arrived[i].astype(F32)
    total = total.reshape(2, 16, 2 * width)
    cot = total[:, :, :width] * wave_scale
    spec = total[:, :, width:] * spec_scale
    g = gain[...].astype(F32)
    grad_filter[...] = cot[0] * spec[0] + cot[1] * spec[1]
    filt = (g[None] * spec * (wave_scale / spec_scale)).astype(BF16)
    dspec = (g[None] * cot).astype(BF16)
    both = jnp.concatenate([filt, dspec], 2).reshape(32, 2 * width)
    for i in range(n):
        out[i] = both


def half_gradients(dc, cs, kvrel, stacked, beads_all):
    n_xy, beads = cs.shape[1], cs.shape[4]
    width = beads_all.shape[1] // 2
    both = stacked[...].reshape(n_xy * 32, 2 * width)
    ab = lax.dot_general(both, beads_all, (((1,), (1,)), ((), ())), preferred_element_type=F32)
    ab = ab.reshape(n_xy, 2, 16, beads)
    d = cs[dc, :, 0].astype(F32) * ab[:, 1] - cs[dc, :, 1].astype(F32) * ab[:, 0]
    d = d.reshape(n_xy * 16, beads).astype(BF16)
    kv = kvrel[dc * n_xy * 16 : (dc + 1) * n_xy * 16, :]
    gp = lax.dot_general(kv, d, (((0,), (0,)), ((), ())), preferred_element_type=F32)
    rows = cs[dc].reshape(n_xy * 32, beads)
    gf = lax.dot_general(
        rows, both[:, width:], (((0,), (0,)), ((), ())), preferred_element_type=F32
    )
    return gf, gp[0:8] + gp[8:16]


def grads_near_kernel(cs, kvrel, stacked, *refs):
    pieces, (gf_out, gp_out) = refs[:-2], refs[-2:]
    beads_all = joined(pieces)
    gf, gp = half_gradients(0, cs, kvrel, stacked, beads_all)
    gf_out[...] = gf
    gp_out[...] = gp


def grads_far_kernel(spec_scale, scal, cs, kvrel, stacked, gf_in, gp_in, *refs):
    pieces, out = refs[:-1], refs[-1]
    beads_all = joined(pieces)
    gf, gp = half_gradients(1, cs, kvrel, stacked, beads_all)
    gf = ((gf + gf_in[...]) * spec_scale).astype(BF16)
    gp = (gp + gp_in[...]) * spec_scale
    hi = gp.astype(BF16)
    lo = (gp - hi.astype(F32)).astype(BF16)
    n_z = out.shape[0]
    here = scal[0] * (n_z // 2) + scal[1]
    for shift in range(n_z):
        at = slice(shift * LANES, (shift + 1) * LANES)
        to = lax.rem(here + n_z - shift, n_z)
        out[to, 0:LANES, :] = gf[at]
        out[to, LANES : LANES + 8, :] = jnp.concatenate([hi[:, at], lo[:, at]], 1)


def total_kernel(arrived, gf_out, gp_out):
    total = arrived[0].astype(F32)
    for i in range(1, arrived.shape[0]):
        total = total + arrived[i].astype(F32)
    gf_out[...] = total[:LANES].astype(BF16)
    tail = total[LANES : LANES + 8]
    gp_out[...] = (tail[:, :LANES] + tail[:, LANES:])[0:3]


def call(kernel, out_shape, n_in, scalars=0, scratch=(), aliases=None, space=pltpu.VMEM):
    specs = [pl.BlockSpec(memory_space=pltpu.SMEM)] * scalars
    specs += [pl.BlockSpec(memory_space=space)] * (n_in - scalars)
    outs = jax.tree.map(lambda _: pl.BlockSpec(memory_space=pltpu.VMEM), out_shape)
    return pl.pallas_call(
        kernel,
        out_shape=out_shape,
        in_specs=specs,
        out_specs=outs,
        scratch_shapes=scratch,
        input_output_aliases=aliases or {},
        compiler_params=pltpu.CompilerParams(vmem_limit_bytes=16 << 20),
    )


def shape(dims, dtype):
    return jax.ShapeDtypeStruct(dims, dtype)


def body(positions, features, cotangent, wavevectors, filter_gain):
    n_z = lax.axis_size(Z)
    n_xy = lax.axis_size(XY)
    beads_dev, width = features.shape
    beads_grp = beads_dev * n_z
    n_beads = beads_grp * n_xy * 2
    spec_scale = 1.0 / math.sqrt(n_beads)
    wave_scale = 1.0 / math.sqrt(wavevectors.shape[1])

    def along_z(a, k):
        return lax.ppermute(a, Z, [(i, (i + k) % n_z) for i in range(n_z)])

    def across(a):
        return lax.ppermute(a, "core", [(0, 1), (1, 0)])

    inputs = (cotangent, features, positions, wavevectors)
    inputs = [pltpu.with_memory_space_constraint(a, pltpu.HBM) for a in inputs]
    own, sent, pos_near, wv_near = call(
        load_kernel,
        (
            shape((beads_dev, 2 * width), BF16),
            shape((beads_dev + 16, 2 * width), BF16),
            shape(positions.shape, F32),
            shape(wavevectors.shape, F32),
        ),
        4,
        scratch=[pltpu.SemaphoreType.DMA((4,))],
        space=pltpu.HBM,
    )(*inputs)
    pieces = {0: own, 2: along_z(sent, 2), 6: along_z(sent, -2)}

    scal = jnp.stack([lax.axis_index("zh"), lax.axis_index("zl"), lax.axis_index("core")])
    scal = scal.astype(jnp.int32)
    n_rows = 2 * n_xy * 16
    cs_shape = shape((2, n_xy, 2, 16, beads_grp), BF16)
    trig = call(
        trig_near_kernel,
        (cs_shape, shape((n_rows, 16), BF16), shape((n_rows, 8), F32)),
        3,
        scalars=1,
        scratch=[pltpu.VMEM((n_xy, LANES, 8), F32)],
    )(scal, pos_near, wv_near)
    own, trig = lax.optimization_barrier((own, trig))
    pieces[1], pieces[7] = along_z(own, 1), along_z(own, -1)
    pieces[2], pieces[6], trig = lax.optimization_barrier((pieces[2], pieces[6], trig))
    ahead, behind = pieces[2][:beads_dev], pieces[6][:beads_dev]
    onward = jnp.where(lax.axis_index("core") == 0, ahead, behind)
    n_zl = lax.axis_size("zl")

    def at(z, core):
        return (z // n_zl * 2 + core) * n_zl + z % n_zl

    pairs = [(at(z, c), at((z + 2 - 4 * c) % n_z, c)) for z in range(n_z) for c in range(2)]
    pieces[4] = lax.ppermute(onward, ("zh", "core", "zl"), pairs)
    pieces[3], pieces[5] = along_z(ahead, 1), along_z(behind, -1)
    blocks = [pieces[k] for k in range(n_z)]
    cs = call(trig_far_kernel, cs_shape, 5, scalars=1, aliases={4: 0})(
        scal, pieces[2], pieces[6], trig[2], trig[0]
    )
    kvrel = trig[1]

    near_blocks = [blocks[k] for k in (0, 1, 2, n_z - 2, n_z - 1)]
    late_blocks = [blocks[k] for k in range(3, n_z - 2)]
    early = call(
        early_kernel, shape((2, n_xy, 32, 2 * width), F32), 1 + len(near_blocks)
    )(cs, *near_blocks)

    def spectra(dc, dtype):
        return call(
            lambda *refs: late_kernel(dc, *refs),
            shape((n_xy, 32, 2 * width), dtype),
            2 + len(late_blocks),
        )(cs, early, *late_blocks)

    theirs = across(spectra(1, BF16))
    mine = (spectra(0, F32) + theirs.astype(F32)).astype(BF16)
    arrived = lax.all_to_all(mine, XY, 0, 0, tiled=True)
    copies, grad_filter = call(
        lambda *refs: filter_kernel(spec_scale, wave_scale, *refs),
        (shape((n_xy, 32, 2 * width), BF16), shape((16, width), F32)),
        2,
    )(arrived, filter_gain)
    near = lax.all_to_all(copies, XY, 0, 0, tiled=True)
    far = across(near)
    gf, gp = call(
        grads_near_kernel,
        (shape((beads_grp, width), F32), shape((8, beads_grp), F32)),
        3 + len(blocks),
    )(cs, kvrel, near, *blocks)
    parts = call(
        lambda *refs: grads_far_kernel(spec_scale, *refs),
        shape((n_z, beads_dev + 8, width), BF16),
        6 + len(blocks),
        scalars=1,
    )(scal, cs, kvrel, far, gf, gp, *blocks)
    grad_feat, grad_pos = call(
        total_kernel, (shape((beads_dev, width), BF16), shape((3, beads_dev), F32)), 1
    )(lax.all_to_all(parts, Z, 0, 0, tiled=True))
    return grad_feat, grad_pos, grad_filter


def solution(mesh):
    torus = Mesh(mesh.devices.reshape(4, 4, 2, 2, mesh.shape["waves"]), ALL)
    beads = ("x", "y", "zh", "core")
    return jax.shard_map(
        body,
        mesh=torus,
        in_specs=(P(None, beads), P(ALL, None), P(ALL, None), P(), P(ALL, None)),
        out_specs=(P(ALL, None), P(None, ALL), P(ALL, None)),
        check_vma=False,
    )
```

```python
import math

import jax
import jax.numpy as jnp
from jax import lax
from jax.experimental import pallas as pl
from jax.experimental.pallas import tpu as pltpu
from jax.sharding import Mesh
from jax.sharding import PartitionSpec as P


ALL = ("x", "y", "zh", "core", "zl")
Z = ("zh", "zl")
XY = ("x", "y")
BF16 = jnp.bfloat16
F32 = jnp.float32
LANES = 128

SIN_TURN = (6.28318501, -41.3416557, 81.6010056, -76.5497818, 39.536705)


def sin_turn(h):
    s = h * h
    poly = SIN_TURN[-1]
    for c in SIN_TURN[-2::-1]:
        poly = poly * s + c
    return poly * h


def load_kernel(cot, feat, pos, wv, own, sent, pos_near, wv_near, sems):
    beads, width = cot.shape
    copies = [
        pltpu.make_async_copy(cot, own.at[:, :width], sems.at[0]),
        pltpu.make_async_copy(feat, own.at[:, width:], sems.at[1]),
        pltpu.make_async_copy(pos, pos_near, sems.at[2]),
        pltpu.make_async_copy(wv, wv_near, sems.at[3]),
    ]
    for c in copies:
        c.start()
    for c in copies:
        c.wait()
    sent[:beads, :] = own[...]
    left = pos_near[...]
    parts = []
    for _ in range(3):
        part = left.astype(BF16).astype(F32)
        parts.append(part)
        left = left - part
    parts.append(jnp.zeros((7, left.shape[1]), F32))
    sent[beads:, :] = jnp.concatenate(parts, 0).astype(BF16)


def trig_rows(kcols, pos, cs, zh, zl, first):
    n_xy = cs.shape[1]
    n_z = cs.shape[4] // LANES
    n_zl = n_z // 2
    columns = [
        pl.multiple_of(lax.rem(zh * n_zl + zl + n_z - first - i, n_z) * LANES, LANES)
        for i in range(n_zl)
    ]

    def step(i, carry):
        dc, xy = i // n_xy, lax.rem(i, n_xy)
        cols = kcols[pl.ds(pl.multiple_of(i * 16, 16), 16), :]
        t = cols[:, 0:1] * pos[0:1] + cols[:, 1:2] * pos[1:2] + cols[:, 2:3] * pos[2:3]
        f = t - jnp.round(t)
        cosine = sin_turn(0.25 - jnp.abs(f)).astype(BF16)
        sine = sin_turn(jnp.maximum(jnp.minimum(f, 0.5 - f), -0.5 - f)).astype(BF16)
        for j, column in enumerate(columns):
            part = slice(j * LANES, (j + 1) * LANES)
            cs[dc, xy, 0, :, pl.ds(column, LANES)] = cosine[:, part]
            cs[dc, xy, 1, :, pl.ds(column, LANES)] = sine[:, part]
        return carry

    lax.fori_loop(0, 2 * n_xy, step, 0, unroll=4)


def trig_near_kernel(scal, pos, wv, cs, kvrel, kcols, kvt):
    zh, zl, core = scal[0], scal[1], scal[2]
    n_xy = cs.shape[1]
    n_zl = cs.shape[4] // LANES // 2
    for xy in range(n_xy):
        at = pl.multiple_of((xy * 2 + zh) * LANES, LANES)
        piece = wv[:, pl.ds(at, LANES)]
        piece = jnp.concatenate([piece, jnp.zeros((5, LANES), F32)], 0)
        kvt[xy, :, 0:8] = piece.T
    for dc in range(2):
        at = pl.multiple_of((jnp.bitwise_xor(core, dc) * n_zl + zl) * 16, 16)
        for xy in range(n_xy):
            cols = kvt[xy, pl.ds(at, 16), 0:8]
            rows = slice((dc * n_xy + xy) * 16, (dc * n_xy + xy + 1) * 16)
            hi = cols.astype(BF16)
            lo = (cols - hi.astype(F32)).astype(BF16)
            kvrel[rows, :] = jnp.concatenate([hi, lo], 1)
            kcols[rows, :] = cols * (1.0 / (2.0 * math.pi))
    trig_rows(kcols, pos[...], cs, zh, zl, zh * n_zl)


def trig_far_kernel(scal, ahead, behind, kcols, _, cs):
    zh, zl = scal[0], scal[1]
    n_zl = cs.shape[4] // LANES // 2
    beads = ahead.shape[0] - 16
    rows = jnp.where(zl < n_zl // 2, ahead[beads:, :], behind[beads:, :]).astype(F32)
    pos = rows[0:3] + rows[3:6] + rows[6:9]
    trig_rows(kcols, pos, cs, zh, zl, jnp.bitwise_xor(zh, 1) * n_zl)


def joined(pieces):
    return jnp.concatenate([p[:LANES] for p in pieces], 0)


def early_kernel(cs, *refs):
    pieces, out = refs[:-1], refs[-1]
    rows = cs[...].reshape(-1, cs.shape[4])
    n = rows.shape[1] // 2
    first = n // LANES
    near = jnp.dot(rows[:, :n], joined(pieces[:first]), preferred_element_type=F32)
    n += LANES
    near += jnp.dot(rows[:, n:], joined(pieces[first:]), preferred_element_type=F32)
    out[...] = near.reshape(out.shape)


def late_kernel(dc, cs, early, block, out):
    rows = cs[dc].reshape(-1, cs.shape[4])
    n = rows.shape[1] // 2
    part = jnp.dot(rows[:, n : n + LANES], block[...], preferred_element_type=F32)
    out[...] = (part.reshape(out.shape) + early[dc]).astype(out.dtype)


def filter_kernel(spec_scale, wave_scale, arrived, gain, out, grad_filter):
    n = arrived.shape[0]
    width = gain.shape[1]
    total = arrived[0].astype(F32)
    for i in range(1, n):
        total = total + arrived[i].astype(F32)
    total = total.reshape(2, 16, 2 * width)
    cot = total[:, :, :width] * wave_scale
    spec = total[:, :, width:] * spec_scale
    g = gain[...].astype(F32)
    grad_filter[...] = cot[0] * spec[0] + cot[1] * spec[1]
    filt = (g[None] * spec * (wave_scale / spec_scale)).astype(BF16)
    dspec = (g[None] * cot).astype(BF16)
    both = jnp.concatenate([filt, dspec], 2).reshape(32, 2 * width)
    for i in range(n):
        out[i] = both


def half_gradients(dc, cs, kvrel, stacked, beads_all):
    n_xy, beads = cs.shape[1], cs.shape[4]
    width = beads_all.shape[1] // 2
    both = stacked[...].reshape(n_xy * 32, 2 * width)
    ab = lax.dot_general(both, beads_all, (((1,), (1,)), ((), ())), preferred_element_type=F32)
    ab = ab.reshape(n_xy, 2, 16, beads)
    d = cs[dc, :, 0].astype(F32) * ab[:, 1] - cs[dc, :, 1].astype(F32) * ab[:, 0]
    d = d.reshape(n_xy * 16, beads).astype(BF16)
    kv = kvrel[dc * n_xy * 16 : (dc + 1) * n_xy * 16, :]
    gp = lax.dot_general(kv, d, (((0,), (0,)), ((), ())), preferred_element_type=F32)
    rows = cs[dc].reshape(n_xy * 32, beads)
    gf = lax.dot_general(
        rows, both[:, width:], (((0,), (0,)), ((), ())), preferred_element_type=F32
    )
    return gf, gp[0:8] + gp[8:16]


def grads_near_kernel(cs, kvrel, stacked, *refs):
    pieces, (gf_out, gp_out) = refs[:-2], refs[-2:]
    beads_all = joined(pieces)
    gf, gp = half_gradients(0, cs, kvrel, stacked, beads_all)
    gf_out[...] = gf
    gp_out[...] = gp


def grads_far_kernel(spec_scale, scal, cs, kvrel, stacked, gf_in, gp_in, *refs):
    pieces, out = refs[:-1], refs[-1]
    beads_all = joined(pieces)
    gf, gp = half_gradients(1, cs, kvrel, stacked, beads_all)
    gf = ((gf + gf_in[...]) * spec_scale).astype(BF16)
    gp = (gp + gp_in[...]) * spec_scale
    hi = gp.astype(BF16)
    lo = (gp - hi.astype(F32)).astype(BF16)
    n_z = out.shape[0]
    here = scal[0] * (n_z // 2) + scal[1]
    for shift in range(n_z):
        at = slice(shift * LANES, (shift + 1) * LANES)
        to = lax.rem(here + n_z - shift, n_z)
        out[to, 0:LANES, :] = gf[at]
        out[to, LANES : LANES + 8, :] = jnp.concatenate([hi[:, at], lo[:, at]], 1)


def total_kernel(arrived, gf_out, gp_out):
    total = arrived[0].astype(F32)
    for i in range(1, arrived.shape[0]):
        total = total + arrived[i].astype(F32)
    gf_out[...] = total[:LANES].astype(BF16)
    tail = total[LANES : LANES + 8]
    gp_out[...] = (tail[:, :LANES] + tail[:, LANES:])[0:3]


def call(kernel, out_shape, n_in, scalars=0, scratch=(), aliases=None, space=pltpu.VMEM):
    specs = [pl.BlockSpec(memory_space=pltpu.SMEM)] * scalars
    specs += [pl.BlockSpec(memory_space=space)] * (n_in - scalars)
    outs = jax.tree.map(lambda _: pl.BlockSpec(memory_space=pltpu.VMEM), out_shape)
    return pl.pallas_call(
        kernel,
        out_shape=out_shape,
        in_specs=specs,
        out_specs=outs,
        scratch_shapes=scratch,
        input_output_aliases=aliases or {},
        compiler_params=pltpu.CompilerParams(vmem_limit_bytes=16 << 20),
    )


def shape(dims, dtype):
    return jax.ShapeDtypeStruct(dims, dtype)


def body(positions, features, cotangent, wavevectors, filter_gain):
    n_z = lax.axis_size(Z)
    n_xy = lax.axis_size(XY)
    beads_dev, width = features.shape
    beads_grp = beads_dev * n_z
    n_beads = beads_grp * n_xy * 2
    spec_scale = 1.0 / math.sqrt(n_beads)
    wave_scale = 1.0 / math.sqrt(wavevectors.shape[1])

    def along_z(a, k):
        return lax.ppermute(a, Z, [(i, (i + k) % n_z) for i in range(n_z)])

    def across(a):
        return lax.ppermute(a, "core", [(0, 1), (1, 0)])

    inputs = (cotangent, features, positions, wavevectors)
    inputs = [pltpu.with_memory_space_constraint(a, pltpu.HBM) for a in inputs]
    own, sent, pos_near, wv_near = call(
        load_kernel,
        (
            shape((beads_dev, 2 * width), BF16),
            shape((beads_dev + 16, 2 * width), BF16),
            shape(positions.shape, F32),
            shape(wavevectors.shape, F32),
        ),
        4,
        scratch=[pltpu.SemaphoreType.DMA((4,))],
        space=pltpu.HBM,
    )(*inputs)
    pieces = {0: own, 2: along_z(sent, 2), 6: along_z(sent, -2)}

    scal = jnp.stack([lax.axis_index("zh"), lax.axis_index("zl"), lax.axis_index("core")])
    scal = scal.astype(jnp.int32)
    n_rows = 2 * n_xy * 16
    cs_shape = shape((2, n_xy, 2, 16, beads_grp), BF16)
    trig = call(
        trig_near_kernel,
        (cs_shape, shape((n_rows, 16), BF16), shape((n_rows, 8), F32)),
        3,
        scalars=1,
        scratch=[pltpu.VMEM((n_xy, LANES, 8), F32)],
    )(scal, pos_near, wv_near)
    own, trig = lax.optimization_barrier((own, trig))
    pieces[1], pieces[7] = along_z(own, 1), along_z(own, -1)
    pieces[2], pieces[6], trig = lax.optimization_barrier((pieces[2], pieces[6], trig))
    pieces[3] = along_z(pieces[2][:beads_dev], 1)
    pieces[5] = along_z(pieces[6][:beads_dev], -1)
    cs = call(trig_far_kernel, cs_shape, 5, scalars=1, aliases={4: 0})(
        scal, pieces[2], pieces[6], trig[2], trig[0]
    )
    kvrel = trig[1]
    pieces[3], pieces[5], cs = lax.optimization_barrier((pieces[3], pieces[5], cs))
    onward = jnp.where(lax.axis_index("core") == 0, pieces[3], pieces[5])
    n_zl = lax.axis_size("zl")

    def at(z, core):
        return (z // n_zl * 2 + core) * n_zl + z % n_zl

    pairs = [(at(z, c), at((z + 1 - 2 * c) % n_z, c)) for z in range(n_z) for c in range(2)]
    pieces[4] = lax.ppermute(onward, ("zh", "core", "zl"), pairs)
    blocks = [pieces[k] for k in range(n_z)]

    near_blocks = [blocks[k] for k in range(n_z) if k != n_z // 2]
    early = call(
        early_kernel, shape((2, n_xy, 32, 2 * width), F32), 1 + len(near_blocks)
    )(cs, *near_blocks)

    def spectra(dc, dtype):
        return call(
            lambda *refs: late_kernel(dc, *refs),
            shape((n_xy, 32, 2 * width), dtype),
            3,
        )(cs, early, blocks[n_z // 2])

    theirs = across(spectra(1, BF16))
    mine = (spectra(0, F32) + theirs.astype(F32)).astype(BF16)
    arrived = lax.all_to_all(mine, XY, 0, 0, tiled=True)
    copies, grad_filter = call(
        lambda *refs: filter_kernel(spec_scale, wave_scale, *refs),
        (shape((n_xy, 32, 2 * width), BF16), shape((16, width), F32)),
        2,
    )(arrived, filter_gain)
    near = lax.all_to_all(copies, XY, 0, 0, tiled=True)
    far = across(near)
    gf, gp = call(
        grads_near_kernel,
        (shape((beads_grp, width), F32), shape((8, beads_grp), F32)),
        3 + len(blocks),
    )(cs, kvrel, near, *blocks)
    parts = call(
        lambda *refs: grads_far_kernel(spec_scale, *refs),
        shape((n_z, beads_dev + 8, width), BF16),
        6 + len(blocks),
        scalars=1,
    )(scal, cs, kvrel, far, gf, gp, *blocks)
    grad_feat, grad_pos = call(
        total_kernel, (shape((beads_dev, width), BF16), shape((3, beads_dev), F32)), 1
    )(lax.all_to_all(parts, Z, 0, 0, tiled=True))
    return grad_feat, grad_pos, grad_filter


def solution(mesh):
    torus = Mesh(mesh.devices.reshape(4, 4, 2, 2, mesh.shape["waves"]), ALL)
    beads = ("x", "y", "zh", "core")
    return jax.shard_map(
        body,
        mesh=torus,
        in_specs=(P(None, beads), P(ALL, None), P(ALL, None), P(), P(ALL, None)),
        out_specs=(P(ALL, None), P(None, ALL), P(ALL, None)),
        check_vma=False,
    )
```

```python
import math

import jax
import jax.numpy as jnp
from jax import lax
from jax.experimental import pallas as pl
from jax.experimental.pallas import tpu as pltpu
from jax.sharding import Mesh
from jax.sharding import PartitionSpec as P


ALL = ("x", "y", "zh", "core", "zl")
Z = ("zh", "zl")
XY = ("x", "y")
BF16 = jnp.bfloat16
F32 = jnp.float32
LANES = 128

SIN_TURN = (6.28318501, -41.3416557, 81.6010056, -76.5497818, 39.536705)


def sin_turn(h):
    s = h * h
    poly = SIN_TURN[-1]
    for c in SIN_TURN[-2::-1]:
        poly = poly * s + c
    return poly * h


def load_kernel(cot, feat, pos, wv, own, sent, pos_near, wv_near, sems):
    beads, width = cot.shape
    copies = [
        pltpu.make_async_copy(cot, own.at[:, :width], sems.at[0]),
        pltpu.make_async_copy(feat, own.at[:, width:], sems.at[1]),
        pltpu.make_async_copy(pos, pos_near, sems.at[2]),
        pltpu.make_async_copy(wv, wv_near, sems.at[3]),
    ]
    for c in copies:
        c.start()
    for c in copies:
        c.wait()
    sent[:beads, :] = own[...]
    left = pos_near[...]
    parts = []
    for _ in range(3):
        part = left.astype(BF16).astype(F32)
        parts.append(part)
        left = left - part
    parts.append(jnp.zeros((7, left.shape[1]), F32))
    sent[beads:, :] = jnp.concatenate(parts, 0).astype(BF16)


def trig_rows(kcols, pos, cs, zh, zl, first):
    n_xy = cs.shape[1]
    n_z = cs.shape[4] // LANES
    n_zl = n_z // 2
    columns = [
        pl.multiple_of(lax.rem(zh * n_zl + zl + n_z - first - i, n_z) * LANES, LANES)
        for i in range(n_zl)
    ]

    def step(i, carry):
        dc, xy = i // n_xy, lax.rem(i, n_xy)
        cols = kcols[pl.ds(pl.multiple_of(i * 16, 16), 16), :]
        t = cols[:, 0:1] * pos[0:1] + cols[:, 1:2] * pos[1:2] + cols[:, 2:3] * pos[2:3]
        f = t - jnp.round(t)
        cosine = sin_turn(0.25 - jnp.abs(f)).astype(BF16)
        sine = sin_turn(jnp.maximum(jnp.minimum(f, 0.5 - f), -0.5 - f)).astype(BF16)
        for j, column in enumerate(columns):
            part = slice(j * LANES, (j + 1) * LANES)
            cs[dc, xy, 0, :, pl.ds(column, LANES)] = cosine[:, part]
            cs[dc, xy, 1, :, pl.ds(column, LANES)] = sine[:, part]
        return carry

    lax.fori_loop(0, 2 * n_xy, step, 0, unroll=4)


def trig_near_kernel(scal, pos, wv, cs, kvrel, kcols, kvt):
    zh, zl, core = scal[0], scal[1], scal[2]
    n_xy = cs.shape[1]
    n_zl = cs.shape[4] // LANES // 2
    for xy in range(n_xy):
        at = pl.multiple_of((xy * 2 + zh) * LANES, LANES)
        piece = wv[:, pl.ds(at, LANES)]
        piece = jnp.concatenate([piece, jnp.zeros((5, LANES), F32)], 0)
        kvt[xy, :, 0:8] = piece.T
    for dc in range(2):
        at = pl.multiple_of((jnp.bitwise_xor(core, dc) * n_zl + zl) * 16, 16)
        for xy in range(n_xy):
            cols = kvt[xy, pl.ds(at, 16), 0:8]
            rows = slice((dc * n_xy + xy) * 16, (dc * n_xy + xy + 1) * 16)
            hi = cols.astype(BF16)
            lo = (cols - hi.astype(F32)).astype(BF16)
            kvrel[rows, :] = jnp.concatenate([hi, lo], 1)
            kcols[rows, :] = cols * (1.0 / (2.0 * math.pi))
    trig_rows(kcols, pos[...], cs, zh, zl, zh * n_zl)


def trig_far_kernel(scal, ahead, behind, kcols, _, cs):
    zh, zl = scal[0], scal[1]
    n_zl = cs.shape[4] // LANES // 2
    beads = ahead.shape[0] - 16
    rows = jnp.where(zl < n_zl // 2, ahead[beads:, :], behind[beads:, :]).astype(F32)
    pos = rows[0:3] + rows[3:6] + rows[6:9]
    trig_rows(kcols, pos, cs, zh, zl, jnp.bitwise_xor(zh, 1) * n_zl)


def joined(pieces):
    return jnp.concatenate([p[:LANES] for p in pieces], 0)


def early_kernel(cs, *refs):
    pieces, out = refs[:-1], refs[-1]
    rows = cs[...].reshape(-1, cs.shape[4])
    n = rows.shape[1] - LANES
    rows = jnp.concatenate([rows[:, :LANES], rows[:, 2 * LANES : n]], 1)
    part = jnp.dot(rows, joined(pieces), preferred_element_type=F32)
    out[...] = part.reshape(out.shape)


def late_kernel(dc, cs, early, ahead, behind, out):
    rows = cs[dc].reshape(-1, cs.shape[4])
    n = rows.shape[1] - LANES
    rows = jnp.concatenate([rows[:, LANES : 2 * LANES], rows[:, n:]], 1)
    part = jnp.dot(rows, joined([ahead, behind]), preferred_element_type=F32)
    out[...] = (part.reshape(out.shape) + early[dc]).astype(out.dtype)


def filter_kernel(spec_scale, wave_scale, arrived, gain, out, grad_filter):
    n = arrived.shape[0]
    width = gain.shape[1]
    total = arrived[0].astype(F32)
    for i in range(1, n):
        total = total + arrived[i].astype(F32)
    total = total.reshape(2, 16, 2 * width)
    cot = total[:, :, :width] * wave_scale
    spec = total[:, :, width:] * spec_scale
    g = gain[...].astype(F32)
    grad_filter[...] = cot[0] * spec[0] + cot[1] * spec[1]
    filt = (g[None] * spec * (wave_scale / spec_scale)).astype(BF16)
    dspec = (g[None] * cot).astype(BF16)
    both = jnp.concatenate([filt, dspec], 2).reshape(32, 2 * width)
    for i in range(n):
        out[i] = both


def half_gradients(dc, cs, kvrel, stacked, beads_all):
    n_xy, beads = cs.shape[1], cs.shape[4]
    width = beads_all.shape[1] // 2
    both = stacked[...].reshape(n_xy * 32, 2 * width)
    ab = lax.dot_general(both, beads_all, (((1,), (1,)), ((), ())), preferred_element_type=F32)
    ab = ab.reshape(n_xy, 2, 16, beads)
    d = cs[dc, :, 0].astype(F32) * ab[:, 1] - cs[dc, :, 1].astype(F32) * ab[:, 0]
    d = d.reshape(n_xy * 16, beads).astype(BF16)
    kv = kvrel[dc * n_xy * 16 : (dc + 1) * n_xy * 16, :]
    gp = lax.dot_general(kv, d, (((0,), (0,)), ((), ())), preferred_element_type=F32)
    rows = cs[dc].reshape(n_xy * 32, beads)
    gf = lax.dot_general(
        rows, both[:, width:], (((0,), (0,)), ((), ())), preferred_element_type=F32
    )
    return gf, gp[0:8] + gp[8:16]


def grads_near_kernel(cs, kvrel, stacked, *refs):
    pieces, (gf_out, gp_out) = refs[:-2], refs[-2:]
    beads_all = joined(pieces)
    gf, gp = half_gradients(0, cs, kvrel, stacked, beads_all)
    gf_out[...] = gf
    gp_out[...] = gp


def grads_far_kernel(spec_scale, scal, cs, kvrel, stacked, gf_in, gp_in, *refs):
    pieces, out = refs[:-1], refs[-1]
    beads_all = joined(pieces)
    gf, gp = half_gradients(1, cs, kvrel, stacked, beads_all)
    gf = ((gf + gf_in[...]) * spec_scale).astype(BF16)
    gp = (gp + gp_in[...]) * spec_scale
    hi = gp.astype(BF16)
    lo = (gp - hi.astype(F32)).astype(BF16)
    n_z = out.shape[0]
    here = scal[0] * (n_z // 2) + scal[1]
    for shift in range(n_z):
        at = slice(shift * LANES, (shift + 1) * LANES)
        to = lax.rem(here + n_z - shift, n_z)
        out[to, 0:LANES, :] = gf[at]
        out[to, LANES : LANES + 8, :] = jnp.concatenate([hi[:, at], lo[:, at]], 1)


def total_kernel(arrived, gf_out, gp_out):
    total = arrived[0].astype(F32)
    for i in range(1, arrived.shape[0]):
        total = total + arrived[i].astype(F32)
    gf_out[...] = total[:LANES].astype(BF16)
    tail = total[LANES : LANES + 8]
    gp_out[...] = (tail[:, :LANES] + tail[:, LANES:])[0:3]


def call(kernel, out_shape, n_in, scalars=0, scratch=(), aliases=None, space=pltpu.VMEM):
    specs = [pl.BlockSpec(memory_space=pltpu.SMEM)] * scalars
    specs += [pl.BlockSpec(memory_space=space)] * (n_in - scalars)
    outs = jax.tree.map(lambda _: pl.BlockSpec(memory_space=pltpu.VMEM), out_shape)
    return pl.pallas_call(
        kernel,
        out_shape=out_shape,
        in_specs=specs,
        out_specs=outs,
        scratch_shapes=scratch,
        input_output_aliases=aliases or {},
        compiler_params=pltpu.CompilerParams(vmem_limit_bytes=16 << 20),
    )


def shape(dims, dtype):
    return jax.ShapeDtypeStruct(dims, dtype)


def body(positions, features, cotangent, wavevectors, filter_gain):
    n_z = lax.axis_size(Z)
    n_xy = lax.axis_size(XY)
    beads_dev, width = features.shape
    beads_grp = beads_dev * n_z
    n_beads = beads_grp * n_xy * 2
    spec_scale = 1.0 / math.sqrt(n_beads)
    wave_scale = 1.0 / math.sqrt(wavevectors.shape[1])

    def along_z(a, k):
        return lax.ppermute(a, Z, [(i, (i + k) % n_z) for i in range(n_z)])

    def across(a):
        return lax.ppermute(a, "core", [(0, 1), (1, 0)])

    inputs = (cotangent, features, positions, wavevectors)
    inputs = [pltpu.with_memory_space_constraint(a, pltpu.HBM) for a in inputs]
    own, sent, pos_near, wv_near = call(
        load_kernel,
        (
            shape((beads_dev, 2 * width), BF16),
            shape((beads_dev + 16, 2 * width), BF16),
            shape(positions.shape, F32),
            shape(wavevectors.shape, F32),
        ),
        4,
        scratch=[pltpu.SemaphoreType.DMA((4,))],
        space=pltpu.HBM,
    )(*inputs)
    pieces = {0: own, 2: along_z(sent, 2), 6: along_z(sent, -2)}

    scal = jnp.stack([lax.axis_index("zh"), lax.axis_index("zl"), lax.axis_index("core")])
    scal = scal.astype(jnp.int32)
    n_rows = 2 * n_xy * 16
    cs_shape = shape((2, n_xy, 2, 16, beads_grp), BF16)
    trig = call(
        trig_near_kernel,
        (cs_shape, shape((n_rows, 16), BF16), shape((n_rows, 8), F32)),
        3,
        scalars=1,
        scratch=[pltpu.VMEM((n_xy, LANES, 8), F32)],
    )(scal, pos_near, wv_near)
    pieces[2], pieces[6], trig = lax.optimization_barrier((pieces[2], pieces[6], trig))
    pieces[3], pieces[5] = along_z(pieces[2], 1), along_z(pieces[6], -1)
    onward = jnp.where(lax.axis_index("core") == 0, pieces[2], pieces[6])
    n_zl = lax.axis_size("zl")

    def at(z, core):
        return (z // n_zl * 2 + core) * n_zl + z % n_zl

    pairs = [(at(z, c), at((z + 2 - 4 * c) % n_z, c)) for z in range(n_z) for c in range(2)]
    pieces[4] = lax.ppermute(onward, ("zh", "core", "zl"), pairs)
    pieces[1], pieces[7] = along_z(own, 1), along_z(own, -1)
    cs = call(trig_far_kernel, cs_shape, 5, scalars=1, aliases={4: 0})(
        scal, pieces[2], pieces[6], trig[2], trig[0]
    )
    kvrel = trig[1]
    blocks = [pieces[k] for k in range(n_z)]
    near_blocks = [blocks[k] for k in range(n_z) if k not in (1, n_z - 1)]
    late_blocks = [blocks[1], blocks[n_z - 1]]
    early = call(
        early_kernel, shape((2, n_xy, 32, 2 * width), F32), 1 + len(near_blocks)
    )(cs, *near_blocks)

    def spectra(dc, dtype):
        return call(
            lambda *refs: late_kernel(dc, *refs),
            shape((n_xy, 32, 2 * width), dtype),
            2 + len(late_blocks),
        )(cs, early, *late_blocks)

    theirs = across(spectra(1, BF16))
    mine = (spectra(0, F32) + theirs.astype(F32)).astype(BF16)
    arrived = lax.all_to_all(mine, XY, 0, 0, tiled=True)
    copies, grad_filter = call(
        lambda *refs: filter_kernel(spec_scale, wave_scale, *refs),
        (shape((n_xy, 32, 2 * width), BF16), shape((16, width), F32)),
        2,
    )(arrived, filter_gain)
    near = lax.all_to_all(copies, XY, 0, 0, tiled=True)
    far = across(near)
    gf, gp = call(
        grads_near_kernel,
        (shape((beads_grp, width), F32), shape((8, beads_grp), F32)),
        3 + len(blocks),
    )(cs, kvrel, near, *blocks)
    parts = call(
        lambda *refs: grads_far_kernel(spec_scale, *refs),
        shape((n_z, beads_dev + 8, width), BF16),
        6 + len(blocks),
        scalars=1,
    )(scal, cs, kvrel, far, gf, gp, *blocks)
    grad_feat, grad_pos = call(
        total_kernel, (shape((beads_dev, width), BF16), shape((3, beads_dev), F32)), 1
    )(lax.all_to_all(parts, Z, 0, 0, tiled=True))
    return grad_feat, grad_pos, grad_filter


def solution(mesh):
    torus = Mesh(mesh.devices.reshape(4, 4, 2, 2, mesh.shape["waves"]), ALL)
    beads = ("x", "y", "zh", "core")
    return jax.shard_map(
        body,
        mesh=torus,
        in_specs=(P(None, beads), P(ALL, None), P(ALL, None), P(), P(ALL, None)),
        out_specs=(P(ALL, None), P(None, ALL), P(ALL, None)),
        check_vma=False,
    )
```

```python
import math

import jax
import jax.numpy as jnp
from jax import lax
from jax.experimental import pallas as pl
from jax.experimental.pallas import tpu as pltpu
from jax.sharding import Mesh
from jax.sharding import PartitionSpec as P

ALL = ("x", "y", "zh", "core", "zl")
Z = ("zh", "zl")
XY = ("x", "y")
BF16 = jnp.bfloat16
F32 = jnp.float32
LANES = 128

SIN_TURN = (6.28318501, -41.3416557, 81.6010056, -76.5497818, 39.536705)


def sin_turn(h):
    s = h * h
    poly = SIN_TURN[-1]
    for c in SIN_TURN[-2::-1]:
        poly = poly * s + c
    return poly * h


def load_kernel(cot, feat, pos, wv, own, sent, pos_near, wv_near, sems):
    beads, width = cot.shape
    copies = [
        pltpu.make_async_copy(cot, own.at[:, :width], sems.at[0]),
        pltpu.make_async_copy(feat, own.at[:, width:], sems.at[1]),
        pltpu.make_async_copy(pos, pos_near, sems.at[2]),
        pltpu.make_async_copy(wv, wv_near, sems.at[3]),
    ]
    for c in copies:
        c.start()
    for c in copies:
        c.wait()
    sent[:beads, :] = own[...]
    left = pos_near[...]
    parts = []
    for _ in range(3):
        part = left.astype(BF16).astype(F32)
        parts.append(part)
        left = left - part
    parts.append(jnp.zeros((7, left.shape[1]), F32))
    sent[beads:, :] = jnp.concatenate(parts, 0).astype(BF16)


def trig_rows(kcols, pos, cs, zh, zl, first):
    n_xy = cs.shape[1]
    n_z = cs.shape[4] // LANES
    n_zl = n_z // 2
    columns = [
        pl.multiple_of(lax.rem(zh * n_zl + zl + n_z - first - i, n_z) * LANES, LANES)
        for i in range(n_zl)
    ]

    def step(i, carry):
        dc, xy = i // n_xy, lax.rem(i, n_xy)
        cols = kcols[pl.ds(pl.multiple_of(i * 16, 16), 16), :]
        t = cols[:, 0:1] * pos[0:1] + cols[:, 1:2] * pos[1:2] + cols[:, 2:3] * pos[2:3]
        f = t - jnp.round(t)
        cosine = sin_turn(0.25 - jnp.abs(f)).astype(BF16)
        sine = sin_turn(jnp.maximum(jnp.minimum(f, 0.5 - f), -0.5 - f)).astype(BF16)
        for j, column in enumerate(columns):
            part = slice(j * LANES, (j + 1) * LANES)
            cs[dc, xy, 0, :, pl.ds(column, LANES)] = cosine[:, part]
            cs[dc, xy, 1, :, pl.ds(column, LANES)] = sine[:, part]
        return carry

    lax.fori_loop(0, 2 * n_xy, step, 0, unroll=4)


def trig_near_kernel(scal, pos, wv, cs, kvrel, kcols, kvt):
    zh, zl, core = scal[0], scal[1], scal[2]
    n_xy = cs.shape[1]
    n_zl = cs.shape[4] // LANES // 2
    for xy in range(n_xy):
        at = pl.multiple_of((xy * 2 + zh) * LANES, LANES)
        piece = wv[:, pl.ds(at, LANES)]
        piece = jnp.concatenate([piece, jnp.zeros((5, LANES), F32)], 0)
        kvt[xy, :, 0:8] = piece.T
    for dc in range(2):
        at = pl.multiple_of((jnp.bitwise_xor(core, dc) * n_zl + zl) * 16, 16)
        for xy in range(n_xy):
            cols = kvt[xy, pl.ds(at, 16), 0:8]
            rows = slice((dc * n_xy + xy) * 16, (dc * n_xy + xy + 1) * 16)
            hi = cols.astype(BF16)
            lo = (cols - hi.astype(F32)).astype(BF16)
            kvrel[rows, :] = jnp.concatenate([hi, lo], 1)
            kcols[rows, :] = cols * (1.0 / (2.0 * math.pi))
    trig_rows(kcols, pos[...], cs, zh, zl, zh * n_zl)


def trig_far_kernel(scal, ahead, behind, kcols, _, cs):
    zh, zl = scal[0], scal[1]
    n_zl = cs.shape[4] // LANES // 2
    beads = ahead.shape[0] - 16
    rows = jnp.where(zl < n_zl // 2, ahead[beads:, :], behind[beads:, :]).astype(F32)
    pos = rows[0:3] + rows[3:6] + rows[6:9]
    trig_rows(kcols, pos, cs, zh, zl, jnp.bitwise_xor(zh, 1) * n_zl)


def joined(pieces):
    return jnp.concatenate([p[:LANES] for p in pieces], 0)


def early_kernel(cs, *refs):
    pieces, out = refs[:-1], refs[-1]
    rows = cs[...].reshape(-1, cs.shape[4])
    n = 3 * LANES
    near = jnp.dot(rows[:, :n], joined(pieces[:3]), preferred_element_type=F32)
    m = rows.shape[1] - 2 * LANES
    near += jnp.dot(rows[:, m:], joined(pieces[3:]), preferred_element_type=F32)
    out[...] = near.reshape(out.shape)


def late_kernel(dc, cs, early, *refs):
    pieces, out = refs[:-1], refs[-1]
    rows = cs[dc].reshape(-1, cs.shape[4])
    m = rows.shape[1] - 2 * LANES
    part = jnp.dot(rows[:, 3 * LANES : m], joined(pieces), preferred_element_type=F32)
    out[...] = (part.reshape(out.shape) + early[dc]).astype(out.dtype)


def filter_kernel(spec_scale, wave_scale, arrived, gain, out, grad_filter):
    n = arrived.shape[0]
    width = gain.shape[1]
    total = arrived[0].astype(F32)
    for i in range(1, n):
        total = total + arrived[i].astype(F32)
    total = total.reshape(2, 16, 2 * width)
    cot = total[:, :, :width] * wave_scale
    spec = total[:, :, width:] * spec_scale
    g = gain[...].astype(F32)
    grad_filter[...] = cot[0] * spec[0] + cot[1] * spec[1]
    filt = (g[None] * spec * (wave_scale / spec_scale)).astype(BF16)
    dspec = (g[None] * cot).astype(BF16)
    both = jnp.concatenate([filt, dspec], 2).reshape(32, 2 * width)
    for i in range(n):
        out[i] = both


def half_gradients(dc, cs, kvrel, stacked, beads_all):
    n_xy, beads = cs.shape[1], cs.shape[4]
    width = beads_all.shape[1] // 2
    both = stacked[...].reshape(n_xy * 32, 2 * width)
    ab = lax.dot_general(both, beads_all, (((1,), (1,)), ((), ())), preferred_element_type=F32)
    ab = ab.reshape(n_xy, 2, 16, beads)
    d = cs[dc, :, 0].astype(F32) * ab[:, 1] - cs[dc, :, 1].astype(F32) * ab[:, 0]
    d = d.reshape(n_xy * 16, beads).astype(BF16)
    kv = kvrel[dc * n_xy * 16 : (dc + 1) * n_xy * 16, :]
    gp = lax.dot_general(kv, d, (((0,), (0,)), ((), ())), preferred_element_type=F32)
    rows = cs[dc].reshape(n_xy * 32, beads)
    gf = lax.dot_general(
        both[:, width:], rows, (((0,), (0,)), ((), ())), preferred_element_type=F32
    )
    return gf, gp[0:8] + gp[8:16]


def grads_near_kernel(cs, kvrel, stacked, *refs):
    pieces, (gf_out, gp_out) = refs[:-2], refs[-2:]
    beads_all = joined(pieces)
    gf, gp = half_gradients(0, cs, kvrel, stacked, beads_all)
    gf_out[...] = gf
    gp_out[...] = gp


def grads_far_kernel(spec_scale, scal, cs, kvrel, stacked, gf_in, gp_in, *refs):
    pieces, out = refs[:-1], refs[-1]
    beads_all = joined(pieces)
    gf, gp = half_gradients(1, cs, kvrel, stacked, beads_all)
    gf = ((gf + gf_in[...]) * spec_scale).astype(BF16)
    gp = (gp + gp_in[...]) * spec_scale
    hi = gp.astype(BF16).astype(F32)
    tail = jnp.concatenate([hi[0:3], (gp - hi)[0:3], jnp.zeros_like(gp[0:2])], 0).astype(BF16)
    n_z = out.shape[0]
    width = gf.shape[0]
    here = scal[0] * (n_z // 2) + scal[1]
    for shift in range(n_z):
        at = slice(shift * LANES, (shift + 1) * LANES)
        to = lax.rem(here + n_z - shift, n_z)
        out[to, 0:width, :] = gf[:, at]
        out[to, width : width + 8, :] = tail[:, at]


def total_kernel(arrived, gf_out, gp_out):
    total = arrived[0].astype(F32)
    for i in range(1, arrived.shape[0]):
        total = total + arrived[i].astype(F32)
    width = gf_out.shape[1]
    gf_out[...] = total[:width].T.astype(BF16)
    gp_out[...] = total[width : width + 3] + total[width + 3 : width + 6]


def call(kernel, out_shape, n_in, scalars=0, scratch=(), aliases=None, space=pltpu.VMEM):
    specs = [pl.BlockSpec(memory_space=pltpu.SMEM)] * scalars
    specs += [pl.BlockSpec(memory_space=space)] * (n_in - scalars)
    outs = jax.tree.map(lambda _: pl.BlockSpec(memory_space=pltpu.VMEM), out_shape)
    return pl.pallas_call(
        kernel,
        out_shape=out_shape,
        in_specs=specs,
        out_specs=outs,
        scratch_shapes=scratch,
        input_output_aliases=aliases or {},
        compiler_params=pltpu.CompilerParams(vmem_limit_bytes=16 << 20),
    )


def shape(dims, dtype):
    return jax.ShapeDtypeStruct(dims, dtype)


def body(positions, features, cotangent, wavevectors, filter_gain):
    n_z = lax.axis_size(Z)
    n_xy = lax.axis_size(XY)
    beads_dev, width = features.shape
    beads_grp = beads_dev * n_z
    n_beads = beads_grp * n_xy * 2
    spec_scale = 1.0 / math.sqrt(n_beads)
    wave_scale = 1.0 / math.sqrt(wavevectors.shape[1])

    def along_z(a, k):
        return lax.ppermute(a, Z, [(i, (i + k) % n_z) for i in range(n_z)])

    def across(a):
        return lax.ppermute(a, "core", [(0, 1), (1, 0)])

    inputs = (cotangent, features, positions, wavevectors)
    inputs = [pltpu.with_memory_space_constraint(a, pltpu.HBM) for a in inputs]
    own, sent, pos_near, wv_near = call(
        load_kernel,
        (
            shape((beads_dev, 2 * width), BF16),
            shape((beads_dev + 16, 2 * width), BF16),
            shape(positions.shape, F32),
            shape(wavevectors.shape, F32),
        ),
        4,
        scratch=[pltpu.SemaphoreType.DMA((4,))],
        space=pltpu.HBM,
    )(*inputs)
    pieces = {0: own, 2: along_z(sent, 2), 6: along_z(sent, -2)}

    scal = jnp.stack([lax.axis_index("zh"), lax.axis_index("zl"), lax.axis_index("core")])
    scal = scal.astype(jnp.int32)
    n_rows = 2 * n_xy * 16
    cs_shape = shape((2, n_xy, 2, 16, beads_grp), BF16)
    trig = call(
        trig_near_kernel,
        (cs_shape, shape((n_rows, 16), BF16), shape((n_rows, 8), F32)),
        3,
        scalars=1,
        scratch=[pltpu.VMEM((n_xy, LANES, 8), F32)],
    )(scal, pos_near, wv_near)
    own, trig = lax.optimization_barrier((own, trig))
    pieces[1], pieces[7] = along_z(own, 1), along_z(own, -1)
    pieces[2], pieces[6], trig = lax.optimization_barrier((pieces[2], pieces[6], trig))
    ahead, behind = pieces[2][:beads_dev], pieces[6][:beads_dev]
    half = beads_dev // 2
    pieces[3], pieces[5] = along_z(ahead, 1), along_z(behind, -1)
    late_blocks = [pieces[3], along_z(ahead[:half], 2), along_z(behind[half:], -2), pieces[5]]
    blocks = [pieces[0], pieces[1], pieces[2], *late_blocks, pieces[6], pieces[7]]
    cs = call(trig_far_kernel, cs_shape, 5, scalars=1, aliases={4: 0})(
        scal, pieces[2], pieces[6], trig[2], trig[0]
    )
    kvrel = trig[1]

    near_blocks = blocks[:3] + blocks[-2:]
    early = call(
        early_kernel, shape((2, n_xy, 32, 2 * width), F32), 1 + len(near_blocks)
    )(cs, *near_blocks)

    def spectra(dc, dtype):
        return call(
            lambda *refs: late_kernel(dc, *refs),
            shape((n_xy, 32, 2 * width), dtype),
            2 + len(late_blocks),
        )(cs, early, *late_blocks)

    theirs = across(spectra(1, BF16))
    mine = (spectra(0, F32) + theirs.astype(F32)).astype(BF16)
    arrived = lax.all_to_all(mine, XY, 0, 0, tiled=True)
    copies, grad_filter = call(
        lambda *refs: filter_kernel(spec_scale, wave_scale, *refs),
        (shape((n_xy, 32, 2 * width), BF16), shape((16, width), F32)),
        2,
    )(arrived, filter_gain)
    near = lax.all_to_all(copies, XY, 0, 0, tiled=True)
    far = across(near)
    gf, gp = call(
        grads_near_kernel,
        (shape((width, beads_grp), F32), shape((8, beads_grp), F32)),
        3 + len(blocks),
    )(cs, kvrel, near, *blocks)
    parts = call(
        lambda *refs: grads_far_kernel(spec_scale, *refs),
        shape((n_z, width + 8, beads_dev), BF16),
        6 + len(blocks),
        scalars=1,
    )(scal, cs, kvrel, far, gf, gp, *blocks)
    grad_feat, grad_pos = call(
        total_kernel, (shape((beads_dev, width), BF16), shape((3, beads_dev), F32)), 1
    )(lax.all_to_all(parts, Z, 0, 0, tiled=True))
    return grad_feat, grad_pos, grad_filter


def solution(mesh):
    torus = Mesh(mesh.devices.reshape(4, 4, 2, 2, mesh.shape["waves"]), ALL)
    beads = ("x", "y", "zh", "core")
    return jax.shard_map(
        body,
        mesh=torus,
        in_specs=(P(None, beads), P(ALL, None), P(ALL, None), P(), P(ALL, None)),
        out_specs=(P(ALL, None), P(None, ALL), P(ALL, None)),
        check_vma=False,
    )
```

```python
import math

import jax
import jax.numpy as jnp
from jax import lax
from jax.experimental import pallas as pl
from jax.experimental.pallas import tpu as pltpu
from jax.sharding import Mesh
from jax.sharding import PartitionSpec as P


ALL = ("x", "y", "zh", "core", "zl")
Z = ("zh", "zl")
XY = ("x", "y")
BF16 = jnp.bfloat16
F32 = jnp.float32
LANES = 128

SIN_TURN = (6.28318501, -41.3416557, 81.6010056, -76.5497818, 39.536705)


def sin_turn(h):
    s = h * h
    poly = SIN_TURN[-1]
    for c in SIN_TURN[-2::-1]:
        poly = poly * s + c
    return poly * h


def load_kernel(cot, feat, pos, wv, own, sent, pos_near, wv_near, sems):
    beads, width = cot.shape
    copies = [
        pltpu.make_async_copy(cot, own.at[:, :width], sems.at[0]),
        pltpu.make_async_copy(feat, own.at[:, width:], sems.at[1]),
        pltpu.make_async_copy(pos, pos_near, sems.at[2]),
        pltpu.make_async_copy(wv, wv_near, sems.at[3]),
    ]
    for c in copies:
        c.start()
    for c in copies:
        c.wait()
    sent[:beads, :] = own[...]
    left = pos_near[...]
    parts = []
    for _ in range(3):
        part = left.astype(BF16).astype(F32)
        parts.append(part)
        left = left - part
    parts.append(jnp.zeros((7, left.shape[1]), F32))
    sent[beads:, :] = jnp.concatenate(parts, 0).astype(BF16)


def trig_rows(kcols, pos, cs, zh, zl, first):
    n_xy = cs.shape[1]
    n_z = cs.shape[4] // LANES
    n_zl = n_z // 2
    columns = [
        pl.multiple_of(lax.rem(zh * n_zl + zl + n_z - first - i, n_z) * LANES, LANES)
        for i in range(n_zl)
    ]

    def step(i, carry):
        dc, xy = i // n_xy, lax.rem(i, n_xy)
        cols = kcols[pl.ds(pl.multiple_of(i * 16, 16), 16), :]
        t = cols[:, 0:1] * pos[0:1] + cols[:, 1:2] * pos[1:2] + cols[:, 2:3] * pos[2:3]
        f = t - jnp.round(t)
        cosine = sin_turn(0.25 - jnp.abs(f)).astype(BF16)
        sine = sin_turn(jnp.maximum(jnp.minimum(f, 0.5 - f), -0.5 - f)).astype(BF16)
        for j, column in enumerate(columns):
            part = slice(j * LANES, (j + 1) * LANES)
            cs[dc, xy, 0, :, pl.ds(column, LANES)] = cosine[:, part]
            cs[dc, xy, 1, :, pl.ds(column, LANES)] = sine[:, part]
        return carry

    lax.fori_loop(0, 2 * n_xy, step, 0, unroll=4)


def trig_near_kernel(scal, pos, wv, cs, kvrel, kcols, kvt):
    zh, zl, core = scal[0], scal[1], scal[2]
    n_xy = cs.shape[1]
    n_zl = cs.shape[4] // LANES // 2
    for xy in range(n_xy):
        at = pl.multiple_of((xy * 2 + zh) * LANES, LANES)
        piece = wv[:, pl.ds(at, LANES)]
        piece = jnp.concatenate([piece, jnp.zeros((5, LANES), F32)], 0)
        kvt[xy, :, 0:8] = piece.T
    for dc in range(2):
        at = pl.multiple_of((jnp.bitwise_xor(core, dc) * n_zl + zl) * 16, 16)
        for xy in range(n_xy):
            cols = kvt[xy, pl.ds(at, 16), 0:8]
            rows = slice((dc * n_xy + xy) * 16, (dc * n_xy + xy + 1) * 16)
            hi = cols.astype(BF16)
            lo = (cols - hi.astype(F32)).astype(BF16)
            kvrel[rows, :] = jnp.concatenate([hi, lo], 1)
            kcols[rows, :] = cols * (1.0 / (2.0 * math.pi))
    trig_rows(kcols, pos[...], cs, zh, zl, zh * n_zl)


def trig_far_kernel(scal, ahead, behind, kcols, _, cs):
    zh, zl = scal[0], scal[1]
    n_zl = cs.shape[4] // LANES // 2
    beads = ahead.shape[0] - 16
    rows = jnp.where(zl < n_zl // 2, ahead[beads:, :], behind[beads:, :]).astype(F32)
    pos = rows[0:3] + rows[3:6] + rows[6:9]
    trig_rows(kcols, pos, cs, zh, zl, jnp.bitwise_xor(zh, 1) * n_zl)


def joined(pieces):
    return jnp.concatenate([p[:LANES] for p in pieces], 0)


def early_kernel(cs, *refs):
    pieces, out = refs[:-1], refs[-1]
    rows = cs[...].reshape(-1, cs.shape[4])
    n = 3 * LANES
    near = jnp.dot(rows[:, :n], joined(pieces[:3]), preferred_element_type=F32)
    m = rows.shape[1] - 2 * LANES
    near += jnp.dot(rows[:, m:], joined(pieces[3:]), preferred_element_type=F32)
    out[...] = near.reshape(out.shape)


def late_kernel(dc, cs, early, *refs):
    pieces, out = refs[:-1], refs[-1]
    rows = cs[dc].reshape(-1, cs.shape[4])
    m = rows.shape[1] - 2 * LANES
    part = jnp.dot(rows[:, 3 * LANES : m], joined(pieces), preferred_element_type=F32)
    out[...] = (part.reshape(out.shape) + early[dc]).astype(out.dtype)


def filter_kernel(spec_scale, wave_scale, arrived, gain, out, grad_filter):
    n = arrived.shape[0]
    width = gain.shape[1]
    total = arrived[0].astype(F32)
    for i in range(1, n):
        total = total + arrived[i].astype(F32)
    total = total.reshape(2, 16, 2 * width)
    cot = total[:, :, :width] * wave_scale
    spec = total[:, :, width:] * spec_scale
    g = gain[...].astype(F32)
    grad_filter[...] = cot[0] * spec[0] + cot[1] * spec[1]
    filt = (g[None] * spec * (wave_scale / spec_scale)).astype(BF16)
    dspec = (g[None] * cot).astype(BF16)
    both = jnp.concatenate([filt, dspec], 2).reshape(32, 2 * width)
    for i in range(n):
        out[i] = both


def half_gradients(dc, cs, kvrel, stacked, beads_all):
    n_xy, beads = cs.shape[1], cs.shape[4]
    width = beads_all.shape[1] // 2
    both = stacked[...].reshape(n_xy * 32, 2 * width)
    ab = lax.dot_general(both, beads_all, (((1,), (1,)), ((), ())), preferred_element_type=F32)
    ab = ab.reshape(n_xy, 2, 16, beads)
    d = cs[dc, :, 0].astype(F32) * ab[:, 1] - cs[dc, :, 1].astype(F32) * ab[:, 0]
    d = d.reshape(n_xy * 16, beads).astype(BF16)
    kv = kvrel[dc * n_xy * 16 : (dc + 1) * n_xy * 16, :]
    gp = lax.dot_general(kv, d, (((0,), (0,)), ((), ())), preferred_element_type=F32)
    rows = cs[dc].reshape(n_xy * 32, beads)
    gf = lax.dot_general(
        both[:, width:], rows, (((0,), (0,)), ((), ())), preferred_element_type=F32
    )
    return gf, gp[0:8] + gp[8:16]


def grads_near_kernel(cs, kvrel, stacked, *refs):
    pieces, (gf_out, gp_out) = refs[:-2], refs[-2:]
    beads_all = joined(pieces)
    gf, gp = half_gradients(0, cs, kvrel, stacked, beads_all)
    gf_out[...] = gf
    gp_out[...] = gp


def grads_far_kernel(spec_scale, scal, cs, kvrel, stacked, gf_in, gp_in, *refs):
    pieces, out = refs[:-1], refs[-1]
    beads_all = joined(pieces)
    gf, gp = half_gradients(1, cs, kvrel, stacked, beads_all)
    gf = ((gf + gf_in[...]) * spec_scale).astype(BF16)
    gp = (gp + gp_in[...]) * spec_scale
    hi = gp.astype(BF16).astype(F32)
    tail = jnp.concatenate([hi[0:3], (gp - hi)[0:3], jnp.zeros_like(gp[0:2])], 0).astype(BF16)
    n_z = out.shape[0]
    width = gf.shape[0]
    here = scal[0] * (n_z // 2) + scal[1]
    for shift in range(n_z):
        at = slice(shift * LANES, (shift + 1) * LANES)
        to = lax.rem(here + n_z - shift, n_z)
        out[to, 0:width, :] = gf[:, at]
        out[to, width : width + 8, :] = tail[:, at]


def total_kernel(arrived, gf_out, gp_out):
    total = arrived[0].astype(F32)
    for i in range(1, arrived.shape[0]):
        total = total + arrived[i].astype(F32)
    width = gf_out.shape[1]
    gf_out[...] = total[:width].T.astype(BF16)
    gp_out[...] = total[width : width + 3] + total[width + 3 : width + 6]


def call(kernel, out_shape, n_in, scalars=0, scratch=(), aliases=None, space=pltpu.VMEM):
    specs = [pl.BlockSpec(memory_space=pltpu.SMEM)] * scalars
    specs += [pl.BlockSpec(memory_space=space)] * (n_in - scalars)
    outs = jax.tree.map(lambda _: pl.BlockSpec(memory_space=pltpu.VMEM), out_shape)
    return pl.pallas_call(
        kernel,
        out_shape=out_shape,
        in_specs=specs,
        out_specs=outs,
        scratch_shapes=scratch,
        input_output_aliases=aliases or {},
        compiler_params=pltpu.CompilerParams(vmem_limit_bytes=16 << 20),
    )


def shape(dims, dtype):
    return jax.ShapeDtypeStruct(dims, dtype)


def body(positions, features, cotangent, wavevectors, filter_gain):
    n_z = lax.axis_size(Z)
    n_xy = lax.axis_size(XY)
    beads_dev, width = features.shape
    beads_grp = beads_dev * n_z
    n_beads = beads_grp * n_xy * 2
    spec_scale = 1.0 / math.sqrt(n_beads)
    wave_scale = 1.0 / math.sqrt(wavevectors.shape[1])

    def along_z(a, k):
        return lax.ppermute(a, Z, [(i, (i + k) % n_z) for i in range(n_z)])

    def across(a):
        return lax.ppermute(a, "core", [(0, 1), (1, 0)])

    inputs = (cotangent, features, positions, wavevectors)
    inputs = [pltpu.with_memory_space_constraint(a, pltpu.HBM) for a in inputs]
    own, sent, pos_near, wv_near = call(
        load_kernel,
        (
            shape((beads_dev, 2 * width), BF16),
            shape((beads_dev + 16, 2 * width), BF16),
            shape(positions.shape, F32),
            shape(wavevectors.shape, F32),
        ),
        4,
        scratch=[pltpu.SemaphoreType.DMA((4,))],
        space=pltpu.HBM,
    )(*inputs)
    pieces = {0: own, 2: along_z(sent, 2), 6: along_z(sent, -2)}

    scal = jnp.stack([lax.axis_index("zh"), lax.axis_index("zl"), lax.axis_index("core")])
    scal = scal.astype(jnp.int32)
    n_rows = 2 * n_xy * 16
    cs_shape = shape((2, n_xy, 2, 16, beads_grp), BF16)
    trig = call(
        trig_near_kernel,
        (cs_shape, shape((n_rows, 16), BF16), shape((n_rows, 8), F32)),
        3,
        scalars=1,
        scratch=[pltpu.VMEM((n_xy, LANES, 8), F32)],
    )(scal, pos_near, wv_near)
    own, trig = lax.optimization_barrier((own, trig))
    pieces[1], pieces[7] = along_z(own, 1), along_z(own, -1)
    pieces[2], pieces[6], trig = lax.optimization_barrier((pieces[2], pieces[6], trig))
    ahead, behind = pieces[2][:beads_dev], pieces[6][:beads_dev]
    onward = jnp.where(lax.axis_index("core") == 0, ahead, behind)
    n_zl = lax.axis_size("zl")

    def at(z, core):
        return (z // n_zl * 2 + core) * n_zl + z % n_zl

    pairs = [(at(z, c), at((z + 2 - 4 * c) % n_z, c)) for z in range(n_z) for c in range(2)]
    pieces[4] = lax.ppermute(onward, ("zh", "core", "zl"), pairs)
    pieces[3], pieces[5] = along_z(ahead, 1), along_z(behind, -1)
    late_blocks = [pieces[3], pieces[4], pieces[5]]
    blocks = [pieces[k] for k in range(n_z)]
    cs = call(trig_far_kernel, cs_shape, 5, scalars=1, aliases={4: 0})(
        scal, pieces[2], pieces[6], trig[2], trig[0]
    )
    kvrel = trig[1]

    near_blocks = blocks[:3] + blocks[-2:]
    early = call(
        early_kernel, shape((2, n_xy, 32, 2 * width), F32), 1 + len(near_blocks)
    )(cs, *near_blocks)

    def spectra(dc, dtype):
        return call(
            lambda *refs: late_kernel(dc, *refs),
            shape((n_xy, 32, 2 * width), dtype),
            2 + len(late_blocks),
        )(cs, early, *late_blocks)

    theirs = across(spectra(1, BF16))
    mine = (spectra(0, F32) + theirs.astype(F32)).astype(BF16)
    arrived = lax.all_to_all(mine, XY, 0, 0, tiled=True)
    copies, grad_filter = call(
        lambda *refs: filter_kernel(spec_scale, wave_scale, *refs),
        (shape((n_xy, 32, 2 * width), BF16), shape((16, width), F32)),
        2,
    )(arrived, filter_gain)
    near = lax.all_to_all(copies, XY, 0, 0, tiled=True)
    far = across(near)
    gf, gp = call(
        grads_near_kernel,
        (shape((width, beads_grp), F32), shape((8, beads_grp), F32)),
        3 + len(blocks),
    )(cs, kvrel, near, *blocks)
    parts = call(
        lambda *refs: grads_far_kernel(spec_scale, *refs),
        shape((n_z, width + 8, beads_dev), BF16),
        6 + len(blocks),
        scalars=1,
    )(scal, cs, kvrel, far, gf, gp, *blocks)
    grad_feat, grad_pos = call(
        total_kernel, (shape((beads_dev, width), BF16), shape((3, beads_dev), F32)), 1
    )(lax.all_to_all(parts, Z, 0, 0, tiled=True))
    return grad_feat, grad_pos, grad_filter


def solution(mesh):
    torus = Mesh(mesh.devices.reshape(4, 4, 2, 2, mesh.shape["waves"]), ALL)
    beads = ("x", "y", "zh", "core")
    return jax.shard_map(
        body,
        mesh=torus,
        in_specs=(P(None, beads), P(ALL, None), P(ALL, None), P(), P(ALL, None)),
        out_specs=(P(ALL, None), P(None, ALL), P(ALL, None)),
        check_vma=False,
    )
```

```python
import math

import jax
import jax.numpy as jnp
from jax import lax
from jax.experimental import pallas as pl
from jax.experimental.pallas import tpu as pltpu
from jax.sharding import Mesh
from jax.sharding import PartitionSpec as P


ALL = ("x", "y", "zh", "core", "zl")
Z = ("zh", "zl")
XY = ("x", "y")
BF16 = jnp.bfloat16
F32 = jnp.float32
LANES = 128

SIN_TURN = (6.28318501, -41.3416557, 81.6010056, -76.5497818, 39.536705)


def sin_turn(h):
    s = h * h
    poly = SIN_TURN[-1]
    for c in SIN_TURN[-2::-1]:
        poly = poly * s + c
    return poly * h


def load_kernel(cot, feat, pos, wv, own, sent, pos_near, wv_near, sems):
    beads, width = cot.shape
    copies = [
        pltpu.make_async_copy(cot, own.at[:, :width], sems.at[0]),
        pltpu.make_async_copy(feat, own.at[:, width:], sems.at[1]),
        pltpu.make_async_copy(pos, pos_near, sems.at[2]),
        pltpu.make_async_copy(wv, wv_near, sems.at[3]),
    ]
    for c in copies:
        c.start()
    for c in copies:
        c.wait()
    sent[:beads, :] = own[...]
    left = pos_near[...]
    parts = []
    for _ in range(3):
        part = left.astype(BF16).astype(F32)
        parts.append(part)
        left = left - part
    parts.append(jnp.zeros((7, left.shape[1]), F32))
    sent[beads:, :] = jnp.concatenate(parts, 0).astype(BF16)


def trig_rows(kcols, pos, cs, zh, zl, first):
    n_xy = cs.shape[1]
    n_z = cs.shape[4] // LANES
    n_zl = n_z // 2
    columns = [
        pl.multiple_of(lax.rem(zh * n_zl + zl + n_z - first - i, n_z) * LANES, LANES)
        for i in range(n_zl)
    ]

    def step(i, carry):
        dc, xy = i // n_xy, lax.rem(i, n_xy)
        cols = kcols[pl.ds(pl.multiple_of(i * 16, 16), 16), :]
        t = cols[:, 0:1] * pos[0:1] + cols[:, 1:2] * pos[1:2] + cols[:, 2:3] * pos[2:3]
        f = t - jnp.round(t)
        cosine = sin_turn(0.25 - jnp.abs(f)).astype(BF16)
        sine = sin_turn(jnp.maximum(jnp.minimum(f, 0.5 - f), -0.5 - f)).astype(BF16)
        for j, column in enumerate(columns):
            part = slice(j * LANES, (j + 1) * LANES)
            cs[dc, xy, 0, :, pl.ds(column, LANES)] = cosine[:, part]
            cs[dc, xy, 1, :, pl.ds(column, LANES)] = sine[:, part]
        return carry

    lax.fori_loop(0, 2 * n_xy, step, 0, unroll=4)


def trig_near_kernel(scal, pos, wv, cs, kvrel, kcols, kvt):
    zh, zl, core = scal[0], scal[1], scal[2]
    n_xy = cs.shape[1]
    n_zl = cs.shape[4] // LANES // 2
    for xy in range(n_xy):
        at = pl.multiple_of((xy * 2 + zh) * LANES, LANES)
        piece = wv[:, pl.ds(at, LANES)]
        piece = jnp.concatenate([piece, jnp.zeros((5, LANES), F32)], 0)
        kvt[xy, :, 0:8] = piece.T
    for dc in range(2):
        at = pl.multiple_of((jnp.bitwise_xor(core, dc) * n_zl + zl) * 16, 16)
        for xy in range(n_xy):
            cols = kvt[xy, pl.ds(at, 16), 0:8]
            rows = slice((dc * n_xy + xy) * 16, (dc * n_xy + xy + 1) * 16)
            hi = cols.astype(BF16)
            lo = (cols - hi.astype(F32)).astype(BF16)
            kvrel[rows, :] = jnp.concatenate([hi, lo], 1)
            kcols[rows, :] = cols * (1.0 / (2.0 * math.pi))
    trig_rows(kcols, pos[...], cs, zh, zl, zh * n_zl)


def trig_far_kernel(scal, ahead, behind, kcols, _, cs):
    zh, zl = scal[0], scal[1]
    n_zl = cs.shape[4] // LANES // 2
    beads = ahead.shape[0] - 16
    rows = jnp.where(zl < n_zl // 2, ahead[beads:, :], behind[beads:, :]).astype(F32)
    pos = rows[0:3] + rows[3:6] + rows[6:9]
    trig_rows(kcols, pos, cs, zh, zl, jnp.bitwise_xor(zh, 1) * n_zl)


def joined(pieces):
    return jnp.concatenate([p[:LANES] for p in pieces], 0)


def early_kernel(cs, *refs):
    pieces, out = refs[:-1], refs[-1]
    rows = cs[...].reshape(-1, cs.shape[4])
    n, m = 3 * LANES, rows.shape[1] - 3 * LANES
    parts = [rows[:, :n], rows[:, n + LANES : m], rows[:, m + LANES :]]
    part = jnp.dot(jnp.concatenate(parts, 1), joined(pieces), preferred_element_type=F32)
    out[...] = part.reshape(out.shape)


def late_kernel(dc, cs, early, ahead, behind, out):
    rows = cs[dc].reshape(-1, cs.shape[4])
    n, m = 3 * LANES, rows.shape[1] - 3 * LANES
    rows = jnp.concatenate([rows[:, n : n + LANES], rows[:, m : m + LANES]], 1)
    part = jnp.dot(rows, joined([ahead, behind]), preferred_element_type=F32)
    out[...] = (part.reshape(out.shape) + early[dc]).astype(out.dtype)


def filter_kernel(spec_scale, wave_scale, arrived, gain, out, grad_filter):
    n = arrived.shape[0]
    width = gain.shape[1]
    total = arrived[0].astype(F32)
    for i in range(1, n):
        total = total + arrived[i].astype(F32)
    total = total.reshape(2, 16, 2 * width)
    cot = total[:, :, :width] * wave_scale
    spec = total[:, :, width:] * spec_scale
    g = gain[...].astype(F32)
    grad_filter[...] = cot[0] * spec[0] + cot[1] * spec[1]
    filt = (g[None] * spec * (wave_scale / spec_scale)).astype(BF16)
    dspec = (g[None] * cot).astype(BF16)
    both = jnp.concatenate([filt, dspec], 2).reshape(32, 2 * width)
    for i in range(n):
        out[i] = both


def half_gradients(dc, cs, kvrel, stacked, beads_all):
    n_xy, beads = cs.shape[1], cs.shape[4]
    width = beads_all.shape[1] // 2
    both = stacked[...].reshape(n_xy * 32, 2 * width)
    ab = lax.dot_general(both, beads_all, (((1,), (1,)), ((), ())), preferred_element_type=F32)
    ab = ab.reshape(n_xy, 2, 16, beads)
    d = cs[dc, :, 0].astype(F32) * ab[:, 1] - cs[dc, :, 1].astype(F32) * ab[:, 0]
    d = d.reshape(n_xy * 16, beads).astype(BF16)
    kv = kvrel[dc * n_xy * 16 : (dc + 1) * n_xy * 16, :]
    gp = lax.dot_general(kv, d, (((0,), (0,)), ((), ())), preferred_element_type=F32)
    rows = cs[dc].reshape(n_xy * 32, beads)
    gf = lax.dot_general(
        both[:, width:], rows, (((0,), (0,)), ((), ())), preferred_element_type=F32
    )
    return gf, gp[0:8] + gp[8:16]


def grads_near_kernel(cs, kvrel, stacked, *refs):
    pieces, (gf_out, gp_out) = refs[:-2], refs[-2:]
    beads_all = joined(pieces)
    gf, gp = half_gradients(0, cs, kvrel, stacked, beads_all)
    gf_out[...] = gf
    gp_out[...] = gp


def grads_far_kernel(scal, cs, kvrel, stacked, gf_in, gp_in, *refs):
    pieces, out = refs[:-1], refs[-1]
    beads_all = joined(pieces)
    gf, gp = half_gradients(1, cs, kvrel, stacked, beads_all)
    gf = (gf + gf_in[...]).astype(BF16)
    gp = gp + gp_in[...]
    hi = gp.astype(BF16).astype(F32)
    tail = jnp.concatenate([hi[0:3], (gp - hi)[0:3], jnp.zeros_like(gp[0:2])], 0).astype(BF16)
    n_z = out.shape[0]
    width = gf.shape[0]
    here = scal[0] * (n_z // 2) + scal[1]
    for shift in range(n_z):
        at = slice(shift * LANES, (shift + 1) * LANES)
        to = lax.rem(here + n_z - shift, n_z)
        out[to, 0:width, :] = gf[:, at]
        out[to, width : width + 8, :] = tail[:, at]


def total_kernel(spec_scale, arrived, grad_filter, gf_out, gp_out, filter_out):
    total = arrived[0].astype(F32)
    for i in range(1, arrived.shape[0]):
        total = total + arrived[i].astype(F32)
    total = total * spec_scale
    width = gf_out.shape[1]
    gf_out[...] = total[:width].T.astype(BF16)
    gp_out[...] = total[width : width + 3] + total[width + 3 : width + 6]
    filter_out[...] = grad_filter[...]


def call(kernel, out_shape, n_in, scalars=0, scratch=(), aliases=None, space=pltpu.VMEM):
    specs = [pl.BlockSpec(memory_space=pltpu.SMEM)] * scalars
    specs += [pl.BlockSpec(memory_space=space)] * (n_in - scalars)
    outs = jax.tree.map(lambda _: pl.BlockSpec(memory_space=pltpu.VMEM), out_shape)
    return pl.pallas_call(
        kernel,
        out_shape=out_shape,
        in_specs=specs,
        out_specs=outs,
        scratch_shapes=scratch,
        input_output_aliases=aliases or {},
        compiler_params=pltpu.CompilerParams(vmem_limit_bytes=16 << 20),
    )


def shape(dims, dtype):
    return jax.ShapeDtypeStruct(dims, dtype)


def body(positions, features, cotangent, wavevectors, filter_gain):
    n_z = lax.axis_size(Z)
    n_xy = lax.axis_size(XY)
    beads_dev, width = features.shape
    beads_grp = beads_dev * n_z
    n_beads = beads_grp * n_xy * 2
    spec_scale = 1.0 / math.sqrt(n_beads)
    wave_scale = 1.0 / math.sqrt(wavevectors.shape[1])

    def along_z(a, k):
        return lax.ppermute(a, Z, [(i, (i + k) % n_z) for i in range(n_z)])

    def across(a):
        return lax.ppermute(a, "core", [(0, 1), (1, 0)])

    inputs = (cotangent, features, positions, wavevectors)
    inputs = [pltpu.with_memory_space_constraint(a, pltpu.HBM) for a in inputs]
    own, sent, pos_near, wv_near = call(
        load_kernel,
        (
            shape((beads_dev, 2 * width), BF16),
            shape((beads_dev + 16, 2 * width), BF16),
            shape(positions.shape, F32),
            shape(wavevectors.shape, F32),
        ),
        4,
        scratch=[pltpu.SemaphoreType.DMA((4,))],
        space=pltpu.HBM,
    )(*inputs)
    pieces = {0: own, 2: along_z(sent, 2), 6: along_z(sent, -2)}

    scal = jnp.stack([lax.axis_index("zh"), lax.axis_index("zl"), lax.axis_index("core")])
    scal = scal.astype(jnp.int32)
    n_rows = 2 * n_xy * 16
    cs_shape = shape((2, n_xy, 2, 16, beads_grp), BF16)
    trig = call(
        trig_near_kernel,
        (cs_shape, shape((n_rows, 16), BF16), shape((n_rows, 8), F32)),
        3,
        scalars=1,
        scratch=[pltpu.VMEM((n_xy, LANES, 8), F32)],
    )(scal, pos_near, wv_near)
    own, trig = lax.optimization_barrier((own, trig))
    pieces[1], pieces[7] = along_z(own, 1), along_z(own, -1)
    pieces[2], pieces[6], trig = lax.optimization_barrier((pieces[2], pieces[6], trig))
    ahead, behind = pieces[2][:beads_dev], pieces[6][:beads_dev]
    onward = jnp.where(lax.axis_index("core") == 0, ahead, behind)
    n_zl = lax.axis_size("zl")

    def at(z, core):
        return (z // n_zl * 2 + core) * n_zl + z % n_zl

    pairs = [(at(z, c), at((z + 2 - 4 * c) % n_z, c)) for z in range(n_z) for c in range(2)]
    pieces[4] = lax.ppermute(onward, ("zh", "core", "zl"), pairs)
    pieces[3], pieces[5] = along_z(ahead, 1), along_z(behind, -1)
    late_blocks = [pieces[3], pieces[5]]
    blocks = [pieces[k] for k in range(n_z)]
    cs = call(trig_far_kernel, cs_shape, 5, scalars=1, aliases={4: 0})(
        scal, pieces[2], pieces[6], trig[2], trig[0]
    )
    kvrel = trig[1]

    near_blocks = [blocks[k] for k in range(n_z) if k not in (3, n_z - 3)]
    early = call(
        early_kernel, shape((2, n_xy, 32, 2 * width), F32), 1 + len(near_blocks)
    )(cs, *near_blocks)

    def spectra(dc, dtype):
        return call(
            lambda *refs: late_kernel(dc, *refs),
            shape((n_xy, 32, 2 * width), dtype),
            2 + len(late_blocks),
        )(cs, early, *late_blocks)

    theirs = across(spectra(1, BF16))
    mine = (spectra(0, F32) + theirs.astype(F32)).astype(BF16)
    arrived = lax.all_to_all(mine, XY, 0, 0, tiled=True)
    copies, grad_filter = call(
        lambda *refs: filter_kernel(spec_scale, wave_scale, *refs),
        (shape((n_xy, 32, 2 * width), BF16), shape((16, width), F32)),
        2,
    )(arrived, filter_gain)
    near = lax.all_to_all(copies, XY, 0, 0, tiled=True)
    far = across(near)
    gf, gp = call(
        grads_near_kernel,
        (shape((width, beads_grp), F32), shape((8, beads_grp), F32)),
        3 + len(blocks),
    )(cs, kvrel, near, *blocks)
    parts = call(
        grads_far_kernel,
        shape((n_z, width + 8, beads_dev), BF16),
        6 + len(blocks),
        scalars=1,
    )(scal, cs, kvrel, far, gf, gp, *blocks)
    outs = (
        shape((beads_dev, width), BF16),
        shape((3, beads_dev), F32),
        shape((16, width), F32),
    )
    return call(lambda *refs: total_kernel(spec_scale, *refs), outs, 2)(
        lax.all_to_all(parts, Z, 0, 0, tiled=True), grad_filter
    )


def solution(mesh):
    torus = Mesh(mesh.devices.reshape(4, 4, 2, 2, mesh.shape["waves"]), ALL)
    beads = ("x", "y", "zh", "core")
    return jax.shard_map(
        body,
        mesh=torus,
        in_specs=(P(None, beads), P(ALL, None), P(ALL, None), P(), P(ALL, None)),
        out_specs=(P(ALL, None), P(None, ALL), P(ALL, None)),
        check_vma=False,
    )
```

```python
import math

import jax
import jax.numpy as jnp
from jax import lax
from jax.experimental import pallas as pl
from jax.experimental.pallas import tpu as pltpu
from jax.sharding import Mesh
from jax.sharding import PartitionSpec as P


ALL = ("x", "y", "zh", "core", "zl")
Z = ("zh", "zl")
XY = ("x", "y")
BF16 = jnp.bfloat16
F32 = jnp.float32
LANES = 128

SIN_TURN = (6.28318501, -41.3416557, 81.6010056, -76.5497818, 39.536705)


def sin_turn(h):
    s = h * h
    poly = SIN_TURN[-1]
    for c in SIN_TURN[-2::-1]:
        poly = poly * s + c
    return poly * h


def load_kernel(cot, feat, pos, wv, own, sent, pos_near, wv_near, sems):
    beads, width = cot.shape
    copies = [
        pltpu.make_async_copy(cot, own.at[:, :width], sems.at[0]),
        pltpu.make_async_copy(feat, own.at[:, width:], sems.at[1]),
        pltpu.make_async_copy(pos, pos_near, sems.at[2]),
        pltpu.make_async_copy(wv, wv_near, sems.at[3]),
    ]
    for c in copies:
        c.start()
    for c in copies:
        c.wait()
    sent[:beads, :] = own[...]
    left = pos_near[...]
    parts = []
    for _ in range(3):
        part = left.astype(BF16).astype(F32)
        parts.append(part)
        left = left - part
    parts.append(jnp.zeros((7, left.shape[1]), F32))
    sent[beads:, :] = jnp.concatenate(parts, 0).astype(BF16)


def trig_rows(kcols, pos, cs, zh, zl, first):
    n_xy = cs.shape[1]
    n_z = cs.shape[4] // LANES
    n_zl = n_z // 2
    columns = [
        pl.multiple_of(lax.rem(zh * n_zl + zl + n_z - first - i, n_z) * LANES, LANES)
        for i in range(n_zl)
    ]

    def step(i, carry):
        dc, xy = i // n_xy, lax.rem(i, n_xy)
        cols = kcols[pl.ds(pl.multiple_of(i * 16, 16), 16), :]
        t = cols[:, 0:1] * pos[0:1] + cols[:, 1:2] * pos[1:2] + cols[:, 2:3] * pos[2:3]
        f = t - jnp.round(t)
        cosine = sin_turn(0.25 - jnp.abs(f)).astype(BF16)
        sine = sin_turn(jnp.maximum(jnp.minimum(f, 0.5 - f), -0.5 - f)).astype(BF16)
        for j, column in enumerate(columns):
            part = slice(j * LANES, (j + 1) * LANES)
            cs[dc, xy, 0, :, pl.ds(column, LANES)] = cosine[:, part]
            cs[dc, xy, 1, :, pl.ds(column, LANES)] = sine[:, part]
        return carry

    lax.fori_loop(0, 2 * n_xy, step, 0, unroll=4)


def trig_near_kernel(pos, wv, cs, kvrel, kcols, kvt):
    zh, zl, core = (lax.axis_index(a) for a in ("zh", "zl", "core"))
    n_xy = cs.shape[1]
    n_zl = cs.shape[4] // LANES // 2
    for xy in range(n_xy):
        at = pl.multiple_of((xy * 2 + zh) * LANES, LANES)
        piece = wv[:, pl.ds(at, LANES)]
        piece = jnp.concatenate([piece, jnp.zeros((5, LANES), F32)], 0)
        kvt[xy, :, 0:8] = piece.T
    for dc in range(2):
        at = pl.multiple_of((jnp.bitwise_xor(core, dc) * n_zl + zl) * 16, 16)
        for xy in range(n_xy):
            cols = kvt[xy, pl.ds(at, 16), 0:8]
            rows = slice((dc * n_xy + xy) * 16, (dc * n_xy + xy + 1) * 16)
            hi = cols.astype(BF16)
            lo = (cols - hi.astype(F32)).astype(BF16)
            kvrel[rows, :] = jnp.concatenate([hi, lo], 1)
            kcols[rows, :] = cols * (1.0 / (2.0 * math.pi))
    trig_rows(kcols, pos[...], cs, zh, zl, zh * n_zl)


def trig_far_kernel(ahead, behind, kcols, _, cs):
    zh, zl = lax.axis_index("zh"), lax.axis_index("zl")
    n_zl = cs.shape[4] // LANES // 2
    beads = ahead.shape[0] - 16
    rows = jnp.where(zl < n_zl // 2, ahead[beads:, :], behind[beads:, :]).astype(F32)
    pos = rows[0:3] + rows[3:6] + rows[6:9]
    trig_rows(kcols, pos, cs, zh, zl, jnp.bitwise_xor(zh, 1) * n_zl)


def joined(pieces):
    return jnp.concatenate([p[:LANES] for p in pieces], 0)


def early_kernel(cs, *refs):
    pieces, out = refs[:-1], refs[-1]
    rows = cs[...].reshape(-1, cs.shape[4])
    n, m = 3 * LANES, rows.shape[1] - 3 * LANES
    parts = [rows[:, :n], rows[:, n + LANES : m], rows[:, m + LANES :]]
    part = jnp.dot(jnp.concatenate(parts, 1), joined(pieces), preferred_element_type=F32)
    out[...] = part.reshape(out.shape)


def late_kernel(dc, cs, early, ahead, behind, out):
    rows = cs[dc].reshape(-1, cs.shape[4])
    n, m = 3 * LANES, rows.shape[1] - 3 * LANES
    rows = jnp.concatenate([rows[:, n : n + LANES], rows[:, m : m + LANES]], 1)
    part = jnp.dot(rows, joined([ahead, behind]), preferred_element_type=F32)
    out[...] = (part.reshape(out.shape) + early[dc]).astype(out.dtype)


def filter_kernel(spec_scale, wave_scale, arrived, gain, out, grad_filter):
    n = arrived.shape[0]
    width = gain.shape[1]
    total = arrived[0].astype(F32)
    for i in range(1, n):
        total = total + arrived[i].astype(F32)
    total = total.reshape(2, 16, 2 * width)
    cot = total[:, :, :width] * wave_scale
    spec = total[:, :, width:] * spec_scale
    g = gain[...].astype(F32)
    grad_filter[...] = cot[0] * spec[0] + cot[1] * spec[1]
    filt = (g[None] * spec * (wave_scale / spec_scale)).astype(BF16)
    dspec = (g[None] * cot).astype(BF16)
    both = jnp.concatenate([filt, dspec], 2).reshape(32, 2 * width)
    for i in range(n):
        out[i] = both


def half_gradients(dc, cs, kvrel, stacked, beads_all):
    n_xy, beads = cs.shape[1], cs.shape[4]
    width = beads_all.shape[1] // 2
    both = stacked[...].reshape(n_xy * 32, 2 * width)
    ab = lax.dot_general(both, beads_all, (((1,), (1,)), ((), ())), preferred_element_type=F32)
    ab = ab.reshape(n_xy, 2, 16, beads)
    d = cs[dc, :, 0].astype(F32) * ab[:, 1] - cs[dc, :, 1].astype(F32) * ab[:, 0]
    d = d.reshape(n_xy * 16, beads).astype(BF16)
    kv = kvrel[dc * n_xy * 16 : (dc + 1) * n_xy * 16, :]
    gp = lax.dot_general(kv, d, (((0,), (0,)), ((), ())), preferred_element_type=F32)
    rows = cs[dc].reshape(n_xy * 32, beads)
    gf = lax.dot_general(
        both[:, width:], rows, (((0,), (0,)), ((), ())), preferred_element_type=F32
    )
    return gf, gp[0:8] + gp[8:16]


def grads_near_kernel(cs, kvrel, stacked, *refs):
    pieces, (gf_out, gp_out) = refs[:-2], refs[-2:]
    beads_all = joined(pieces)
    gf, gp = half_gradients(0, cs, kvrel, stacked, beads_all)
    gf_out[...] = gf
    gp_out[...] = gp


def grads_far_kernel(cs, kvrel, stacked, gf_in, gp_in, *refs):
    pieces, out = refs[:-1], refs[-1]
    beads_all = joined(pieces)
    gf, gp = half_gradients(1, cs, kvrel, stacked, beads_all)
    gf = (gf + gf_in[...]).astype(BF16)
    gp = gp + gp_in[...]
    hi = gp.astype(BF16).astype(F32)
    tail = jnp.concatenate([hi[0:3], (gp - hi)[0:3], jnp.zeros_like(gp[0:2])], 0).astype(BF16)
    n_z = out.shape[0]
    width = gf.shape[0]
    here = lax.axis_index(Z)
    for shift in range(n_z):
        at = slice(shift * LANES, (shift + 1) * LANES)
        to = lax.rem(here + n_z - shift, n_z)
        out[to, 0:width, :] = gf[:, at]
        out[to, width : width + 8, :] = tail[:, at]


def total_kernel(spec_scale, arrived, grad_filter, gf_out, gp_out, filter_out):
    total = arrived[0].astype(F32)
    for i in range(1, arrived.shape[0]):
        total = total + arrived[i].astype(F32)
    total = total * spec_scale
    width = gf_out.shape[1]
    gf_out[...] = total[:width].T.astype(BF16)
    gp_out[...] = total[width : width + 3] + total[width + 3 : width + 6]
    filter_out[...] = grad_filter[...]


def call(kernel, out_shape, n_in, scratch=(), aliases=None, space=pltpu.VMEM):
    specs = [pl.BlockSpec(memory_space=space)] * n_in
    outs = jax.tree.map(lambda _: pl.BlockSpec(memory_space=pltpu.VMEM), out_shape)
    return pl.pallas_call(
        kernel,
        out_shape=out_shape,
        in_specs=specs,
        out_specs=outs,
        scratch_shapes=scratch,
        input_output_aliases=aliases or {},
        compiler_params=pltpu.CompilerParams(vmem_limit_bytes=16 << 20),
    )


def shape(dims, dtype):
    return jax.ShapeDtypeStruct(dims, dtype)


def body(positions, features, cotangent, wavevectors, filter_gain):
    n_z = lax.axis_size(Z)
    n_xy = lax.axis_size(XY)
    beads_dev, width = features.shape
    beads_grp = beads_dev * n_z
    n_beads = beads_grp * n_xy * 2
    spec_scale = 1.0 / math.sqrt(n_beads)
    wave_scale = 1.0 / math.sqrt(wavevectors.shape[1])

    def along_z(a, k):
        return lax.ppermute(a, Z, [(i, (i + k) % n_z) for i in range(n_z)])

    def across(a):
        return lax.ppermute(a, "core", [(0, 1), (1, 0)])

    inputs = (cotangent, features, positions, wavevectors)
    inputs = [pltpu.with_memory_space_constraint(a, pltpu.HBM) for a in inputs]
    own, sent, pos_near, wv_near = call(
        load_kernel,
        (
            shape((beads_dev, 2 * width), BF16),
            shape((beads_dev + 16, 2 * width), BF16),
            shape(positions.shape, F32),
            shape(wavevectors.shape, F32),
        ),
        4,
        scratch=[pltpu.SemaphoreType.DMA((4,))],
        space=pltpu.HBM,
    )(*inputs)
    pieces = {0: own, 2: along_z(sent, 2), 6: along_z(sent, -2)}

    n_rows = 2 * n_xy * 16
    cs_shape = shape((2, n_xy, 2, 16, beads_grp), BF16)
    trig = call(
        trig_near_kernel,
        (cs_shape, shape((n_rows, 16), BF16), shape((n_rows, 8), F32)),
        2,
        scratch=[pltpu.VMEM((n_xy, LANES, 8), F32)],
    )(pos_near, wv_near)
    own, trig = lax.optimization_barrier((own, trig))
    pieces[1], pieces[7] = along_z(own, 1), along_z(own, -1)
    pieces[2], pieces[6], trig = lax.optimization_barrier((pieces[2], pieces[6], trig))
    ahead, behind = pieces[2][:beads_dev], pieces[6][:beads_dev]
    onward = jnp.where(lax.axis_index("core") == 0, ahead, behind)
    n_zl = lax.axis_size("zl")

    def at(z, core):
        return (z // n_zl * 2 + core) * n_zl + z % n_zl

    pairs = [(at(z, c), at((z + 2 - 4 * c) % n_z, c)) for z in range(n_z) for c in range(2)]
    pieces[4] = lax.ppermute(onward, ("zh", "core", "zl"), pairs)
    pieces[3], pieces[5] = along_z(ahead, 1), along_z(behind, -1)
    late_blocks = [pieces[3], pieces[5]]
    blocks = [pieces[k] for k in range(n_z)]
    cs = call(trig_far_kernel, cs_shape, 4, aliases={3: 0})(
        pieces[2], pieces[6], trig[2], trig[0]
    )
    kvrel = trig[1]

    near_blocks = [blocks[k] for k in range(n_z) if k not in (3, n_z - 3)]
    early = call(
        early_kernel, shape((2, n_xy, 32, 2 * width), F32), 1 + len(near_blocks)
    )(cs, *near_blocks)

    def spectra(dc, dtype):
        return call(
            lambda *refs: late_kernel(dc, *refs),
            shape((n_xy, 32, 2 * width), dtype),
            2 + len(late_blocks),
        )(cs, early, *late_blocks)

    theirs = across(spectra(1, BF16))
    mine = (spectra(0, F32) + theirs.astype(F32)).astype(BF16)
    arrived = lax.all_to_all(mine, XY, 0, 0, tiled=True)
    copies, grad_filter = call(
        lambda *refs: filter_kernel(spec_scale, wave_scale, *refs),
        (shape((n_xy, 32, 2 * width), BF16), shape((16, width), F32)),
        2,
    )(arrived, filter_gain)
    near = lax.all_to_all(copies, XY, 0, 0, tiled=True)
    far = across(near)
    gf, gp = call(
        grads_near_kernel,
        (shape((width, beads_grp), F32), shape((8, beads_grp), F32)),
        3 + len(blocks),
    )(cs, kvrel, near, *blocks)
    parts = call(
        grads_far_kernel,
        shape((n_z, width + 8, beads_dev), BF16),
        5 + len(blocks),
    )(cs, kvrel, far, gf, gp, *blocks)
    outs = (
        shape((beads_dev, width), BF16),
        shape((3, beads_dev), F32),
        shape((16, width), F32),
    )
    return call(lambda *refs: total_kernel(spec_scale, *refs), outs, 2)(
        lax.all_to_all(parts, Z, 0, 0, tiled=True), grad_filter
    )


def solution(mesh):
    torus = Mesh(mesh.devices.reshape(4, 4, 2, 2, mesh.shape["waves"]), ALL)
    beads = ("x", "y", "zh", "core")
    return jax.shard_map(
        body,
        mesh=torus,
        in_specs=(P(None, beads), P(ALL, None), P(ALL, None), P(), P(ALL, None)),
        out_specs=(P(ALL, None), P(None, ALL), P(ALL, None)),
        check_vma=False,
    )
```

```python
import math

import jax
import jax.numpy as jnp
from jax import lax
from jax.experimental import pallas as pl
from jax.experimental.pallas import tpu as pltpu
from jax.sharding import Mesh
from jax.sharding import PartitionSpec as P


ALL = ("x", "y", "zh", "core", "zl")
Z = ("zh", "zl")
XY = ("x", "y")
BF16 = jnp.bfloat16
F32 = jnp.float32
LANES = 128

SIN_TURN = (6.28318501, -41.3416557, 81.6010056, -76.5497818, 39.536705)


def sin_turn(h):
    s = h * h
    poly = SIN_TURN[-1]
    for c in SIN_TURN[-2::-1]:
        poly = poly * s + c
    return poly * h


def load_kernel(cot, feat, pos, wv, own, pos_near, wv_near, sems):
    width = cot.shape[1]
    copies = [
        pltpu.make_async_copy(cot, own.at[:, :width], sems.at[0]),
        pltpu.make_async_copy(feat, own.at[:, width:], sems.at[1]),
        pltpu.make_async_copy(pos, pos_near, sems.at[2]),
        pltpu.make_async_copy(wv, wv_near, sems.at[3]),
    ]
    for c in copies:
        c.start()
    for c in copies:
        c.wait()


def trig_rows(kcols, pos, cs, zh, zl, first):
    n_xy = cs.shape[1]
    n_z = cs.shape[4] // LANES
    n_zl = n_z // 2
    columns = [
        pl.multiple_of(lax.rem(zh * n_zl + zl + n_z - first - i, n_z) * LANES, LANES)
        for i in range(n_zl)
    ]

    def step(i, carry):
        dc, xy = i // n_xy, lax.rem(i, n_xy)
        cols = kcols[pl.ds(pl.multiple_of(i * 16, 16), 16), :]
        t = cols[:, 0:1] * pos[0:1] + cols[:, 1:2] * pos[1:2] + cols[:, 2:3] * pos[2:3]
        f = t - jnp.round(t)
        cosine = sin_turn(0.25 - jnp.abs(f)).astype(BF16)
        sine = sin_turn(jnp.maximum(jnp.minimum(f, 0.5 - f), -0.5 - f)).astype(BF16)
        for j, column in enumerate(columns):
            part = slice(j * LANES, (j + 1) * LANES)
            cs[dc, xy, 0, :, pl.ds(column, LANES)] = cosine[:, part]
            cs[dc, xy, 1, :, pl.ds(column, LANES)] = sine[:, part]
        return carry

    lax.fori_loop(0, 2 * n_xy, step, 0, unroll=4)


def trig_near_kernel(pos, wv, cs, kvrel, kcols, kvt):
    zh, zl, core = (lax.axis_index(a) for a in ("zh", "zl", "core"))
    n_xy = cs.shape[1]
    n_zl = cs.shape[4] // LANES // 2
    for xy in range(n_xy):
        at = pl.multiple_of((xy * 2 + zh) * LANES, LANES)
        piece = wv[:, pl.ds(at, LANES)]
        piece = jnp.concatenate([piece, jnp.zeros((5, LANES), F32)], 0)
        kvt[xy, :, 0:8] = piece.T
    for dc in range(2):
        at = pl.multiple_of((jnp.bitwise_xor(core, dc) * n_zl + zl) * 16, 16)
        for xy in range(n_xy):
            cols = kvt[xy, pl.ds(at, 16), 0:8]
            rows = slice((dc * n_xy + xy) * 16, (dc * n_xy + xy + 1) * 16)
            hi = cols.astype(BF16)
            lo = (cols - hi.astype(F32)).astype(BF16)
            kvrel[rows, :] = jnp.concatenate([hi, lo], 1)
            kcols[rows, :] = cols * (1.0 / (2.0 * math.pi))
    trig_rows(kcols, pos[...], cs, zh, zl, zh * n_zl)


def trig_far_kernel(pos, kcols, _, cs):
    zh, zl = lax.axis_index("zh"), lax.axis_index("zl")
    n_zl = cs.shape[4] // LANES // 2
    trig_rows(kcols, pos[...], cs, zh, zl, jnp.bitwise_xor(zh, 1) * n_zl)


def joined(pieces):
    return jnp.concatenate([p[:LANES] for p in pieces], 0)


def early_kernel(cs, *refs):
    pieces, out = refs[:-1], refs[-1]
    rows = cs[...].reshape(-1, cs.shape[4])
    n = rows.shape[1] // 2
    rows = jnp.concatenate([rows[:, :n], rows[:, n + LANES :]], 1)
    part = jnp.dot(rows, joined(pieces), preferred_element_type=F32)
    out[...] = part.reshape(out.shape)


def late_kernel(dc, cs, early, block, out):
    rows = cs[dc].reshape(-1, cs.shape[4])
    n = rows.shape[1] // 2
    part = jnp.dot(rows[:, n : n + LANES], block[...], preferred_element_type=F32)
    out[...] = (part.reshape(out.shape) + early[dc]).astype(out.dtype)


def filter_kernel(spec_scale, wave_scale, arrived, gain, out, grad_filter):
    n = arrived.shape[0]
    width = gain.shape[1]
    total = arrived[0].astype(F32)
    for i in range(1, n):
        total = total + arrived[i].astype(F32)
    total = total.reshape(2, 16, 2 * width)
    cot = total[:, :, :width] * wave_scale
    spec = total[:, :, width:] * spec_scale
    g = gain[...].astype(F32)
    grad_filter[...] = cot[0] * spec[0] + cot[1] * spec[1]
    filt = (g[None] * spec * (wave_scale / spec_scale)).astype(BF16)
    dspec = (g[None] * cot).astype(BF16)
    both = jnp.concatenate([filt, dspec], 2).reshape(32, 2 * width)
    for i in range(n):
        out[i] = both


def half_gradients(dc, cs, kvrel, stacked, beads_all):
    n_xy, beads = cs.shape[1], cs.shape[4]
    width = beads_all.shape[1] // 2
    both = stacked[...].reshape(n_xy * 32, 2 * width)
    ab = lax.dot_general(both, beads_all, (((1,), (1,)), ((), ())), preferred_element_type=F32)
    ab = ab.reshape(n_xy, 2, 16, beads)
    d = cs[dc, :, 0].astype(F32) * ab[:, 1] - cs[dc, :, 1].astype(F32) * ab[:, 0]
    d = d.reshape(n_xy * 16, beads).astype(BF16)
    kv = kvrel[dc * n_xy * 16 : (dc + 1) * n_xy * 16, :]
    gp = lax.dot_general(kv, d, (((0,), (0,)), ((), ())), preferred_element_type=F32)
    rows = cs[dc].reshape(n_xy * 32, beads)
    gf = lax.dot_general(
        both[:, width:], rows, (((0,), (0,)), ((), ())), preferred_element_type=F32
    )
    return gf, gp[0:8] + gp[8:16]


def grads_near_kernel(cs, kvrel, stacked, *refs):
    pieces, (gf_out, gp_out) = refs[:-2], refs[-2:]
    beads_all = joined(pieces)
    gf, gp = half_gradients(0, cs, kvrel, stacked, beads_all)
    gf_out[...] = gf
    gp_out[...] = gp


def grads_far_kernel(cs, kvrel, stacked, gf_in, gp_in, *refs):
    pieces, out = refs[:-1], refs[-1]
    beads_all = joined(pieces)
    gf, gp = half_gradients(1, cs, kvrel, stacked, beads_all)
    gf = (gf + gf_in[...]).astype(BF16)
    gp = gp + gp_in[...]
    hi = gp.astype(BF16).astype(F32)
    tail = jnp.concatenate([hi[0:3], (gp - hi)[0:3], jnp.zeros_like(gp[0:2])], 0).astype(BF16)
    n_z = out.shape[0]
    width = gf.shape[0]
    here = lax.axis_index(Z)
    for shift in range(n_z):
        at = slice(shift * LANES, (shift + 1) * LANES)
        to = lax.rem(here + n_z - shift, n_z)
        out[to, 0:width, :] = gf[:, at]
        out[to, width : width + 8, :] = tail[:, at]


def total_kernel(spec_scale, arrived, grad_filter, gf_out, gp_out, filter_out):
    total = arrived[0].astype(F32)
    for i in range(1, arrived.shape[0]):
        total = total + arrived[i].astype(F32)
    total = total * spec_scale
    width = gf_out.shape[1]
    gf_out[...] = total[:width].T.astype(BF16)
    gp_out[...] = total[width : width + 3] + total[width + 3 : width + 6]
    filter_out[...] = grad_filter[...]


def call(kernel, out_shape, n_in, scratch=(), aliases=None, space=pltpu.VMEM):
    specs = [pl.BlockSpec(memory_space=space)] * n_in
    outs = jax.tree.map(lambda _: pl.BlockSpec(memory_space=pltpu.VMEM), out_shape)
    return pl.pallas_call(
        kernel,
        out_shape=out_shape,
        in_specs=specs,
        out_specs=outs,
        scratch_shapes=scratch,
        input_output_aliases=aliases or {},
        compiler_params=pltpu.CompilerParams(vmem_limit_bytes=16 << 20),
    )


def shape(dims, dtype):
    return jax.ShapeDtypeStruct(dims, dtype)


def body(positions, features, cotangent, wavevectors, filter_gain):
    n_z = lax.axis_size(Z)
    n_xy = lax.axis_size(XY)
    beads_dev, width = features.shape
    beads_grp = beads_dev * n_z
    n_beads = beads_grp * n_xy * 2
    spec_scale = 1.0 / math.sqrt(n_beads)
    wave_scale = 1.0 / math.sqrt(wavevectors.shape[1])

    def along_z(a, k):
        return lax.ppermute(a, Z, [(i, (i + k) % n_z) for i in range(n_z)])

    def across(a):
        return lax.ppermute(a, "core", [(0, 1), (1, 0)])

    inputs = (cotangent, features, positions, wavevectors)
    inputs = [pltpu.with_memory_space_constraint(a, pltpu.HBM) for a in inputs]
    own, pos_near, wv_near = call(
        load_kernel,
        (
            shape((beads_dev, 2 * width), BF16),
            shape(positions.shape, F32),
            shape(wavevectors.shape, F32),
        ),
        4,
        scratch=[pltpu.SemaphoreType.DMA((4,))],
        space=pltpu.HBM,
    )(*inputs)
    pieces = {0: own, 2: along_z(own, 2), 6: along_z(own, -2)}

    n_rows = 2 * n_xy * 16
    cs_shape = shape((2, n_xy, 2, 16, beads_grp), BF16)
    trig = call(
        trig_near_kernel,
        (cs_shape, shape((n_rows, 16), BF16), shape((n_rows, 8), F32)),
        2,
        scratch=[pltpu.VMEM((n_xy, LANES, 8), F32)],
    )(pos_near, wv_near)
    own, trig, pos_near = lax.optimization_barrier((own, trig, pos_near))
    pieces[1], pieces[7] = along_z(own, 1), along_z(own, -1)
    turns = [2 if i % (n_z // 2) < n_z // 4 else -2 for i in range(n_z)]
    pos_far = lax.ppermute(pos_near, Z, [((i - turns[i]) % n_z, i) for i in range(n_z)])
    pieces[2], pieces[6], trig = lax.optimization_barrier((pieces[2], pieces[6], trig))
    pieces[3], pieces[5] = along_z(pieces[2], 1), along_z(pieces[6], -1)
    cs = call(trig_far_kernel, cs_shape, 3, aliases={2: 0})(pos_far, trig[2], trig[0])
    kvrel = trig[1]
    pieces[3], pieces[5], cs = lax.optimization_barrier((pieces[3], pieces[5], cs))
    onward = jnp.where(lax.axis_index("core") == 0, pieces[3], pieces[5])
    n_zl = lax.axis_size("zl")

    def at(z, core):
        return (z // n_zl * 2 + core) * n_zl + z % n_zl

    pairs = [(at(z, c), at((z + 1 - 2 * c) % n_z, c)) for z in range(n_z) for c in range(2)]
    pieces[4] = lax.ppermute(onward, ("zh", "core", "zl"), pairs)
    blocks = [pieces[k] for k in range(n_z)]
    near_blocks = [blocks[k] for k in range(n_z) if k != n_z // 2]
    early = call(
        early_kernel, shape((2, n_xy, 32, 2 * width), F32), 1 + len(near_blocks)
    )(cs, *near_blocks)

    def spectra(dc, dtype):
        return call(
            lambda *refs: late_kernel(dc, *refs),
            shape((n_xy, 32, 2 * width), dtype),
            3,
        )(cs, early, pieces[4])

    theirs = across(spectra(1, BF16))
    mine = (spectra(0, F32) + theirs.astype(F32)).astype(BF16)
    arrived = lax.all_to_all(mine, XY, 0, 0, tiled=True)
    copies, grad_filter = call(
        lambda *refs: filter_kernel(spec_scale, wave_scale, *refs),
        (shape((n_xy, 32, 2 * width), BF16), shape((16, width), F32)),
        2,
    )(arrived, filter_gain)
    near = lax.all_to_all(copies, XY, 0, 0, tiled=True)
    far = across(near)
    gf, gp = call(
        grads_near_kernel,
        (shape((width, beads_grp), F32), shape((8, beads_grp), F32)),
        3 + len(blocks),
    )(cs, kvrel, near, *blocks)
    parts = call(
        grads_far_kernel,
        shape((n_z, width + 8, beads_dev), BF16),
        5 + len(blocks),
    )(cs, kvrel, far, gf, gp, *blocks)
    outs = (
        shape((beads_dev, width), BF16),
        shape((3, beads_dev), F32),
        shape((16, width), F32),
    )
    return call(lambda *refs: total_kernel(spec_scale, *refs), outs, 2)(
        lax.all_to_all(parts, Z, 0, 0, tiled=True), grad_filter
    )


def solution(mesh):
    torus = Mesh(mesh.devices.reshape(4, 4, 2, 2, mesh.shape["waves"]), ALL)
    beads = ("x", "y", "zh", "core")
    return jax.shard_map(
        body,
        mesh=torus,
        in_specs=(P(None, beads), P(ALL, None), P(ALL, None), P(), P(ALL, None)),
        out_specs=(P(ALL, None), P(None, ALL), P(ALL, None)),
        check_vma=False,
    )
```

```python
import math

import jax
import jax.numpy as jnp
from jax import lax
from jax.experimental import pallas as pl
from jax.experimental.pallas import tpu as pltpu
from jax.sharding import Mesh
from jax.sharding import PartitionSpec as P


ALL = ("x", "y", "zh", "core", "zl")
Z = ("zh", "zl")
XY = ("x", "y")
BF16 = jnp.bfloat16
F32 = jnp.float32
LANES = 128

SIN_TURN = (6.28318501, -41.3416557, 81.6010056, -76.5497818, 39.536705)


def sin_turn(h):
    s = h * h
    poly = SIN_TURN[-1]
    for c in SIN_TURN[-2::-1]:
        poly = poly * s + c
    return poly * h


def load_kernel(cot, feat, pos, wv, own, pos_near, wv_near, sems):
    width = cot.shape[1]
    copies = [
        pltpu.make_async_copy(cot, own.at[:, :width], sems.at[0]),
        pltpu.make_async_copy(feat, own.at[:, width:], sems.at[1]),
        pltpu.make_async_copy(pos, pos_near, sems.at[2]),
        pltpu.make_async_copy(wv, wv_near, sems.at[3]),
    ]
    for c in copies:
        c.start()
    for c in copies:
        c.wait()


def trig_rows(kcols, pos, cs, zh, zl, first):
    n_xy = cs.shape[1]
    n_z = cs.shape[4] // LANES
    n_zl = n_z // 2
    columns = [
        pl.multiple_of(lax.rem(zh * n_zl + zl + n_z - first - i, n_z) * LANES, LANES)
        for i in range(n_zl)
    ]

    def step(i, carry):
        dc, xy = i // n_xy, lax.rem(i, n_xy)
        cols = kcols[pl.ds(pl.multiple_of(i * 16, 16), 16), :]
        t = cols[:, 0:1] * pos[0:1] + cols[:, 1:2] * pos[1:2] + cols[:, 2:3] * pos[2:3]
        f = t - jnp.round(t)
        cosine = sin_turn(0.25 - jnp.abs(f)).astype(BF16)
        sine = sin_turn(jnp.maximum(jnp.minimum(f, 0.5 - f), -0.5 - f)).astype(BF16)
        for j, column in enumerate(columns):
            part = slice(j * LANES, (j + 1) * LANES)
            cs[dc, xy, 0, :, pl.ds(column, LANES)] = cosine[:, part]
            cs[dc, xy, 1, :, pl.ds(column, LANES)] = sine[:, part]
        return carry

    lax.fori_loop(0, 2 * n_xy, step, 0, unroll=4)


def trig_near_kernel(pos, wv, cs, kvrel, kcols, kvt):
    zh, zl, core = (lax.axis_index(a) for a in ("zh", "zl", "core"))
    n_xy = cs.shape[1]
    n_zl = cs.shape[4] // LANES // 2
    for xy in range(n_xy):
        at = pl.multiple_of((xy * 2 + zh) * LANES, LANES)
        piece = wv[:, pl.ds(at, LANES)]
        piece = jnp.concatenate([piece, jnp.zeros((5, LANES), F32)], 0)
        kvt[xy, :, 0:8] = piece.T
    for dc in range(2):
        at = pl.multiple_of((jnp.bitwise_xor(core, dc) * n_zl + zl) * 16, 16)
        for xy in range(n_xy):
            cols = kvt[xy, pl.ds(at, 16), 0:8]
            rows = slice((dc * n_xy + xy) * 16, (dc * n_xy + xy + 1) * 16)
            hi = cols.astype(BF16)
            lo = (cols - hi.astype(F32)).astype(BF16)
            kvrel[rows, :] = jnp.concatenate([hi, lo], 1)
            kcols[rows, :] = cols * (1.0 / (2.0 * math.pi))
    trig_rows(kcols, pos[...], cs, zh, zl, zh * n_zl)


def trig_far_kernel(pos, kcols, _, cs):
    zh, zl = lax.axis_index("zh"), lax.axis_index("zl")
    n_zl = cs.shape[4] // LANES // 2
    trig_rows(kcols, pos[...], cs, zh, zl, jnp.bitwise_xor(zh, 1) * n_zl)


def joined(pieces):
    return jnp.concatenate([p[:LANES] for p in pieces], 0)


def early_kernel(cs, *refs):
    pieces, out = refs[:-1], refs[-1]
    rows = cs[...].reshape(-1, cs.shape[4])
    n = rows.shape[1] // 2
    rows = jnp.concatenate([rows[:, :n], rows[:, n + LANES :]], 1)
    part = jnp.dot(rows, joined(pieces), preferred_element_type=F32)
    out[...] = part.reshape(out.shape)


def late_kernel(dc, cs, early, block, out):
    rows = cs[dc].reshape(-1, cs.shape[4])
    n = rows.shape[1] // 2
    part = jnp.dot(rows[:, n : n + LANES], block[...], preferred_element_type=F32)
    out[...] = (part.reshape(out.shape) + early[dc]).astype(out.dtype)


def filter_kernel(spec_scale, wave_scale, arrived, gain, out, grad_filter):
    n = arrived.shape[0]
    width = gain.shape[1]
    total = arrived[0].astype(F32)
    for i in range(1, n):
        total = total + arrived[i].astype(F32)
    total = total.reshape(2, 16, 2 * width)
    cot = total[:, :, :width] * wave_scale
    spec = total[:, :, width:] * spec_scale
    g = gain[...].astype(F32)
    grad_filter[...] = cot[0] * spec[0] + cot[1] * spec[1]
    filt = (g[None] * spec * (wave_scale / spec_scale)).astype(BF16)
    dspec = (g[None] * cot).astype(BF16)
    both = jnp.concatenate([filt, dspec], 2).reshape(32, 2 * width)
    for i in range(n):
        out[i] = both


def half_gradients(dc, cs, kvrel, stacked, beads_all):
    n_xy, beads = cs.shape[1], cs.shape[4]
    width = beads_all.shape[1] // 2
    both = stacked[...].reshape(n_xy * 32, 2 * width)
    ab = lax.dot_general(both, beads_all, (((1,), (1,)), ((), ())), preferred_element_type=F32)
    ab = ab.reshape(n_xy, 2, 16, beads)
    d = cs[dc, :, 0].astype(F32) * ab[:, 1] - cs[dc, :, 1].astype(F32) * ab[:, 0]
    d = d.reshape(n_xy * 16, beads).astype(BF16)
    kv = kvrel[dc * n_xy * 16 : (dc + 1) * n_xy * 16, :]
    gp = lax.dot_general(kv, d, (((0,), (0,)), ((), ())), preferred_element_type=F32)
    rows = cs[dc].reshape(n_xy * 32, beads)
    gf = lax.dot_general(
        both[:, width:], rows, (((0,), (0,)), ((), ())), preferred_element_type=F32
    )
    return gf, gp[0:8] + gp[8:16]


def grads_near_kernel(cs, kvrel, stacked, *refs):
    pieces, (gf_out, gp_out) = refs[:-2], refs[-2:]
    beads_all = joined(pieces)
    gf, gp = half_gradients(0, cs, kvrel, stacked, beads_all)
    gf_out[...] = gf
    gp_out[...] = gp


def grads_far_kernel(cs, kvrel, stacked, gf_in, gp_in, *refs):
    pieces, out = refs[:-1], refs[-1]
    beads_all = joined(pieces)
    gf, gp = half_gradients(1, cs, kvrel, stacked, beads_all)
    gf = (gf + gf_in[...]).astype(BF16)
    gp = gp + gp_in[...]
    hi = gp.astype(BF16).astype(F32)
    tail = jnp.concatenate([hi[0:3], (gp - hi)[0:3], jnp.zeros_like(gp[0:2])], 0).astype(BF16)
    n_z = out.shape[0]
    width = gf.shape[0]
    here = lax.axis_index(Z)
    for shift in range(n_z):
        at = slice(shift * LANES, (shift + 1) * LANES)
        to = lax.rem(here + n_z - shift, n_z)
        out[to, 0:width, :] = gf[:, at]
        out[to, width : width + 8, :] = tail[:, at]


def total_kernel(spec_scale, arrived, grad_filter, gf_out, gp_out, filter_out):
    total = arrived[0].astype(F32)
    for i in range(1, arrived.shape[0]):
        total = total + arrived[i].astype(F32)
    total = total * spec_scale
    width = gf_out.shape[1]
    gf_out[...] = total[:width].T.astype(BF16)
    gp_out[...] = total[width : width + 3] + total[width + 3 : width + 6]
    filter_out[...] = grad_filter[...]


def call(kernel, out_shape, n_in, scratch=(), aliases=None, space=pltpu.VMEM):
    specs = [pl.BlockSpec(memory_space=space)] * n_in
    outs = jax.tree.map(lambda _: pl.BlockSpec(memory_space=pltpu.VMEM), out_shape)
    return pl.pallas_call(
        kernel,
        out_shape=out_shape,
        in_specs=specs,
        out_specs=outs,
        scratch_shapes=scratch,
        input_output_aliases=aliases or {},
        compiler_params=pltpu.CompilerParams(vmem_limit_bytes=16 << 20),
    )


def shape(dims, dtype):
    return jax.ShapeDtypeStruct(dims, dtype)


def body(positions, features, cotangent, wavevectors, filter_gain):
    n_z = lax.axis_size(Z)
    n_xy = lax.axis_size(XY)
    beads_dev, width = features.shape
    beads_grp = beads_dev * n_z
    n_beads = beads_grp * n_xy * 2
    spec_scale = 1.0 / math.sqrt(n_beads)
    wave_scale = 1.0 / math.sqrt(wavevectors.shape[1])

    def along_z(a, k):
        return lax.ppermute(a, Z, [(i, (i + k) % n_z) for i in range(n_z)])

    def across(a):
        return lax.ppermute(a, "core", [(0, 1), (1, 0)])

    inputs = (cotangent, features, positions, wavevectors)
    inputs = [pltpu.with_memory_space_constraint(a, pltpu.HBM) for a in inputs]
    own, pos_near, wv_near = call(
        load_kernel,
        (
            shape((beads_dev, 2 * width), BF16),
            shape(positions.shape, F32),
            shape(wavevectors.shape, F32),
        ),
        4,
        scratch=[pltpu.SemaphoreType.DMA((4,))],
        space=pltpu.HBM,
    )(*inputs)
    pieces = {0: own, 2: along_z(own, 2), 6: along_z(own, -2)}

    n_rows = 2 * n_xy * 16
    cs_shape = shape((2, n_xy, 2, 16, beads_grp), BF16)
    trig = call(
        trig_near_kernel,
        (cs_shape, shape((n_rows, 16), BF16), shape((n_rows, 8), F32)),
        2,
        scratch=[pltpu.VMEM((n_xy, LANES, 8), F32)],
    )(pos_near, wv_near)
    own, trig, pos_near = lax.optimization_barrier((own, trig, pos_near))
    pieces[1], pieces[7] = along_z(own, 1), along_z(own, -1)
    turns = [2 if i % (n_z // 2) < n_z // 4 else -2 for i in range(n_z)]
    pos_far = lax.ppermute(pos_near, Z, [((i - turns[i]) % n_z, i) for i in range(n_z)])
    pieces[2], pieces[6], trig = lax.optimization_barrier((pieces[2], pieces[6], trig))
    ahead, behind = pieces[2], pieces[6]
    onward = jnp.where(lax.axis_index("core") == 0, ahead, behind)
    n_zl = lax.axis_size("zl")

    def at(z, core):
        return (z // n_zl * 2 + core) * n_zl + z % n_zl

    pairs = [(at(z, c), at((z + 2 - 4 * c) % n_z, c)) for z in range(n_z) for c in range(2)]
    pieces[4] = lax.ppermute(onward, ("zh", "core", "zl"), pairs)
    pieces[3], pieces[5] = along_z(ahead, 1), along_z(behind, -1)
    blocks = [pieces[k] for k in range(n_z)]
    cs = call(trig_far_kernel, cs_shape, 3, aliases={2: 0})(pos_far, trig[2], trig[0])
    kvrel = trig[1]

    near_blocks = [blocks[k] for k in range(n_z) if k != n_z // 2]
    early = call(
        early_kernel, shape((2, n_xy, 32, 2 * width), F32), 1 + len(near_blocks)
    )(cs, *near_blocks)

    def spectra(dc, dtype):
        return call(
            lambda *refs: late_kernel(dc, *refs),
            shape((n_xy, 32, 2 * width), dtype),
            3,
        )(cs, early, pieces[4])

    theirs = across(spectra(1, BF16))
    mine = (spectra(0, F32) + theirs.astype(F32)).astype(BF16)
    arrived = lax.all_to_all(mine, XY, 0, 0, tiled=True)
    copies, grad_filter = call(
        lambda *refs: filter_kernel(spec_scale, wave_scale, *refs),
        (shape((n_xy, 32, 2 * width), BF16), shape((16, width), F32)),
        2,
    )(arrived, filter_gain)
    near = lax.all_to_all(copies, XY, 0, 0, tiled=True)
    far = across(near)
    gf, gp = call(
        grads_near_kernel,
        (shape((width, beads_grp), F32), shape((8, beads_grp), F32)),
        3 + len(blocks),
    )(cs, kvrel, near, *blocks)
    parts = call(
        grads_far_kernel,
        shape((n_z, width + 8, beads_dev), BF16),
        5 + len(blocks),
    )(cs, kvrel, far, gf, gp, *blocks)
    outs = (
        shape((beads_dev, width), BF16),
        shape((3, beads_dev), F32),
        shape((16, width), F32),
    )
    return call(lambda *refs: total_kernel(spec_scale, *refs), outs, 2)(
        lax.all_to_all(parts, Z, 0, 0, tiled=True), grad_filter
    )


def solution(mesh):
    torus = Mesh(mesh.devices.reshape(4, 4, 2, 2, mesh.shape["waves"]), ALL)
    beads = ("x", "y", "zh", "core")
    return jax.shard_map(
        body,
        mesh=torus,
        in_specs=(P(None, beads), P(ALL, None), P(ALL, None), P(), P(ALL, None)),
        out_specs=(P(ALL, None), P(None, ALL), P(ALL, None)),
        check_vma=False,
    )
```

```python
import math

import jax
import jax.numpy as jnp
from jax import lax
from jax.experimental import pallas as pl
from jax.experimental.pallas import tpu as pltpu
from jax.sharding import Mesh
from jax.sharding import PartitionSpec as P


ALL = ("x", "y", "zh", "core", "zl")
Z = ("zh", "zl")
XY = ("x", "y")
BF16 = jnp.bfloat16
F32 = jnp.float32
LANES = 128

SIN_TURN = (6.28318501, -41.3416557, 81.6010056, -76.5497818, 39.536705)


def sin_turn(h):
    s = h * h
    poly = SIN_TURN[-1]
    for c in SIN_TURN[-2::-1]:
        poly = poly * s + c
    return poly * h


def load_kernel(cot, feat, pos, wv, own, pos_near, wv_near, sems):
    width = cot.shape[1]
    copies = [
        pltpu.make_async_copy(cot, own.at[:, :width], sems.at[0]),
        pltpu.make_async_copy(feat, own.at[:, width:], sems.at[1]),
        pltpu.make_async_copy(pos, pos_near, sems.at[2]),
        pltpu.make_async_copy(wv, wv_near, sems.at[3]),
    ]
    for c in copies:
        c.start()
    for c in copies:
        c.wait()


def trig_rows(kcols, pos, cs, zh, zl, first):
    n_xy = cs.shape[1]
    n_z = cs.shape[4] // LANES
    n_zl = n_z // 2
    columns = [
        pl.multiple_of(lax.rem(zh * n_zl + zl + n_z - first - i, n_z) * LANES, LANES)
        for i in range(n_zl)
    ]

    def step(i, carry):
        dc, xy = i // n_xy, lax.rem(i, n_xy)
        cols = kcols[pl.ds(pl.multiple_of(i * 16, 16), 16), :]
        t = cols[:, 0:1] * pos[0:1] + cols[:, 1:2] * pos[1:2] + cols[:, 2:3] * pos[2:3]
        f = t - jnp.round(t)
        cosine = sin_turn(0.25 - jnp.abs(f)).astype(BF16)
        sine = sin_turn(jnp.maximum(jnp.minimum(f, 0.5 - f), -0.5 - f)).astype(BF16)
        for j, column in enumerate(columns):
            part = slice(j * LANES, (j + 1) * LANES)
            cs[dc, xy, 0, :, pl.ds(column, LANES)] = cosine[:, part]
            cs[dc, xy, 1, :, pl.ds(column, LANES)] = sine[:, part]
        return carry

    lax.fori_loop(0, 2 * n_xy, step, 0, unroll=4)


def trig_near_kernel(pos, wv, cs, kvrel, kcols, kvt):
    zh, zl, core = (lax.axis_index(a) for a in ("zh", "zl", "core"))
    n_xy = cs.shape[1]
    n_zl = cs.shape[4] // LANES // 2
    for xy in range(n_xy):
        at = pl.multiple_of((xy * 2 + zh) * LANES, LANES)
        piece = wv[:, pl.ds(at, LANES)]
        piece = jnp.concatenate([piece, jnp.zeros((5, LANES), F32)], 0)
        kvt[xy, :, 0:8] = piece.T
    for dc in range(2):
        at = pl.multiple_of((jnp.bitwise_xor(core, dc) * n_zl + zl) * 16, 16)
        for xy in range(n_xy):
            cols = kvt[xy, pl.ds(at, 16), 0:8]
            rows = slice((dc * n_xy + xy) * 16, (dc * n_xy + xy + 1) * 16)
            hi = cols.astype(BF16)
            lo = (cols - hi.astype(F32)).astype(BF16)
            kvrel[rows, :] = jnp.concatenate([hi, lo], 1)
            kcols[rows, :] = cols * (1.0 / (2.0 * math.pi))
    trig_rows(kcols, pos[...], cs, zh, zl, zh * n_zl)


def trig_far_kernel(pos, kcols, _, cs):
    zh, zl = lax.axis_index("zh"), lax.axis_index("zl")
    n_zl = cs.shape[4] // LANES // 2
    trig_rows(kcols, pos[...], cs, zh, zl, jnp.bitwise_xor(zh, 1) * n_zl)


def joined(pieces):
    return jnp.concatenate([p[:LANES] for p in pieces], 0)


def early_kernel(cs, *refs):
    pieces, out = refs[:-1], refs[-1]
    rows = cs[...].reshape(-1, cs.shape[4])
    n, m = 3 * LANES, rows.shape[1] - 3 * LANES
    parts = [rows[:, :n], rows[:, n + LANES : m], rows[:, m + LANES :]]
    part = jnp.dot(jnp.concatenate(parts, 1), joined(pieces), preferred_element_type=F32)
    out[...] = part.reshape(out.shape)


def late_kernel(dc, cs, early, ahead, behind, out):
    rows = cs[dc].reshape(-1, cs.shape[4])
    n, m = 3 * LANES, rows.shape[1] - 3 * LANES
    rows = jnp.concatenate([rows[:, n : n + LANES], rows[:, m : m + LANES]], 1)
    part = jnp.dot(rows, joined([ahead, behind]), preferred_element_type=F32)
    out[...] = (part.reshape(out.shape) + early[dc]).astype(out.dtype)


def filter_kernel(spec_scale, wave_scale, arrived, gain, out, grad_filter):
    n = arrived.shape[0]
    width = gain.shape[1]
    total = arrived[0].astype(F32)
    for i in range(1, n):
        total = total + arrived[i].astype(F32)
    total = total.reshape(2, 16, 2 * width)
    cot = total[:, :, :width] * wave_scale
    spec = total[:, :, width:] * spec_scale
    g = gain[...].astype(F32)
    grad_filter[...] = cot[0] * spec[0] + cot[1] * spec[1]
    filt = (g[None] * spec * (wave_scale / spec_scale)).astype(BF16)
    dspec = (g[None] * cot).astype(BF16)
    both = jnp.concatenate([filt, dspec], 2).reshape(32, 2 * width)
    for i in range(n):
        out[i] = both


def half_gradients(dc, cs, kvrel, stacked, beads_all):
    n_xy, beads = cs.shape[1], cs.shape[4]
    width = beads_all.shape[1] // 2
    both = stacked[...].reshape(n_xy * 32, 2 * width)
    ab = lax.dot_general(both, beads_all, (((1,), (1,)), ((), ())), preferred_element_type=F32)
    ab = ab.reshape(n_xy, 2, 16, beads)
    d = cs[dc, :, 0].astype(F32) * ab[:, 1] - cs[dc, :, 1].astype(F32) * ab[:, 0]
    d = d.reshape(n_xy * 16, beads).astype(BF16)
    kv = kvrel[dc * n_xy * 16 : (dc + 1) * n_xy * 16, :]
    gp = lax.dot_general(kv, d, (((0,), (0,)), ((), ())), preferred_element_type=F32)
    rows = cs[dc].reshape(n_xy * 32, beads)
    gf = lax.dot_general(
        both[:, width:], rows, (((0,), (0,)), ((), ())), preferred_element_type=F32
    )
    return gf, gp[0:8] + gp[8:16]


def grads_near_kernel(cs, kvrel, stacked, *refs):
    pieces, (gf_out, gp_out) = refs[:-2], refs[-2:]
    beads_all = joined(pieces)
    gf, gp = half_gradients(0, cs, kvrel, stacked, beads_all)
    gf_out[...] = gf
    gp_out[...] = gp


def grads_far_kernel(cs, kvrel, stacked, gf_in, gp_in, *refs):
    pieces, out = refs[:-1], refs[-1]
    beads_all = joined(pieces)
    gf, gp = half_gradients(1, cs, kvrel, stacked, beads_all)
    gf = (gf + gf_in[...]).astype(BF16)
    gp = gp + gp_in[...]
    hi = gp.astype(BF16).astype(F32)
    tail = jnp.concatenate([hi[0:3], (gp - hi)[0:3], jnp.zeros_like(gp[0:2])], 0).astype(BF16)
    n_z = out.shape[0]
    width = gf.shape[0]
    here = lax.axis_index(Z)
    for shift in range(n_z):
        at = slice(shift * LANES, (shift + 1) * LANES)
        to = lax.rem(here + n_z - shift, n_z)
        out[to, 0:width, :] = gf[:, at]
        out[to, width : width + 8, :] = tail[:, at]


def total_kernel(spec_scale, arrived, grad_filter, gf_out, gp_out, filter_out):
    total = arrived[0].astype(F32)
    for i in range(1, arrived.shape[0]):
        total = total + arrived[i].astype(F32)
    total = total * spec_scale
    width = gf_out.shape[1]
    gf_out[...] = total[:width].T.astype(BF16)
    gp_out[...] = total[width : width + 3] + total[width + 3 : width + 6]
    filter_out[...] = grad_filter[...]


def call(kernel, out_shape, n_in, scratch=(), aliases=None, space=pltpu.VMEM):
    specs = [pl.BlockSpec(memory_space=space)] * n_in
    outs = jax.tree.map(lambda _: pl.BlockSpec(memory_space=pltpu.VMEM), out_shape)
    return pl.pallas_call(
        kernel,
        out_shape=out_shape,
        in_specs=specs,
        out_specs=outs,
        scratch_shapes=scratch,
        input_output_aliases=aliases or {},
        compiler_params=pltpu.CompilerParams(vmem_limit_bytes=16 << 20),
    )


def shape(dims, dtype):
    return jax.ShapeDtypeStruct(dims, dtype)


def body(positions, features, cotangent, wavevectors, filter_gain):
    n_z = lax.axis_size(Z)
    n_xy = lax.axis_size(XY)
    beads_dev, width = features.shape
    beads_grp = beads_dev * n_z
    n_beads = beads_grp * n_xy * 2
    spec_scale = 1.0 / math.sqrt(n_beads)
    wave_scale = 1.0 / math.sqrt(wavevectors.shape[1])

    def along_z(a, k):
        return lax.ppermute(a, Z, [(i, (i + k) % n_z) for i in range(n_z)])

    def across(a):
        return lax.ppermute(a, "core", [(0, 1), (1, 0)])

    inputs = (cotangent, features, positions, wavevectors)
    inputs = [pltpu.with_memory_space_constraint(a, pltpu.HBM) for a in inputs]
    own, pos_near, wv_near = call(
        load_kernel,
        (
            shape((beads_dev, 2 * width), BF16),
            shape(positions.shape, F32),
            shape(wavevectors.shape, F32),
        ),
        4,
        scratch=[pltpu.SemaphoreType.DMA((4,))],
        space=pltpu.HBM,
    )(*inputs)
    pieces = {0: own, 2: along_z(own, 2), 6: along_z(own, -2)}

    n_rows = 2 * n_xy * 16
    cs_shape = shape((2, n_xy, 2, 16, beads_grp), BF16)
    trig = call(
        trig_near_kernel,
        (cs_shape, shape((n_rows, 16), BF16), shape((n_rows, 8), F32)),
        2,
        scratch=[pltpu.VMEM((n_xy, LANES, 8), F32)],
    )(pos_near, wv_near)
    own, trig, pos_near = lax.optimization_barrier((own, trig, pos_near))
    pieces[1], pieces[7] = along_z(own, 1), along_z(own, -1)
    turns = [2 if i % (n_z // 2) < n_z // 4 else -2 for i in range(n_z)]
    pos_far = lax.ppermute(pos_near, Z, [((i - turns[i]) % n_z, i) for i in range(n_z)])
    pieces[2], pieces[6], trig = lax.optimization_barrier((pieces[2], pieces[6], trig))
    ahead, behind = pieces[2], pieces[6]
    first = lax.axis_index("core") == 0
    onward, other = jnp.where(first, ahead, behind), jnp.where(first, behind, ahead)
    n_zl = lax.axis_size("zl")

    def at(z, core):
        return (z // n_zl * 2 + core) * n_zl + z % n_zl

    def by_core(a, k):
        pairs = [(at(z, c), at((z + k - 2 * k * c) % n_z, c)) for z in range(n_z) for c in range(2)]
        return lax.ppermute(a, ("zh", "core", "zl"), pairs)

    pieces[4] = by_core(onward, 2)
    crossed = by_core(other, -1)
    straight = by_core(onward, 1)
    cs = call(trig_far_kernel, cs_shape, 3, aliases={2: 0})(pos_far, trig[2], trig[0])
    kvrel = trig[1]

    near_blocks = [pieces[k] for k in (0, 1, 2, 4, 6, 7)]
    early = call(
        early_kernel, shape((2, n_xy, 32, 2 * width), F32), 1 + len(near_blocks)
    )(cs, *near_blocks)
    early, straight, crossed = lax.optimization_barrier((early, straight, crossed))
    pieces[3] = jnp.where(first, straight, crossed)
    pieces[5] = jnp.where(first, crossed, straight)
    late_blocks = [pieces[3], pieces[5]]
    blocks = [pieces[k] for k in range(n_z)]

    def spectra(dc, dtype):
        return call(
            lambda *refs: late_kernel(dc, *refs),
            shape((n_xy, 32, 2 * width), dtype),
            2 + len(late_blocks),
        )(cs, early, *late_blocks)

    theirs = across(spectra(1, BF16))
    mine = (spectra(0, F32) + theirs.astype(F32)).astype(BF16)
    arrived = lax.all_to_all(mine, XY, 0, 0, tiled=True)
    copies, grad_filter = call(
        lambda *refs: filter_kernel(spec_scale, wave_scale, *refs),
        (shape((n_xy, 32, 2 * width), BF16), shape((16, width), F32)),
        2,
    )(arrived, filter_gain)
    near = lax.all_to_all(copies, XY, 0, 0, tiled=True)
    far = across(near)
    gf, gp = call(
        grads_near_kernel,
        (shape((width, beads_grp), F32), shape((8, beads_grp), F32)),
        3 + len(blocks),
    )(cs, kvrel, near, *blocks)
    parts = call(
        grads_far_kernel,
        shape((n_z, width + 8, beads_dev), BF16),
        5 + len(blocks),
    )(cs, kvrel, far, gf, gp, *blocks)
    outs = (
        shape((beads_dev, width), BF16),
        shape((3, beads_dev), F32),
        shape((16, width), F32),
    )
    return call(lambda *refs: total_kernel(spec_scale, *refs), outs, 2)(
        lax.all_to_all(parts, Z, 0, 0, tiled=True), grad_filter
    )


def solution(mesh):
    torus = Mesh(mesh.devices.reshape(4, 4, 2, 2, mesh.shape["waves"]), ALL)
    beads = ("x", "y", "zh", "core")
    return jax.shard_map(
        body,
        mesh=torus,
        in_specs=(P(None, beads), P(ALL, None), P(ALL, None), P(), P(ALL, None)),
        out_specs=(P(ALL, None), P(None, ALL), P(ALL, None)),
        check_vma=False,
    )
```

```python
import math

import jax
import jax.numpy as jnp
from jax import lax
from jax.experimental import pallas as pl
from jax.experimental.pallas import tpu as pltpu
from jax.sharding import Mesh
from jax.sharding import PartitionSpec as P


ALL = ("x", "y", "zh", "core", "zl")
Z = ("zh", "zl")
XY = ("x", "y")
BF16 = jnp.bfloat16
F32 = jnp.float32
LANES = 128

SIN_TURN = (6.28318501, -41.3416557, 81.6010056, -76.5497818, 39.536705)


def sin_turn(h):
    s = h * h
    poly = SIN_TURN[-1]
    for c in SIN_TURN[-2::-1]:
        poly = poly * s + c
    return poly * h


def load_kernel(cot, feat, pos, wv, own, pos_near, wv_near, sems):
    width = cot.shape[1]
    copies = [
        pltpu.make_async_copy(cot, own.at[:, :width], sems.at[0]),
        pltpu.make_async_copy(feat, own.at[:, width:], sems.at[1]),
        pltpu.make_async_copy(pos, pos_near, sems.at[2]),
        pltpu.make_async_copy(wv, wv_near, sems.at[3]),
    ]
    for c in copies:
        c.start()
    for c in copies:
        c.wait()


def trig_rows(kcols, pos, cs, zh, zl, first):
    n_xy = cs.shape[1]
    n_z = cs.shape[4] // LANES
    n_zl = n_z // 2
    columns = [
        pl.multiple_of(lax.rem(zh * n_zl + zl + n_z - first - i, n_z) * LANES, LANES)
        for i in range(n_zl)
    ]

    def step(i, carry):
        dc, xy = i // n_xy, lax.rem(i, n_xy)
        cols = kcols[pl.ds(pl.multiple_of(i * 16, 16), 16), :]
        t = cols[:, 0:1] * pos[0:1] + cols[:, 1:2] * pos[1:2] + cols[:, 2:3] * pos[2:3]
        f = t - jnp.round(t)
        cosine = sin_turn(0.25 - jnp.abs(f)).astype(BF16)
        sine = sin_turn(jnp.maximum(jnp.minimum(f, 0.5 - f), -0.5 - f)).astype(BF16)
        for j, column in enumerate(columns):
            part = slice(j * LANES, (j + 1) * LANES)
            cs[dc, xy, 0, :, pl.ds(column, LANES)] = cosine[:, part]
            cs[dc, xy, 1, :, pl.ds(column, LANES)] = sine[:, part]
        return carry

    lax.fori_loop(0, 2 * n_xy, step, 0, unroll=4)


def trig_near_kernel(pos, wv, cs, kvrel, kcols, kvt):
    zh, zl, core = (lax.axis_index(a) for a in ("zh", "zl", "core"))
    n_xy = cs.shape[1]
    n_zl = cs.shape[4] // LANES // 2
    for xy in range(n_xy):
        at = pl.multiple_of((xy * 2 + zh) * LANES, LANES)
        piece = wv[:, pl.ds(at, LANES)]
        piece = jnp.concatenate([piece, jnp.zeros((5, LANES), F32)], 0)
        kvt[xy, :, 0:8] = piece.T
    for dc in range(2):
        at = pl.multiple_of((jnp.bitwise_xor(core, dc) * n_zl + zl) * 16, 16)
        for xy in range(n_xy):
            cols = kvt[xy, pl.ds(at, 16), 0:8]
            rows = slice((dc * n_xy + xy) * 16, (dc * n_xy + xy + 1) * 16)
            hi = cols.astype(BF16)
            lo = (cols - hi.astype(F32)).astype(BF16)
            kvrel[rows, :] = jnp.concatenate([hi, lo], 1)
            kcols[rows, :] = cols * (1.0 / (2.0 * math.pi))
    trig_rows(kcols, pos[...], cs, zh, zl, zh * n_zl)


def trig_far_kernel(pos, kcols, _, cs):
    zh, zl = lax.axis_index("zh"), lax.axis_index("zl")
    n_zl = cs.shape[4] // LANES // 2
    trig_rows(kcols, pos[...], cs, zh, zl, jnp.bitwise_xor(zh, 1) * n_zl)


def joined(pieces):
    return jnp.concatenate([p[:LANES] for p in pieces], 0)


def early_kernel(cs, *refs):
    pieces, out = refs[:-1], refs[-1]
    rows = cs[...].reshape(-1, cs.shape[4])
    n, m = 3 * LANES, rows.shape[1] - 3 * LANES
    parts = [rows[:, :n], rows[:, n + LANES : m], rows[:, m + LANES :]]
    part = jnp.dot(jnp.concatenate(parts, 1), joined(pieces), preferred_element_type=F32)
    out[...] = part.reshape(out.shape)


def late_kernel(dc, cs, early, ahead, behind, out):
    rows = cs[dc].reshape(-1, cs.shape[4])
    n, m = 3 * LANES, rows.shape[1] - 3 * LANES
    rows = jnp.concatenate([rows[:, n : n + LANES], rows[:, m : m + LANES]], 1)
    part = jnp.dot(rows, joined([ahead, behind]), preferred_element_type=F32)
    out[...] = (part.reshape(out.shape) + early[dc]).astype(out.dtype)


def filter_kernel(spec_scale, wave_scale, arrived, gain, out, grad_filter):
    n = arrived.shape[0]
    width = gain.shape[1]
    total = arrived[0].astype(F32)
    for i in range(1, n):
        total = total + arrived[i].astype(F32)
    total = total.reshape(2, 16, 2 * width)
    cot = total[:, :, :width] * wave_scale
    spec = total[:, :, width:] * spec_scale
    g = gain[...].astype(F32)
    grad_filter[...] = cot[0] * spec[0] + cot[1] * spec[1]
    filt = (g[None] * spec * (wave_scale / spec_scale)).astype(BF16)
    dspec = (g[None] * cot).astype(BF16)
    both = jnp.concatenate([filt, dspec], 2).reshape(32, 2 * width)
    for i in range(n):
        out[i] = both


def half_gradients(dc, cs, kvrel, stacked, beads_all):
    n_xy, beads = cs.shape[1], cs.shape[4]
    width = beads_all.shape[1] // 2
    both = stacked[...].reshape(n_xy * 32, 2 * width)
    ab = lax.dot_general(both, beads_all, (((1,), (1,)), ((), ())), preferred_element_type=F32)
    ab = ab.reshape(n_xy, 2, 16, beads)
    d = cs[dc, :, 0].astype(F32) * ab[:, 1] - cs[dc, :, 1].astype(F32) * ab[:, 0]
    d = d.reshape(n_xy * 16, beads).astype(BF16)
    kv = kvrel[dc * n_xy * 16 : (dc + 1) * n_xy * 16, :]
    gp = lax.dot_general(kv, d, (((0,), (0,)), ((), ())), preferred_element_type=F32)
    rows = cs[dc].reshape(n_xy * 32, beads)
    gf = lax.dot_general(
        both[:, width:], rows, (((0,), (0,)), ((), ())), preferred_element_type=F32
    )
    return gf, gp[0:8] + gp[8:16]


def grads_near_kernel(cs, kvrel, stacked, *refs):
    pieces, (gf_out, gp_out) = refs[:-2], refs[-2:]
    beads_all = joined(pieces)
    gf, gp = half_gradients(0, cs, kvrel, stacked, beads_all)
    gf_out[...] = gf
    gp_out[...] = gp


def grads_far_kernel(cs, kvrel, stacked, gf_in, gp_in, *refs):
    pieces, out = refs[:-1], refs[-1]
    beads_all = joined(pieces)
    gf, gp = half_gradients(1, cs, kvrel, stacked, beads_all)
    gf = (gf + gf_in[...]).astype(BF16)
    gp = gp + gp_in[...]
    hi = gp.astype(BF16).astype(F32)
    tail = jnp.concatenate([hi[0:3], (gp - hi)[0:3], jnp.zeros_like(gp[0:2])], 0).astype(BF16)
    n_z = out.shape[0]
    width = gf.shape[0]
    here = lax.axis_index(Z)
    for shift in range(n_z):
        at = slice(shift * LANES, (shift + 1) * LANES)
        to = lax.rem(here + n_z - shift, n_z)
        out[to, 0:width, :] = gf[:, at]
        out[to, width : width + 8, :] = tail[:, at]


def total_kernel(spec_scale, arrived, grad_filter, gf_out, gp_out, filter_out):
    total = arrived[0].astype(F32)
    for i in range(1, arrived.shape[0]):
        total = total + arrived[i].astype(F32)
    total = total * spec_scale
    width = gf_out.shape[1]
    gf_out[...] = total[:width].T.astype(BF16)
    gp_out[...] = total[width : width + 3] + total[width + 3 : width + 6]
    filter_out[...] = grad_filter[...]


def call(kernel, out_shape, n_in, scratch=(), aliases=None, space=pltpu.VMEM):
    specs = [pl.BlockSpec(memory_space=space)] * n_in
    outs = jax.tree.map(lambda _: pl.BlockSpec(memory_space=pltpu.VMEM), out_shape)
    return pl.pallas_call(
        kernel,
        out_shape=out_shape,
        in_specs=specs,
        out_specs=outs,
        scratch_shapes=scratch,
        input_output_aliases=aliases or {},
        compiler_params=pltpu.CompilerParams(vmem_limit_bytes=16 << 20),
    )


def shape(dims, dtype):
    return jax.ShapeDtypeStruct(dims, dtype)


def body(positions, features, cotangent, wavevectors, filter_gain):
    n_z = lax.axis_size(Z)
    n_xy = lax.axis_size(XY)
    beads_dev, width = features.shape
    beads_grp = beads_dev * n_z
    n_beads = beads_grp * n_xy * 2
    spec_scale = 1.0 / math.sqrt(n_beads)
    wave_scale = 1.0 / math.sqrt(wavevectors.shape[1])

    def along_z(a, k):
        return lax.ppermute(a, Z, [(i, (i + k) % n_z) for i in range(n_z)])

    def across(a):
        return lax.ppermute(a, "core", [(0, 1), (1, 0)])

    inputs = (cotangent, features, positions, wavevectors)
    inputs = [pltpu.with_memory_space_constraint(a, pltpu.HBM) for a in inputs]
    own, pos_near, wv_near = call(
        load_kernel,
        (
            shape((beads_dev, 2 * width), BF16),
            shape(positions.shape, F32),
            shape(wavevectors.shape, F32),
        ),
        4,
        scratch=[pltpu.SemaphoreType.DMA((4,))],
        space=pltpu.HBM,
    )(*inputs)
    pieces = {0: own, 2: along_z(own, 2), 6: along_z(own, -2)}

    n_rows = 2 * n_xy * 16
    cs_shape = shape((2, n_xy, 2, 16, beads_grp), BF16)
    trig = call(
        trig_near_kernel,
        (cs_shape, shape((n_rows, 16), BF16), shape((n_rows, 8), F32)),
        2,
        scratch=[pltpu.VMEM((n_xy, LANES, 8), F32)],
    )(pos_near, wv_near)
    pieces[1], pieces[7] = along_z(own, 1), along_z(own, -1)
    turns = [2 if i % (n_z // 2) < n_z // 4 else -2 for i in range(n_z)]
    pos_far = lax.ppermute(pos_near, Z, [((i - turns[i]) % n_z, i) for i in range(n_z)])
    pieces[2], pieces[6], trig = lax.optimization_barrier((pieces[2], pieces[6], trig))
    ahead, behind = pieces[2], pieces[6]
    onward = jnp.where(lax.axis_index("core") == 0, ahead, behind)
    n_zl = lax.axis_size("zl")

    def at(z, core):
        return (z // n_zl * 2 + core) * n_zl + z % n_zl

    pairs = [(at(z, c), at((z + 2 - 4 * c) % n_z, c)) for z in range(n_z) for c in range(2)]
    pieces[4] = lax.ppermute(onward, ("zh", "core", "zl"), pairs)
    pieces[3], pieces[5] = along_z(ahead, 1), along_z(behind, -1)
    late_blocks = [pieces[3], pieces[5]]
    blocks = [pieces[k] for k in range(n_z)]
    cs = call(trig_far_kernel, cs_shape, 3, aliases={2: 0})(pos_far, trig[2], trig[0])
    kvrel = trig[1]

    near_blocks = [blocks[k] for k in range(n_z) if k not in (3, n_z - 3)]
    early = call(
        early_kernel, shape((2, n_xy, 32, 2 * width), F32), 1 + len(near_blocks)
    )(cs, *near_blocks)

    def spectra(dc, dtype):
        return call(
            lambda *refs: late_kernel(dc, *refs),
            shape((n_xy, 32, 2 * width), dtype),
            2 + len(late_blocks),
        )(cs, early, *late_blocks)

    theirs = across(spectra(1, BF16))
    mine = (spectra(0, F32) + theirs.astype(F32)).astype(BF16)
    arrived = lax.all_to_all(mine, XY, 0, 0, tiled=True)
    copies, grad_filter = call(
        lambda *refs: filter_kernel(spec_scale, wave_scale, *refs),
        (shape((n_xy, 32, 2 * width), BF16), shape((16, width), F32)),
        2,
    )(arrived, filter_gain)
    near = lax.all_to_all(copies, XY, 0, 0, tiled=True)
    far = across(near)
    gf, gp = call(
        grads_near_kernel,
        (shape((width, beads_grp), F32), shape((8, beads_grp), F32)),
        3 + len(blocks),
    )(cs, kvrel, near, *blocks)
    parts = call(
        grads_far_kernel,
        shape((n_z, width + 8, beads_dev), BF16),
        5 + len(blocks),
    )(cs, kvrel, far, gf, gp, *blocks)
    outs = (
        shape((beads_dev, width), BF16),
        shape((3, beads_dev), F32),
        shape((16, width), F32),
    )
    return call(lambda *refs: total_kernel(spec_scale, *refs), outs, 2)(
        lax.all_to_all(parts, Z, 0, 0, tiled=True), grad_filter
    )


def solution(mesh):
    torus = Mesh(mesh.devices.reshape(4, 4, 2, 2, mesh.shape["waves"]), ALL)
    beads = ("x", "y", "zh", "core")
    return jax.shard_map(
        body,
        mesh=torus,
        in_specs=(P(None, beads), P(ALL, None), P(ALL, None), P(), P(ALL, None)),
        out_specs=(P(ALL, None), P(None, ALL), P(ALL, None)),
        check_vma=False,
    )
```
